32 devices in a mesh: dp: 16 (over z, x, core), mp: 2 (over y).
Axes of the slice: x: 2, y: 2, z: 4, core: 2. Of those that a mesh axis runs over, the one named last changes fastest.
Arguments:
- tokens: bfloat16 [31360, 768], P(('dp', 'mp')), may hold values from -6 to 6
- frame_counts: int32 [16, 2], P('dp'), may hold values from 1 to 8, 10 in all within a row
- norm_gains: float32 [3, 768], replicated, may hold values from 0.1 to 1.9
- norm_shifts: float32 [3, 768], replicated, may hold values from -2 to 2
- attend_weight: bfloat16 [768, 3, 768], P(None, None, 'mp'), may hold values from -0.21875 to 0.21875
- attend_offset: float32 [2, 768], P(None, 'mp'), may hold values from -3 to 3
- output_weight: bfloat16 [768, 768], P('mp'), may hold values from -0.875 to 0.875
- output_offset: float32 [768], replicated, may hold values from -2 to 2
- expand_weight: bfloat16 [768, 3072], P(None, 'mp'), may hold values from -0.21875 to 0.21875
- expand_offset: float32 [3072], P('mp'), may hold values from -3 to 3
- contract_weight: bfloat16 [3072, 768], P('mp'), may hold values from -0.109375 to 0.109375
- contract_offset: float32 [768], replicated, may hold values from -2 to 2
- learner_weight: bfloat16 [768, 8], replicated, may hold values from -0.4375 to 0.4375
- learner_offset: float32 [8], replicated, may hold values from -3 to 3
- pooled_cotangent: bfloat16 [160, 8, 768], P(('dp', 'mp')), may hold values from -6 to 6
Outputs:
- pooled: float32 [160, 8, 768], P(('dp', 'mp'))
- tokens_gradient: float32 [31360, 768], P(('dp', 'mp'))
- gains_gradient: float32 [3, 768], replicated
- shifts_gradient: float32 [3, 768], replicated
- attend_weight_gradient: float32 [768, 3, 768], P(None, None, 'mp')
- attend_offset_gradient: float32 [2, 768], P(None, 'mp')
- output_weight_gradient: float32 [768, 768], P('mp')
- output_offset_gradient: float32 [768], replicated
- expand_weight_gradient: float32 [768, 3072], P(None, 'mp')
- expand_offset_gradient: float32 [3072], P('mp')
- contract_weight_gradient: float32 [3072, 768], P('mp')
- contract_offset_gradient: float32 [768], replicated
- learner_weight_gradient: float32 [768, 8], replicated
- learner_offset_gradient: float32 [8], replicated
The draws below stay inside these ranges and needn't reach their ends.
Inputs may be any that keep to these rules, and one draw needn't show every extreme that they name: `frame_counts`: each row holds the frame counts of one group's 2 clips in order; they sum to 10, and none exceeds 8.
All inputs are finite; a program needn't handle non-finite values.
Results may differ from the reference program's by a relative error of at most 0.0085.
Values may be sent and summed in bfloat16 or wider, within the bound.
No kernel may reach another device: no remote copies, remote signals or barrier semaphores. Data moves between devices by JAX's collectives and lax.ppermute only.
A program may use at most 192 MiB of HBM per device.

```python
import math
import jax
import jax.numpy as jnp
import numpy as np
from jax import lax

D = 768
HEADS = 12
HEAD_DIM = 64
FF = 3072
MAPS = 8
FRAME_TOK = 196
MOST_FR = 8
FRAMES_GRP = 10
CLIPS = 2
GRP_TOK = 1960
TOKENS = 31360
FRAMES = 160
N_DP = 16


def levels(rng, dims, cuts, low, top_value):
    level, own = 1.0, jax.random.fold_in(rng, 6)
    for position, blocks in cuts:
        steps = jnp.exp(jax.random.uniform(jax.random.fold_in(own, position), (blocks,), jnp.float32, low / len(cuts), top_value / len(cuts)))
        level = level * jnp.repeat(steps, dims[position] // blocks).reshape([-1 if axis == position else 1 for axis in range(len(dims))])
    return level


def profile(count, total, limit, slope):
    loads = [(1 << 20) // math.isqrt(grade ** slope) + 1 for grade in range(2, count + 1)]
    rest, given = total - limit - (count - 1), [1] * (count - 1)
    while rest > 0:
        movable = [i for i in range(count - 1) if given[i] < limit]
        mass, budget = sum([loads[i] for i in movable]), rest
        for i in movable:
            addition = min(limit - given[i], max(1, budget * loads[i] // mass), rest)
            given[i] = given[i] + addition
            rest = rest - addition
    return np.array([limit] + given)


def ragged_sizes(rng, count, total, bound, skew):
    if count == 2:
        one = jax.random.randint(rng, (), max(1, total - bound), min(bound, total - 1) + 1)
        return jnp.stack([one, total - one])
    lengths = jnp.asarray(profile(count, total, bound, skew), jnp.int32)
    pairs = (count - 1) // 2
    source_of, receiver = lengths[1:1 + 2 * pairs:2], lengths[2:2 + 2 * pairs:2]
    margin = jnp.minimum(source_of - 1, bound - receiver)
    shifted = jax.random.randint(jax.random.fold_in(rng, 1), (pairs,), 0, 1 << 20) % (margin + 1)
    lengths = lengths.at[1:1 + 2 * pairs:2].set(source_of - shifted).at[2:2 + 2 * pairs:2].set(receiver + shifted)
    return lengths[jax.random.permutation(jax.random.fold_in(rng, 2), count)]


def gaussian(rng, dims, width, limit, shards=(), held_as=jnp.bfloat16):
    array = width * jax.random.normal(rng, dims, jnp.float32)
    if shards:
        array = array * levels(rng, dims, shards, -0.22, 0.18)
    return jnp.clip(array, -limit, limit).astype(held_as)


def setup_inputs(seed: int = 0) -> dict:
    splits = jax.random.split(jax.random.key(seed), 16)
    return {
        "tokens": gaussian(splits[0], (TOKENS, D), 1.0, 6.0, ((0, 32),)),
        "frame_counts": jax.vmap(lambda own: ragged_sizes(own, CLIPS, FRAMES_GRP, MOST_FR, 2))(jax.random.split(splits[1], N_DP)).reshape((N_DP, CLIPS)).astype(jnp.int32),
        "norm_gains": jnp.clip(1.0 + 0.18 * jax.random.normal(splits[2], (3, D), jnp.float32), 0.1, 1.9),
        "norm_shifts": gaussian(splits[3], (3, D), 0.3, 2.0, (), jnp.float32),
        "attend_weight": gaussian(splits[4], (D, 3, D), D ** -0.5, 0.21875, ((2, 2),)),
        "attend_offset": gaussian(splits[5], (2, D), 0.5, 3.0, ((1, 2),), jnp.float32),
        "output_weight": gaussian(splits[6], (D, D), (D // 16) ** -0.5, 0.875, ((0, 2),)),
        "output_offset": gaussian(splits[7], (D,), 0.3, 2.0, (), jnp.float32),
        "expand_weight": gaussian(splits[8], (D, FF), D ** -0.5, 0.21875, ((1, 2),)),
        "expand_offset": gaussian(splits[9], (FF,), 0.5, 3.0, ((0, 2),), jnp.float32),
        "contract_weight": gaussian(splits[10], (FF, D), FF ** -0.5, 0.109375, ((0, 2),)),
        "contract_offset": gaussian(splits[11], (D,), 0.3, 2.0, (), jnp.float32),
        "learner_weight": gaussian(splits[12], (D, MAPS), (D // 4) ** -0.5, 0.4375),
        "learner_offset": gaussian(splits[13], (MAPS,), 0.5, 3.0, (), jnp.float32),
        "pooled_cotangent": gaussian(splits[14], (FRAMES, MAPS, D), 1.0, 6.0, ((0, 32),)),
    }


EPS = 1e-06
MASK_FILL = -1e+30
PRECISE = lax.Precision.HIGHEST

@jax.custom_vjp
def low(v):
    return lax.optimization_barrier(v.astype(jnp.bfloat16)).astype(jnp.float32)

@jax.custom_vjp
def low_back(v):
    return v

def low_keep(v):
    return (low(v), None)

def low_pass(kept, grad):
    return (grad,)

def back_keep(v):
    return (v, None)

def back_low(kept, grad):
    return (low(grad),)
low.defvjp(low_keep, low_pass)
low_back.defvjp(back_keep, back_low)

def layer_norm(values, gain, shift):
    average = lax.optimization_barrier(jnp.mean(values, axis=-1, keepdims=True))
    centred = values - average
    spread = lax.optimization_barrier(jnp.mean(centred * centred, axis=-1, keepdims=True))
    return centred * lax.rsqrt(spread + EPS) * gain + shift

def group_forward(params, group_tokens, counts):
    gain_rows, shift_rows, attend_w, attend_b, output_w, output_b, expand_w, expand_b, contract_w, contract_b, learner_w, learner_b = params
    clip_ends = jnp.cumsum(counts)
    frame_index = jnp.arange(FRAMES_GRP, dtype=jnp.int32)
    clip_of_frame = lax.optimization_barrier(jnp.sum((frame_index[:, None] >= clip_ends[None, :]).astype(jnp.int32), axis=1))
    clip_of_token = jnp.repeat(clip_of_frame, FRAME_TOK)
    same_clip = clip_of_token[:, None] == clip_of_token[None, :]
    first_in = low(layer_norm(group_tokens, gain_rows[0], shift_rows[0]))
    projected = jnp.einsum('td,dcf->tcf', first_in, attend_w, precision=PRECISE)
    offsets = jnp.stack([attend_b[0], jnp.zeros_like(attend_b[0]), attend_b[1]])
    projected = low(low_back(projected + offsets[None]))
    split_heads = projected.reshape(GRP_TOK, 3, HEADS, HEAD_DIM)
    scores = jnp.einsum('qhd,khd->hqk', split_heads[:, 0], split_heads[:, 1], precision=PRECISE) * HEAD_DIM ** (-0.5)
    scores = jnp.where(same_clip[None], low_back(scores), MASK_FILL)
    row_top = lax.optimization_barrier(jnp.max(scores, axis=2, keepdims=True))
    exp_terms = jnp.exp(scores - row_top)
    soft = low(exp_terms / lax.optimization_barrier(jnp.sum(exp_terms, axis=2, keepdims=True)))
    mixed = jnp.einsum('hqk,khd->qhd', soft, split_heads[:, 2], precision=PRECISE).reshape(GRP_TOK, D)
    mixed = low(low_back(mixed))
    attended = low_back(jnp.dot(mixed, output_w, precision=PRECISE))
    residual = group_tokens + attended + output_b
    second_in = low(layer_norm(residual, gain_rows[1], shift_rows[1]))
    pre_gelu = low_back(jnp.dot(second_in, expand_w, precision=PRECISE) + expand_b)
    hidden = low(jax.nn.gelu(pre_gelu, approximate=True))
    block_out = residual + low_back(jnp.dot(hidden, contract_w, precision=PRECISE)) + contract_b
    third_in = low(layer_norm(block_out, gain_rows[2], shift_rows[2]))
    logits = low_back(jnp.dot(third_in, learner_w, precision=PRECISE) + learner_b)
    maps = low(jax.nn.sigmoid(logits)).reshape(FRAMES_GRP, FRAME_TOK, MAPS)
    features = low(block_out).reshape(FRAMES_GRP, FRAME_TOK, D)
    return jnp.einsum('ftk,ftd->fkd', maps, features, precision=PRECISE)

def reference(tokens, frame_counts, norm_gains, norm_shifts, attend_weight, attend_offset, output_weight, output_offset, expand_weight, expand_offset, contract_weight, contract_offset, learner_weight, learner_offset, pooled_cotangent):
    params = (norm_gains.astype(jnp.float32), norm_shifts.astype(jnp.float32), attend_weight.astype(jnp.float32), attend_offset.astype(jnp.float32), output_weight.astype(jnp.float32), output_offset.astype(jnp.float32), expand_weight.astype(jnp.float32), expand_offset.astype(jnp.float32), contract_weight.astype(jnp.float32), contract_offset.astype(jnp.float32), learner_weight.astype(jnp.float32), learner_offset.astype(jnp.float32))
    group_step = jax.checkpoint(group_forward)

    def forward(tokens_wide, weights):
        groups = tokens_wide.reshape(N_DP, GRP_TOK, D)
        pooled_groups = lax.map(lambda inputs: group_step(weights, inputs[0], inputs[1]), (groups, frame_counts))
        return pooled_groups.reshape(FRAMES, MAPS, D)
    pooled, pullback = jax.vjp(forward, tokens.astype(jnp.float32), params)
    tokens_gradient, grads = pullback(pooled_cotangent.astype(jnp.float32))
    return (pooled, tokens_gradient, grads[0], grads[1], grads[2], grads[3], grads[4], grads[5], grads[6], grads[7], grads[8], grads[9], grads[10], grads[11])
```

```python
import functools

import jax
import jax.numpy as jnp
from jax import lax
from jax.experimental import pallas as pl
from jax.experimental.pallas import tpu as pltpu
from jax.sharding import Mesh, PartitionSpec as P

HEAD_DIM = 64
MAPS = 8
FRAME_TOK = 196
EPS = 1e-06
BLK = 256
FAR = 1e30
GELU_C = 0.7978845608028654
GELU_A = 0.044715

F32 = jnp.float32
BF16 = jnp.bfloat16


def nn(a, b):
    return lax.dot_general(a, b, (((1,), (0,)), ((), ())), preferred_element_type=F32)


def nt(a, b):
    return lax.dot_general(a, b, (((1,), (1,)), ((), ())), preferred_element_type=F32)


def tn(a, b):
    return lax.dot_general(a, b, (((0,), (0,)), ((), ())), preferred_element_type=F32)


def fold8(values):
    rows, width = values.shape
    return jnp.sum(values.reshape(rows // 8, 8, width), axis=0)


def centre(values):
    average = jnp.mean(values, axis=-1, keepdims=True)
    centred = values - average
    spread = jnp.mean(centred * centred, axis=-1, keepdims=True)
    scale = lax.rsqrt(spread + EPS)
    return centred * scale, scale


def norm_back(xhat, scale, gain, grad):
    scaled = grad * gain
    along = jnp.mean(scaled * xhat, axis=-1, keepdims=True)
    return scale * (scaled - jnp.mean(scaled, axis=-1, keepdims=True) - xhat * along)


def cost(flops, nbytes):
    return pl.CostEstimate(flops=int(flops), bytes_accessed=int(nbytes), transcendentals=0)


def params(n):
    return pltpu.CompilerParams(
        dimension_semantics=("arbitrary",) * n, vmem_limit_bytes=60 * 1024 * 1024
    )


def whole(shape):
    return pl.BlockSpec(shape, lambda *_: (0,) * len(shape), pipeline_mode=pl.Buffered(1))


def after(value, *others):
    return lax.optimization_barrier((value, others))[0]


def pack_kernel(tokens, cot, out):
    here = tokens.shape[0]
    rows = out.shape[0] - cot.shape[0]
    edge = here // 16 * 16
    out[edge:, :] = jnp.zeros_like(out[edge:, :])
    out[:here, :] = tokens[...]
    out[rows:, :] = cot[...]


def pack(tokens, cot, half_rows):
    rows, width = half_rows + cot.shape[0], tokens.shape[1]
    return pl.pallas_call(
        pack_kernel,
        in_specs=[pl.BlockSpec(tokens.shape), pl.BlockSpec(cot.shape)],
        out_specs=pl.BlockSpec((rows, width)),
        out_shape=jax.ShapeDtypeStruct((rows, width), BF16),
        compiler_params=pltpu.CompilerParams(vmem_limit_bytes=16 * 1024 * 1024),
        cost_estimate=cost(0, 4 * rows * width),
        name="pack",
    )(tokens, cot)


def project_kernel(
    frames_here, scal, oth, own, gain, shift, weight, offset, first, qkv, qfeat, kfeat
):
    step = pl.program_id(0)
    half_blocks = pl.num_programs(0) // 2
    half_rows = half_blocks * BLK
    within = lax.rem(step, half_blocks) * BLK
    rows = pl.ds(pl.multiple_of(within, BLK), BLK)
    values = jnp.where(step < half_blocks, oth[rows, :], own[rows, :]).astype(F32)
    xhat, _ = centre(values)
    low = (xhat * gain[...] + shift[...]).astype(BF16)
    first[...] = low
    out = (nn(low, weight[...]) + offset[...]).astype(BF16)
    third = out.shape[1] // 3
    qkv[:, :third] = out[:, :third] * jnp.asarray(HEAD_DIM**-0.5, BF16)
    qkv[:, third:] = out[:, third:]
    core, count = scal[0], scal[2]
    half = jnp.where(step < half_blocks, 1 - core, core)
    edge = clip_edge(count, frames_here, half_rows)
    token = within + lax.broadcasted_iota(jnp.int32, (BLK, 128), 0)
    lane = lax.broadcasted_iota(jnp.int32, (BLK, 128), 1)
    clip = jnp.where(half * half_rows + token >= edge, 1, 0)
    clip = jnp.where(token >= frames_here * FRAME_TOK, 2, clip)
    hit = lane == clip
    qfeat[...] = jnp.where(hit, 1.0, 0.0).astype(BF16)
    kfeat[...] = jnp.where(hit, 0.0, jnp.where(lane < 3, -FAR, 0.0)).astype(BF16)


def clip_edge(count, frames_here, half_rows):
    return jnp.where(
        count <= frames_here,
        count * FRAME_TOK,
        half_rows + (count - frames_here) * FRAME_TOK,
    )


def clip_span(block, edge, blocks):
    low = jnp.where(block * BLK >= edge, edge // BLK, 0)
    high = jnp.where(block * BLK + BLK - 1 < edge, (edge + BLK - 1) // BLK, blocks)
    return low, high


def project(scal, oth, own, gain, shift, weight, offset, frames_here, half_rows):
    width, cols = weight.shape
    steps = 2 * half_rows // BLK
    rows = 2 * half_rows
    return pl.pallas_call(
        functools.partial(project_kernel, frames_here),
        grid_spec=pltpu.PrefetchScalarGridSpec(
            num_scalar_prefetch=1,
            grid=(steps,),
            in_specs=[
                whole(oth.shape),
                whole(own.shape),
                whole((1, width)),
                whole((1, width)),
                whole((width, cols)),
                whole((1, cols)),
            ],
            out_specs=[
                pl.BlockSpec((BLK, width), lambda i, *_: (i, 0)),
                pl.BlockSpec((BLK, cols), lambda i, *_: (i, 0)),
                pl.BlockSpec((BLK, 128), lambda i, *_: (i, 0)),
                pl.BlockSpec((BLK, 128), lambda i, *_: (i, 0)),
            ],
        ),
        out_shape=[
            jax.ShapeDtypeStruct((rows, width), BF16),
            jax.ShapeDtypeStruct((rows, cols), BF16),
            jax.ShapeDtypeStruct((rows, 128), BF16),
            jax.ShapeDtypeStruct((rows, 128), BF16),
        ],
        compiler_params=params(1),
        cost_estimate=cost(2 * rows * width * cols, 4 * rows * width + 2 * rows * cols),
        name="project",
    )(scal, oth, own, gain, shift, weight, offset)


def attend_kernel(
    frames_here, scal, q, qfeat, k, kfeat, v, mixed_oth, mixed_own, wide, log_total, sa, sb, acc
):
    step = pl.program_id(1)
    blocks = pl.num_programs(1)
    half = blocks // 2
    flip = half * (1 - scal[0])
    edge = clip_edge(scal[2], frames_here, half * BLK)
    low, high = clip_span(step ^ flip, edge, blocks)
    lane = lax.broadcasted_iota(jnp.int32, (BLK, 128), 1)
    left = lane < HEAD_DIM
    none = jnp.zeros((BLK, 128), BF16)
    qa = jnp.concatenate([jnp.where(left, q[...], none), qfeat[...]], axis=1)
    qb = jnp.concatenate([jnp.where(left, none, q[...]), qfeat[...]], axis=1)

    def score(block, tops):
        rows = pl.ds(pl.multiple_of((block ^ flip) * BLK, BLK), BLK)
        keys = jnp.concatenate([k[rows, :], kfeat[rows, :]], axis=1)
        one, two = nt(qa, keys), nt(qb, keys)
        sa[block] = one
        sb[block] = two
        return (
            jnp.maximum(tops[0], jnp.maximum(one[:, :128], one[:, 128:])),
            jnp.maximum(tops[1], jnp.maximum(two[:, :128], two[:, 128:])),
        )

    start = jnp.full((BLK, 128), -3e38, F32)
    tops = lax.fori_loop(low, high, score, (start, start))
    top_a = jnp.max(tops[0], axis=1, keepdims=True)
    top_b = jnp.max(tops[1], axis=1, keepdims=True)
    acc[...] = jnp.zeros_like(acc)
    ones_a = jnp.where(lane == 0, 1.0, 0.0).astype(BF16)
    ones_b = jnp.where(lane == 1, 1.0, 0.0).astype(BF16)

    def mix(block, carry):
        rows = pl.ds(pl.multiple_of((block ^ flip) * BLK, BLK), BLK)
        pa = jnp.exp(sa[block] - top_a).astype(BF16)
        pb = jnp.exp(sb[block] - top_b).astype(BF16)
        both = v[rows, :]
        va = jnp.concatenate([jnp.where(left, both, none), ones_a], axis=1)
        vb = jnp.concatenate([jnp.where(left, none, both), ones_b], axis=1)
        acc[...] += nn(jnp.concatenate([pa, pb], axis=1), jnp.concatenate([va, vb], axis=0))
        return carry

    lax.fori_loop(low, high, mix, 0)
    total_a, total_b = acc[:, 128:129], acc[:, 129:130]
    out = acc[:, :128] / jnp.where(left, total_a, total_b)
    wide[...] = out
    low_out = out.astype(BF16)

    @pl.when(step < half)
    def _():
        mixed_oth[...] = low_out

    @pl.when(step >= half)
    def _():
        mixed_own[...] = low_out

    logs = jnp.where(
        lane == 0,
        top_a + jnp.log(total_a),
        jnp.where(lane == 1, top_b + jnp.log(total_b), 0.0),
    )
    log_total[0, 0] = logs.T[:8]


def attend(scal, qkv, qfeat, kfeat, frames_here, start, count):
    rows = qkv.shape[0]
    pairs = qkv.shape[1] // 384
    blocks = rows // BLK
    half = blocks // 2
    width = count * 128
    return pl.pallas_call(
        functools.partial(attend_kernel, frames_here),
        grid_spec=pltpu.PrefetchScalarGridSpec(
            num_scalar_prefetch=1,
            grid=(count, blocks),
            in_specs=[
                pl.BlockSpec((BLK, 128), lambda p, i, *_: (i, start + p)),
                pl.BlockSpec((BLK, 128), lambda p, i, *_: (i, 0)),
                pl.BlockSpec((rows, 128), lambda p, i, *_: (0, pairs + start + p)),
                pl.BlockSpec((rows, 128), lambda p, i, *_: (0, 0)),
                pl.BlockSpec((rows, 128), lambda p, i, *_: (0, 2 * pairs + start + p)),
            ],
            out_specs=[
                pl.BlockSpec((BLK, 128), lambda p, i, *_: (jnp.minimum(i, half - 1), p)),
                pl.BlockSpec((BLK, 128), lambda p, i, *_: (jnp.maximum(i - half, 0), p)),
                pl.BlockSpec((BLK, 128), lambda p, i, *_: (i, p)),
                pl.BlockSpec((1, 1, 8, BLK), lambda p, i, *_: (p, i, 0, 0)),
            ],
            scratch_shapes=[
                pltpu.VMEM((blocks, BLK, BLK), F32),
                pltpu.VMEM((blocks, BLK, BLK), F32),
                pltpu.VMEM((BLK, 256), F32),
            ],
        ),
        out_shape=[
            jax.ShapeDtypeStruct((rows // 2, width), BF16),
            jax.ShapeDtypeStruct((rows // 2, width), BF16),
            jax.ShapeDtypeStruct((rows, width), F32),
            jax.ShapeDtypeStruct((count, blocks, 8, BLK), F32),
        ],
        compiler_params=params(2),
        cost_estimate=cost(16 * rows * rows * width, 16 * rows * width),
        name="attend",
    )(scal, qkv, qfeat, qkv, kfeat, qkv)


def gather_out_weight(scal, own_out, got_a, got_b, out_weight, hid):
    core, plane = scal[0], scal[1]
    share = own_out.shape[0]
    quarter = share // 2
    out_weight[pl.ds(pl.multiple_of(plane * share, 64), share), :] = own_out[...]
    base = (1 - plane) * share
    out_weight[pl.ds(pl.multiple_of(base + core * quarter, 64), quarter), :] = got_a[
        2 * hid : 2 * hid + quarter, :
    ]
    out_weight[pl.ds(pl.multiple_of(base + (1 - core) * quarter, 64), quarter), :] = got_b[
        2 * hid : 2 * hid + quarter, :
    ]


def up_weight(core, own_up, got_a, got_b, chunk):
    hid = got_a.shape[1]
    if chunk < 2:
        return (got_b, got_a)[chunk][hid : 2 * hid, :]
    pick = (1 - core) if chunk == 2 else core
    return own_up[:, pl.ds(pl.multiple_of(pick * hid, 128), hid)]


def down_weight(core, own_down, got_a, got_b, chunk):
    hid = got_a.shape[1]
    if chunk < 2:
        return (got_b, got_a)[chunk][:hid, :]
    pick = (1 - core) if chunk == 2 else core
    return own_down[pl.ds(pl.multiple_of(pick * hid, 128), hid), :]


def ahead_kernel(
    frames_here,
    scal,
    mixed_own,
    mixed_oth,
    tokens,
    cot,
    own_out,
    own_up,
    own_down,
    got_a,
    got_b,
    up_offset,
    gains,
    shifts,
    out_offset,
    down_offset,
    learner,
    learner_offset,
    out_grad_out,
    xhat_out,
    scale_out,
    hidden_out,
    slope_out,
    second_out,
    out_low_out,
    sums,
    pooled,
    learner_sums,
    learner_offset_sums,
    out_weight,
):
    step = pl.program_id(0)
    core, plane = scal[0], scal[1]
    hid = got_a.shape[1]
    share = own_out.shape[0]

    @pl.when(step == 0)
    def _():
        gather_out_weight(scal, own_out, got_a, got_b, out_weight, hid)
        for ref in (sums, pooled, learner_sums, learner_offset_sums):
            ref[...] = jnp.zeros_like(ref)

    def up_bias(chunk):
        side = (1 - plane) if chunk < 2 else plane
        pick = (1 - core) if chunk % 2 == 0 else core
        return up_offset[pl.ds(2 * side + pick, 1), :]

    mine = pl.ds(pl.multiple_of(core * share, 64), share)
    theirs = pl.ds(pl.multiple_of((1 - core) * share, 64), share)
    attended = nn(mixed_own[...], out_weight[mine, :]) + nn(mixed_oth[...], out_weight[theirs, :])
    residual = tokens[...].astype(F32) + attended + out_offset[...]
    xhat_two, scale_two = centre(residual)
    xhat_out[...] = xhat_two
    scale_out[...] = jnp.broadcast_to(scale_two, scale_out.shape)
    second = (xhat_two * gains[1:2, :] + shifts[1:2, :]).astype(BF16)
    second_out[...] = second
    block_out = residual + down_offset[...]
    for chunk in range(4):
        cols = slice(chunk * hid, (chunk + 1) * hid)
        pre = nn(second, up_weight(core, own_up, got_a, got_b, chunk)) + up_bias(chunk)
        square = pre * pre
        bend = jnp.tanh(GELU_C * (pre + GELU_A * (square * pre)))
        half_up = 0.5 * (1.0 + bend)
        hidden = (pre * half_up).astype(BF16)
        slope_out[:, cols] = half_up + (0.5 * pre) * (1.0 - bend * bend) * (
            GELU_C + (3.0 * GELU_A * GELU_C) * square
        )
        hidden_out[:, cols] = hidden
        block_out = block_out + nn(hidden, down_weight(core, own_down, got_a, got_b, chunk))
    xhat_three, scale_three = centre(block_out)
    third = (xhat_three * gains[2:3, :] + shifts[2:3, :]).astype(BF16)
    logits = nt(third, learner[...]) + learner_offset[...]
    sig = 1.0 / (1.0 + jnp.exp(-logits))
    token = step * BLK + lax.broadcasted_iota(jnp.int32, (BLK, 128), 0)
    first_token = (lax.broadcasted_iota(jnp.int32, (BLK, 128), 1) >> 3) * FRAME_TOK
    inside = (token >= first_token) & (token < first_token + FRAME_TOK)
    inside = inside & (first_token < frames_here * FRAME_TOK)
    maps = jnp.where(inside, sig, 0.0).astype(BF16)
    feature = block_out.astype(BF16)
    pooled[...] += tn(maps, feature)
    maps_grad = nt(feature, cot[...])
    pool_grad = nn(maps, cot[...])
    logits_grad = jnp.where(inside, maps_grad * sig * (1.0 - sig), 0.0).astype(BF16)
    learner_sums[...] += tn(logits_grad, third)
    learner_offset_sums[...] += fold8(logits_grad.astype(F32))
    third_grad = nn(logits_grad, learner[...])
    sums[0:8, :] += fold8(third_grad * xhat_three)
    sums[8:16, :] += fold8(third_grad)
    out_grad = pool_grad + norm_back(xhat_three, scale_three, gains[2:3, :], third_grad)
    sums[16:24, :] += fold8(out_grad)
    out_grad_out[...] = out_grad
    out_low_out[...] = out_grad.astype(BF16)


def behind_kernel(
    scal,
    out_grad,
    out_low,
    xhat_two,
    scale_two,
    slope,
    own_out,
    own_up,
    own_down,
    got_a,
    got_b,
    gains,
    residual_grad_out,
    grad_own,
    grad_oth,
    pre_grad_out,
    residual_low_out,
    sums,
    up_sums,
    out_weight,
):
    core = scal[0]
    hid = got_a.shape[1]
    share = own_out.shape[0]

    @pl.when(pl.program_id(0) == 0)
    def _():
        gather_out_weight(scal, own_out, got_a, got_b, out_weight, hid)
        for ref in (sums, up_sums):
            ref[...] = jnp.zeros_like(ref)

    mine = pl.ds(pl.multiple_of(core * share, 64), share)
    theirs = pl.ds(pl.multiple_of((1 - core) * share, 64), share)
    low = out_low[...]
    second_grad = None
    for chunk in range(4):
        cols = slice(chunk * hid, (chunk + 1) * hid)
        hidden_grad = nt(low, down_weight(core, own_down, got_a, got_b, chunk))
        pre_grad = (hidden_grad * slope[:, cols]).astype(BF16)
        pre_grad_out[:, cols] = pre_grad
        up_sums[:, cols] += fold8(pre_grad.astype(F32))
        term = nt(pre_grad, up_weight(core, own_up, got_a, got_b, chunk))
        second_grad = term if second_grad is None else second_grad + term
    xhat = xhat_two[...]
    sums[0:8, :] += fold8(second_grad * xhat)
    sums[8:16, :] += fold8(second_grad)
    residual_grad = out_grad[...] + norm_back(
        xhat, scale_two[:, :1], gains[1:2, :], second_grad
    )
    sums[16:24, :] += fold8(residual_grad)
    residual_grad_out[...] = residual_grad
    residual_low = residual_grad.astype(BF16)
    residual_low_out[...] = residual_low
    grad_own[...] = nt(residual_low, out_weight[mine, :]).astype(BF16)
    grad_oth[...] = nt(residual_low, out_weight[theirs, :]).astype(BF16)


def row_block(cols):
    return pl.BlockSpec((BLK, cols), lambda i, *_: (i, 0))


def held(shape):
    return pl.BlockSpec(shape, lambda *_: (0,) * len(shape))


def row_call(kernel, name, scal, rowed, wholes, row_outs, held_outs, scratch, flops):
    rows = rowed[0].shape[0]
    nbytes = sum(x.size * x.dtype.itemsize for x in wholes)
    nbytes += rows * sum(c * (2 if t == BF16 else 4) for c, t in row_outs)
    return pl.pallas_call(
        kernel,
        grid_spec=pltpu.PrefetchScalarGridSpec(
            num_scalar_prefetch=1,
            grid=(rows // BLK,),
            in_specs=[row_block(x.shape[1]) for x in rowed] + [whole(x.shape) for x in wholes],
            out_specs=[row_block(cols) for cols, _ in row_outs] + [held(s) for s in held_outs],
            scratch_shapes=scratch,
        ),
        out_shape=[jax.ShapeDtypeStruct((rows, cols), t) for cols, t in row_outs]
        + [jax.ShapeDtypeStruct(s, F32) for s in held_outs],
        compiler_params=params(1),
        cost_estimate=cost(flops, nbytes),
        name=name,
    )(scal, *rowed, *wholes)


def ahead(scal, mixed_own, mixed_oth, packed, cot, weights, up_offset, small, frames_here):
    rows, share = mixed_own.shape
    width = packed.shape[1]
    hidden = up_offset.size
    return row_call(
        functools.partial(ahead_kernel, frames_here),
        "ahead",
        scal,
        [mixed_own, mixed_oth, packed],
        [cot, *weights, up_offset, *small],
        [
            (width, F32),
            (width, F32),
            (128, F32),
            (hidden, BF16),
            (hidden, F32),
            (width, BF16),
            (width, BF16),
        ],
        [(24, width), (128, width), (128, width), (8, 128)],
        [pltpu.VMEM((2 * share, width), BF16)],
        2 * rows * width * (2 * hidden + width),
    )


def behind(scal, out_grad, out_low, xhat_two, scale_two, slope, weights, gains):
    rows, width = out_grad.shape
    share = weights[0].shape[0]
    hidden = slope.shape[1]
    return row_call(
        behind_kernel,
        "behind",
        scal,
        [out_grad, out_low, xhat_two, scale_two, slope],
        [*weights, gains],
        [(width, F32), (share, BF16), (share, BF16), (hidden, BF16), (width, BF16)],
        [(24, width), (8, hidden)],
        [pltpu.VMEM((2 * share, width), BF16)],
        2 * rows * width * (2 * hidden + width),
    )


def down_grad_kernel(hidden, out_low, out):
    out[0] = tn(hidden[...], out_low[...]).astype(BF16)


def down_grad(hidden, out_low, odd):
    rows, width = out_low.shape
    hid = hidden.shape[1] // 4
    return pl.pallas_call(
        down_grad_kernel,
        grid=(2,),
        in_specs=[
            pl.BlockSpec((rows, hid), lambda n: (0, 2 * n + odd)),
            whole((rows, width)),
        ],
        out_specs=pl.BlockSpec((1, hid, width), lambda n: (n, 0, 0)),
        out_shape=jax.ShapeDtypeStruct((2, hid, width), BF16),
        compiler_params=params(1),
        cost_estimate=cost(4 * rows * hid * width, 8 * rows * hid),
        name="down_grad",
    )(hidden, out_low)


def up_grad_kernel(odd, scal, second, pre_grad, mixed_own, mixed_oth, residual_low, out):
    step = pl.program_id(0)
    core, plane = scal[0], scal[1]
    width, hid = second.shape[1], pre_grad.shape[1]
    share = mixed_own.shape[1]
    out[0, :width, :] = tn(second[...], pre_grad[...]).astype(BF16)
    side = jnp.where(step == 0, 1 - plane, plane)
    column = core if odd else 1 - core
    lhs = jnp.where(side == core, mixed_own[...], mixed_oth[...])
    rhs = residual_low[:, pl.ds(pl.multiple_of(column * (width // 2), 128), width // 2)]
    grad = tn(lhs, rhs).astype(BF16)
    out[0, width:, : width // 2] = grad[: share // 2]
    out[0, width:, width // 2 :] = grad[share // 2 :]


def up_grad(scal, second, pre_grad, mixed_own, mixed_oth, residual_low, odd):
    rows, width = second.shape
    hid = pre_grad.shape[1] // 4
    share = mixed_own.shape[1]
    return pl.pallas_call(
        functools.partial(up_grad_kernel, odd),
        grid_spec=pltpu.PrefetchScalarGridSpec(
            num_scalar_prefetch=1,
            grid=(2,),
            in_specs=[
                whole((rows, width)),
                pl.BlockSpec((rows, hid), lambda n, *_: (0, 2 * n + odd)),
                whole((rows, share)),
                whole((rows, share)),
                whole((rows, width)),
            ],
            out_specs=pl.BlockSpec((1, width + share // 2, hid), lambda n, *_: (n, 0, 0)),
        ),
        out_shape=jax.ShapeDtypeStruct((2, width + share // 2, hid), BF16),
        compiler_params=params(1),
        cost_estimate=cost(4 * rows * hid * width * 1.25, 10 * rows * hid),
        name="up_grad",
    )(scal, second, pre_grad, mixed_own, mixed_oth, residual_low)


def attend_back_kernel(
    frames_here,
    scal,
    k,
    v,
    kfeat,
    q,
    qfeat,
    grad_own,
    grad_oth,
    wide,
    log_total,
    out_oth,
    out_own,
    queries,
    grads,
    inner,
    dq,
    dka,
    dkb,
    dva,
    dvb,
):
    step = pl.program_id(1)
    blocks = pl.num_programs(1)
    half = blocks // 2
    flip = half * (1 - scal[0])
    edge = clip_edge(scal[2], frames_here, half * BLK)
    low, high = clip_span(step ^ flip, edge, blocks)
    lane = lax.broadcasted_iota(jnp.int32, (BLK, 128), 1)
    left = lane < HEAD_DIM
    none = jnp.zeros((BLK, 128), BF16)

    @pl.when(step == 0)
    def _():
        dq[...] = jnp.zeros_like(dq)
        half_rows = grad_oth.shape[0]
        grads[:half_rows, :] = grad_oth[...]
        grads[half_rows:, :] = grad_own[...]

        def prepare(block, carry):
            rows = pl.ds(pl.multiple_of(block * BLK, BLK), BLK)
            queries[rows, :128] = q[rows, :]
            queries[rows, 128:] = qfeat[rows, :]
            product = (grads[rows, :].astype(F32) * wide[rows, :]).T
            inner[block, 0:1] = jnp.sum(product[:HEAD_DIM], axis=0, keepdims=True)
            inner[block, 1:2] = jnp.sum(product[HEAD_DIM:], axis=0, keepdims=True)
            return carry

        lax.fori_loop(0, q.shape[0] // BLK, prepare, 0)

    ka = jnp.where(left, k[...], none)
    kb = jnp.where(left, none, k[...])
    key_a = jnp.concatenate([ka, kfeat[...]], axis=1)
    key_b = jnp.concatenate([kb, kfeat[...]], axis=1)
    keys = jnp.concatenate([ka, kb], axis=0)
    va = jnp.where(left, v[...], none)
    vb = jnp.where(left, none, v[...])
    for ref in (dka, dkb, dva, dvb):
        ref[...] = jnp.zeros_like(ref)

    def pair(block, carry):
        local = block ^ flip
        rows = pl.ds(pl.multiple_of(local * BLK, BLK), BLK)
        query = queries[rows, :]
        grad = grads[rows, :]
        soft_a = jnp.exp(nt(key_a, query) - log_total[0, local, 0:1])
        soft_b = jnp.exp(nt(key_b, query) - log_total[0, local, 1:2])
        score_a = (soft_a * (nt(va, grad) - inner[local, 0:1])).astype(BF16)
        score_b = (soft_b * (nt(vb, grad) - inner[local, 1:2])).astype(BF16)
        dva[...] += nn(soft_a.astype(BF16), grad)
        dvb[...] += nn(soft_b.astype(BF16), grad)
        dka[...] += nn(score_a, query[:, :128])
        dkb[...] += nn(score_b, query[:, :128])
        dq[rows, :] += tn(jnp.concatenate([score_a, score_b], axis=0), keys)
        return carry

    lax.fori_loop(low, high, pair, 0)
    dk = jnp.where(left, dka[...], dkb[...]).astype(BF16)
    dv = jnp.where(left, dva[...], dvb[...]).astype(BF16)

    within = pl.ds(pl.multiple_of(lax.rem(step, half) * BLK, BLK), BLK)

    @pl.when(step < half)
    def _():
        out_oth[within, 128:256] = dk
        out_oth[within, 256:] = dv

    @pl.when(step >= half)
    def _():
        out_own[within, 128:256] = dk
        out_own[within, 256:] = dv

    @pl.when(step == blocks - 1)
    def _():
        half_rows = out_oth.shape[0]
        out_oth[:, :128] = (dq[:half_rows, :] * HEAD_DIM**-0.5).astype(BF16)
        out_own[:, :128] = (dq[half_rows:, :] * HEAD_DIM**-0.5).astype(BF16)


def attend_back(
    scal, qkv, qfeat, kfeat, grad_own, grad_oth, wide, log_total, frames_here, pair, place
):
    rows = qkv.shape[0]
    pairs = qkv.shape[1] // 384
    blocks = rows // BLK
    return pl.pallas_call(
        functools.partial(attend_back_kernel, frames_here),
        grid_spec=pltpu.PrefetchScalarGridSpec(
            num_scalar_prefetch=1,
            grid=(1, blocks),
            in_specs=[
                pl.BlockSpec((BLK, 128), lambda p, j, *_: (j, pairs + pair)),
                pl.BlockSpec((BLK, 128), lambda p, j, *_: (j, 2 * pairs + pair)),
                pl.BlockSpec((BLK, 128), lambda p, j, *_: (j, 0)),
                pl.BlockSpec((rows, 128), lambda p, j, *_: (0, pair)),
                pl.BlockSpec((rows, 128), lambda p, j, *_: (0, 0)),
                pl.BlockSpec((rows // 2, 128), lambda p, j, *_: (0, pair)),
                pl.BlockSpec((rows // 2, 128), lambda p, j, *_: (0, pair)),
                pl.BlockSpec((rows, 128), lambda p, j, *_: (0, place)),
                pl.BlockSpec((1, blocks, 8, BLK), lambda p, j, *_: (place, 0, 0, 0)),
            ],
            out_specs=[pl.BlockSpec((rows // 2, 384), lambda p, j, *_: (0, 0))] * 2,
            scratch_shapes=[
                pltpu.VMEM((rows, 256), BF16),
                pltpu.VMEM((rows, 128), BF16),
                pltpu.VMEM((blocks, 8, BLK), F32),
                pltpu.VMEM((rows, 128), F32),
            ]
            + [pltpu.VMEM((BLK, 128), F32)] * 4,
        ),
        out_shape=[jax.ShapeDtypeStruct((rows // 2, 384), BF16)] * 2,
        compiler_params=params(2),
        cost_estimate=cost(40 * rows * rows * 128, 30 * rows * 128),
        name="attend_back",
    )(scal, qkv, qkv, kfeat, qkv, qfeat, grad_own, grad_oth, wide, log_total)


def project_grad_kernel(scal, first, oth, own, theirs, mine, offsets):
    core = scal[0]
    half = oth.shape[0]
    quarter = first.shape[1] // 2
    for target, side in ((theirs, 1 - core), (mine, core)):
        cols = pl.ds(pl.multiple_of(side * quarter, 128), quarter)
        target[...] = (tn(first[:half, cols], oth[...]) + tn(first[half:, cols], own[...])).astype(
            BF16
        )
    offsets[0:8, :] = fold8(oth[...].astype(F32)) + fold8(own[...].astype(F32))


def project_grad(scal, first, oth, own):
    rows, width = first.shape
    cols = oth.shape[1]
    return pl.pallas_call(
        project_grad_kernel,
        grid_spec=pltpu.PrefetchScalarGridSpec(
            num_scalar_prefetch=1,
            grid=(1,),
            in_specs=[whole((rows, width))] + [whole((rows // 2, cols))] * 2,
            out_specs=[
                whole((width // 2, cols)),
                whole((width // 2, cols)),
                whole((8, cols)),
            ],
        ),
        out_shape=[
            jax.ShapeDtypeStruct((width // 2, cols), BF16),
            jax.ShapeDtypeStruct((width // 2, cols), BF16),
            jax.ShapeDtypeStruct((8, cols), F32),
        ],
        compiler_params=params(1),
        cost_estimate=cost(2 * rows * width * cols, 2 * rows * (width + cols)),
        name="project_grad",
    )(scal, first, oth, own)


def first_grad_kernel(pairs, *refs):
    own, got = refs[:pairs], refs[pairs : 2 * pairs]
    mine, theirs, tokens, out, sums = refs[2 * pairs :]
    share = 128 * pairs
    total = None
    for weight, parts in ((mine, own), (theirs, got)):
        for pair, ref in enumerate(parts):
            for part in range(3):
                low = part * share + pair * 128
                term = nt(ref[:, part * 128 : (part + 1) * 128], weight[:, low : low + 128])
                total = term if total is None else total + term
    out[...] = total.astype(BF16)

    @pl.when(pl.program_id(0) == 0)
    def _():
        sums[...] = jnp.zeros_like(sums)

    xhat, _ = centre(tokens[...].astype(F32))
    sums[0:8, :] += fold8(total * xhat)
    sums[8:16, :] += fold8(total)


def first_grad(own, got, mine, theirs, packed):
    pairs = len(own)
    rows, cols = own[0].shape
    width = mine.shape[0]
    return pl.pallas_call(
        functools.partial(first_grad_kernel, pairs),
        grid=(rows // BLK,),
        in_specs=[pl.BlockSpec((BLK, cols), lambda i: (i, 0))] * (2 * pairs)
        + [whole(mine.shape), whole(theirs.shape), pl.BlockSpec((BLK, width), lambda i: (i, 0))],
        out_specs=[
            pl.BlockSpec((BLK, width), lambda i: (i, 0)),
            pl.BlockSpec((16, width), lambda i: (0, 0)),
        ],
        out_shape=[
            jax.ShapeDtypeStruct((rows, width), BF16),
            jax.ShapeDtypeStruct((16, width), F32),
        ],
        compiler_params=params(1),
        cost_estimate=cost(
            4 * pairs * rows * width * cols, 4 * pairs * rows * cols + 4 * width * cols * pairs
        ),
        name="first_grad",
    )(*own, *got, mine, theirs, packed)


def last_kernel(tokens, grad, residual_grad, gain, out):
    xhat, scale = centre(tokens[...].astype(F32))
    wide = grad[...].astype(F32)
    out[...] = residual_grad[...] + norm_back(xhat, scale, gain[...], wide)


def last(packed, grad, residual_grad, gain, tokens_here):
    rows, width = grad.shape
    block = pl.BlockSpec((BLK, width), lambda i: (i, 0))
    return pl.pallas_call(
        last_kernel,
        grid=(rows // BLK,),
        in_specs=[block, block, block, whole((1, width))],
        out_specs=block,
        out_shape=jax.ShapeDtypeStruct((tokens_here, width), F32),
        compiler_params=params(1),
        cost_estimate=cost(20 * rows * width, 12 * rows * width),
        name="last",
    )(packed, grad, residual_grad, gain)


def body(
    tokens,
    frame_counts,
    norm_gains,
    norm_shifts,
    attend_weight,
    attend_offset,
    output_weight,
    output_offset,
    expand_weight,
    expand_offset,
    contract_weight,
    contract_offset,
    learner_weight,
    learner_offset,
    pooled_cotangent,
):
    tokens_here, width = tokens.shape
    frames_here = tokens_here // FRAME_TOK
    half_rows = -(-tokens_here // BLK) * BLK
    share = attend_weight.shape[2]
    hid = contract_weight.shape[0] // 2
    chips = lax.axis_size("chip")
    core, plane = lax.axis_index("core"), lax.axis_index("mp")
    straight = core == plane
    flip2 = [(0, 1), (1, 0)]

    def turn(x):
        return jnp.where(straight, x, lax.ppermute(x, ("core", "mp"), [(1, 2), (2, 1)]))

    def to_core(x):
        return lax.ppermute(x, "core", flip2)

    def to_plane(x):
        return lax.ppermute(x, "mp", flip2)

    packed = pack(tokens, pooled_cotangent.reshape(frames_here * MAPS, width), half_rows)
    small = jnp.concatenate(
        [
            attend_offset,
            jnp.broadcast_to(frame_counts[0, 0].astype(F32), (2, 128)),
        ],
        axis=1,
    )
    small = turn(small)
    expand_got = to_plane(after(expand_offset, small))
    own = turn(after(packed, small))
    weight_here = turn(after(attend_weight.reshape(width, 3 * share), small))
    oth = to_core(own)
    count = small[0, share].astype(jnp.int32)
    scal = jnp.stack([core.astype(jnp.int32), plane.astype(jnp.int32), count])
    offset = jnp.concatenate([small[0, :share], jnp.zeros((share,), F32), small[1, :share]])[None]

    quarter = jnp.concatenate(
        [
            lax.dynamic_slice_in_dim(contract_weight, core * hid, hid, 0),
            lax.dynamic_slice_in_dim(expand_weight, core * hid, hid, 1),
            lax.dynamic_slice_in_dim(output_weight, core * (share // 2), share // 2, 0),
        ],
        axis=0,
    )
    got_a = to_plane(after(quarter, weight_here, oth, expand_got))
    up_offset = jnp.where(
        plane == 0,
        jnp.concatenate([expand_offset, expand_got]),
        jnp.concatenate([expand_got, expand_offset]),
    ).reshape(4, hid)

    first, qkv, qfeat, kfeat = project(
        scal,
        oth,
        own,
        norm_gains[0:1],
        norm_shifts[0:1],
        weight_here,
        offset,
        frames_here,
        half_rows,
    )
    pairs = share // 128
    early = pairs - 1
    send_one, own_one, wide_one, logs_one = attend(scal, qkv, qfeat, kfeat, frames_here, 0, early)
    got_one = to_core(send_one)
    got_b = to_core(after(got_a, own_one))
    weight_there = to_core(after(weight_here, own_one))
    send_two, own_two, wide_two, logs_two = attend(
        after(scal, own_one), qkv, qfeat, kfeat, frames_here, early, pairs - early
    )
    got_two = to_core(send_two)
    mixed_own = jnp.concatenate([own_one, own_two], axis=1)
    mixed_oth = jnp.concatenate([got_one, got_two], axis=1)

    maps_all = frames_here * MAPS
    cot = jnp.pad(own[half_rows:], ((0, 128 - maps_all), (0, 0)))
    learner = jnp.pad(jnp.tile(learner_weight.T, (frames_here, 1)), ((0, 128 - maps_all), (0, 0)))
    learner_bias = jnp.pad(jnp.tile(learner_offset, frames_here), (0, 128 - maps_all))[None]
    weights = (output_weight, expand_weight, contract_weight, got_a, got_b)
    (
        out_grad,
        xhat_two,
        scale_two,
        hidden,
        slope,
        second,
        out_low,
        sums_ahead,
        pooled,
        learner_sums,
        learner_offset_sums,
    ) = ahead(
        scal,
        mixed_own,
        mixed_oth,
        own,
        cot,
        weights,
        up_offset,
        (
            norm_gains,
            norm_shifts,
            output_offset[None],
            contract_offset[None],
            learner,
            learner_bias,
        ),
        frames_here,
    )

    chip = lax.axis_index("chip")
    side = chip % 2
    hops = []
    while (2 << len(hops)) < chips:
        hops.append(2 << len(hops))

    def hop(x, step):
        return lax.ppermute(x, "chip", [(i, i ^ step) for i in range(chips)])

    def low(x):
        return x.astype(BF16)

    def plus(a, b):
        return a.astype(F32) + b.astype(F32)

    def pick(x, index):
        return lax.dynamic_index_in_dim(x, index, 0, keepdims=False)

    def halves_of(x):
        rows = x.shape[-2] // 2
        return x.reshape(*x.shape[:-2], 2, rows, x.shape[-1])

    def join(x, other, index, axis):
        return jnp.concatenate(
            [jnp.where(index == 0, x, other), jnp.where(index == 0, other, x)], axis=axis
        )

    down_theirs = down_grad(hidden, out_low, 0)
    down_got = to_core(down_theirs)
    down_mine = down_grad(hidden, after(out_low, down_theirs), 1)
    down_send = low(plus(down_got[0], down_mine[0]))
    down_keep = plus(down_got[1], down_mine[1])
    down_plane = to_plane(down_send)

    (
        residual_grad,
        grad_own,
        grad_send,
        pre_grad,
        residual_low,
        sums_behind,
        up_sums,
    ) = behind(
        after(scal, down_send),
        out_grad,
        out_low,
        xhat_two,
        scale_two,
        slope,
        weights,
        norm_gains,
    )
    grad_oth = to_core(grad_send)
    up_theirs = up_grad(scal, second, pre_grad, mixed_own, mixed_oth, residual_low, 0)
    up_got = to_core(up_theirs)
    down_half = halves_of(plus(down_keep, after(down_plane, up_theirs)))
    down_x_send = low(pick(down_half, 1 - side))
    down_x_keep = pick(down_half, side)
    down_x = hop(down_x_send, 1)
    up_mine = up_grad(
        after(scal, up_theirs, down_x_send),
        second,
        pre_grad,
        mixed_own,
        mixed_oth,
        residual_low,
        1,
    )
    up_half = halves_of(plus(up_got, up_mine))
    up_x_send = low(lax.dynamic_index_in_dim(up_half, 1 - side, 1, keepdims=False))
    up_x_keep = lax.dynamic_index_in_dim(up_half, side, 1, keepdims=False)
    up_x = hop(up_x_send, 1)

    def back(pair, *gate):
        wide, logs, place = (
            (wide_one, logs_one, pair) if pair < early else (wide_two, logs_two, pair - early)
        )
        return attend_back(
            after(scal, *gate),
            qkv,
            qfeat,
            kfeat,
            grad_own,
            grad_oth,
            wide,
            logs,
            frames_here,
            pair,
            place,
        )

    def project_fold(their, mine):
        got = to_core(their)
        return jnp.where(straight, got, mine), jnp.where(straight, mine, got)

    oth_0, own_0 = back(0, up_x_send)
    got_0 = to_core(oth_0)
    down_z = plus(down_x_keep, after(down_x, oth_0))
    down_z_low = low(down_z)
    down_z_got = hop(down_z_low, hops[0])
    up_y = plus(up_x_keep, after(up_x, oth_0))
    up_y_send = low(up_y[0])
    up_y_got = to_plane(up_y_send)
    their_0, mine_0, offsets_0 = project_grad(after(scal, down_z_low, up_y_send), first, oth_0, own_0)

    oth_1, own_1 = back(1, their_0)
    got_1 = to_core(oth_1)
    down_z = plus(down_z, after(down_z_got, oth_1))
    down_z_low = low(down_z)
    down_z_got = hop(down_z_low, hops[1])
    up_z = plus(up_y[1], after(up_y_got, oth_1))
    up_z_low = low(up_z)
    up_z_got = hop(up_z_low, hops[0])
    their_1, mine_1, offsets_1 = project_grad(after(scal, down_z_low, up_z_low), first, oth_1, own_1)
    early_send, early_keep = project_fold(
        jnp.concatenate([their_0, their_1], axis=1), jnp.concatenate([mine_0, mine_1], axis=1)
    )
    early_got = to_plane(early_send)

    residual_back = turn(after(residual_grad, oth_1))
    pooled_back = turn(after(pooled[:maps_all], oth_1))
    oth_2, own_2 = back(2, their_1, early_send)
    got_2 = to_core(oth_2)
    down_z = plus(down_z, after(down_z_got, oth_2))
    up_z = plus(up_z, after(up_z_got, oth_2))
    for step in hops[2:]:
        down_z = plus(down_z, hop(low(down_z), step))
    down_z_low = low(down_z)
    down_x_got = hop(down_z_low, 1)
    up_z_low = low(up_z)
    up_z_got = hop(up_z_low, hops[1])
    their_2, mine_2, offsets_2 = project_grad(after(scal, down_z_low, up_z_low), first, oth_2, own_2)
    late_send, late_keep = project_fold(their_2, mine_2)
    late_got = to_plane(late_send)
    early_half = halves_of(plus(early_keep, after(early_got, their_2)))
    early_x_send = low(pick(early_half, 1 - side))
    early_x_keep = pick(early_half, side)
    early_x = hop(early_x_send, 1)

    first_low, first_sums = first_grad(
        (own_0, own_1, own_2),
        (got_0, got_1, got_2),
        weight_here,
        weight_there,
        after(own, late_send, early_x_send),
    )
    first_back = turn(first_low)

    def finish(send, keep, got, steps):
        total = plus(keep, got)
        for step in steps:
            total = plus(total, hop(low(total), step))
        total = low(total)
        return join(total, hop(total, 1), side, 0)

    late_half = halves_of(plus(late_keep, late_got))
    late_x_send = low(pick(late_half, 1 - side))
    late_sum = finish(None, pick(late_half, side), hop(late_x_send, 1), hops)
    early_sum = finish(None, early_x_keep, early_x, hops)
    up_z = plus(up_z, up_z_got)
    for step in hops[2:]:
        up_z = plus(up_z, hop(low(up_z), step))
    up_z = low(up_z)
    up_sum = join(up_z, hop(up_z, 1), side, 0)
    down_sum = join(down_z_low, down_x_got, side, 0)

    tokens_gradient = last(packed, first_back, residual_back, norm_gains[0:1], tokens_here)

    col = jnp.sum(jnp.concatenate([sums_ahead, sums_behind, first_sums]).reshape(8, 8, width), axis=1)
    learner_part = jnp.sum(learner_sums[:maps_all].reshape(frames_here, MAPS, width), axis=0)
    learner_offset_part = jnp.sum(
        jnp.sum(learner_offset_sums, axis=0)[:maps_all].reshape(frames_here, MAPS), axis=0
    )
    up_part = jnp.sum(up_sums, axis=0).reshape(2, 2, hid)
    up_part = jnp.where(plane == 1, up_part, up_part[::-1])
    up_part = jnp.where(core == 1, up_part, up_part[:, ::-1]).reshape(4, hid)
    offset_all = jnp.stack([jnp.sum(x, axis=0) for x in (offsets_0, offsets_1, offsets_2)])
    offset_part = jnp.stack([offset_all[:, :128].reshape(share), offset_all[:, 256:].reshape(share)])
    offset_part = jnp.where(
        core == 0,
        jnp.pad(offset_part, ((0, 0), (0, share))),
        jnp.pad(offset_part, ((0, 0), (share, 0))),
    )
    table = jnp.concatenate(
        [
            col[6:7],
            col[3:4],
            col[0:1],
            col[7:8],
            col[4:5],
            col[1:2],
            col[5:6],
            col[2:3],
            learner_part,
            jnp.pad(learner_offset_part, (0, width - MAPS))[None],
            up_part,
            offset_part,
        ],
        axis=0,
    )
    table = table + to_core(table)
    table = table + to_plane(table)
    for step in [1, *hops]:
        table = table + hop(table, step)

    def two(x):
        other = to_core(x)
        return jnp.where(core == 0, x, other), jnp.where(core == 0, other, x)

    def out_block(x):
        return jnp.concatenate([x[width:, : width // 2], x[width:, width // 2 :]], axis=0)

    down_low, down_high = two(down_sum)
    up_low, up_high = two(up_sum)
    contract_gradient = jnp.concatenate([down_low, down_high], axis=0).astype(F32)
    expand_gradient = jnp.concatenate([up_low[:width], up_high[:width]], axis=1).astype(F32)
    output_gradient = jnp.concatenate([out_block(up_low), out_block(up_high)], axis=1).astype(F32)

    halves = [two(early_sum), two(late_sum)]
    columns = []
    for part in range(3):
        for pair in range(pairs):
            first_half, second_half = halves[0] if pair < early else halves[1]
            at = (pair if pair < early else pair - early) * 384 + part * 128
            columns.append(
                jnp.concatenate(
                    [first_half[:, at : at + 128], second_half[:, at : at + 128]], axis=0
                )
            )
    attend_gradient = jnp.concatenate(columns, axis=1).astype(F32).reshape(width, 3, share)
    return (
        pooled_back.reshape(frames_here, MAPS, width),
        tokens_gradient,
        table[0:3],
        table[3:6],
        attend_gradient,
        lax.dynamic_slice_in_dim(table[21:23], plane * share, share, 1),
        output_gradient,
        table[6],
        expand_gradient,
        lax.dynamic_slice_in_dim(table[17:21], 2 * plane, 2, 0).reshape(2 * hid),
        contract_gradient,
        table[7],
        table[8:16].T,
        table[16, :MAPS],
    )


def solution(mesh):
    groups, sides = mesh.devices.shape
    fine = Mesh(mesh.devices.reshape(groups // 2, 2, sides), ("chip", "core", "mp"))
    dp = ("chip", "core")
    every = ("chip", "core", "mp")
    return jax.shard_map(
        body,
        mesh=fine,
        in_specs=(
            P(every, None),
            P(dp, None),
            P(),
            P(),
            P(None, None, "mp"),
            P(None, "mp"),
            P("mp", None),
            P(),
            P(None, "mp"),
            P("mp"),
            P("mp", None),
            P(),
            P(),
            P(),
            P(every, None, None),
        ),
        out_specs=(
            P(every, None, None),
            P(every, None),
            P(),
            P(),
            P(None, None, "mp"),
            P(None, "mp"),
            P("mp", None),
            P(),
            P(None, "mp"),
            P("mp"),
            P("mp", None),
            P(),
            P(),
            P(),
        ),
        check_vma=False,
    )
```

```python
import functools

import jax
import jax.numpy as jnp
from jax import lax
from jax.experimental import pallas as pl
from jax.experimental.pallas import tpu as pltpu
from jax.sharding import Mesh, PartitionSpec as P

HEAD_DIM = 64
MAPS = 8
FRAME_TOK = 196
EPS = 1e-06
BLK = 256
COST = 20.0
FAR = 1e30
GELU_C = 0.7978845608028654
GELU_A = 0.044715

F32 = jnp.float32
BF16 = jnp.bfloat16


def nn(a, b):
    return lax.dot_general(a, b, (((1,), (0,)), ((), ())), preferred_element_type=F32)


def nt(a, b):
    return lax.dot_general(a, b, (((1,), (1,)), ((), ())), preferred_element_type=F32)


def tn(a, b):
    return lax.dot_general(a, b, (((0,), (0,)), ((), ())), preferred_element_type=F32)


def fold8(values):
    rows, width = values.shape
    return jnp.sum(values.reshape(rows // 8, 8, width), axis=0)


def centre(values):
    average = jnp.mean(values, axis=-1, keepdims=True)
    centred = values - average
    spread = jnp.mean(centred * centred, axis=-1, keepdims=True)
    scale = lax.rsqrt(spread + EPS)
    return centred * scale, scale


def norm_back(xhat, scale, gain, grad):
    scaled = grad * gain
    along = jnp.mean(scaled * xhat, axis=-1, keepdims=True)
    return scale * (scaled - jnp.mean(scaled, axis=-1, keepdims=True) - xhat * along)


def cost(flops, nbytes):
    return pl.CostEstimate(
        flops=int(flops * COST), bytes_accessed=int(nbytes * COST), transcendentals=0
    )


def params(n):
    return pltpu.CompilerParams(
        dimension_semantics=("arbitrary",) * n, vmem_limit_bytes=60 * 1024 * 1024
    )


def whole(shape):
    return pl.BlockSpec(shape, lambda *_: (0,) * len(shape), pipeline_mode=pl.Buffered(1))


def after(value, *others):
    return lax.optimization_barrier((value, others))[0]


def pack_kernel(tokens, cot, out):
    here = tokens.shape[0]
    rows = out.shape[0] - cot.shape[0]
    edge = here // 16 * 16
    out[edge:, :] = jnp.zeros_like(out[edge:, :])
    out[:here, :] = tokens[...]
    out[rows:, :] = cot[...]


def pack(tokens, cot, half_rows):
    rows, width = half_rows + cot.shape[0], tokens.shape[1]
    return pl.pallas_call(
        pack_kernel,
        in_specs=[pl.BlockSpec(tokens.shape), pl.BlockSpec(cot.shape)],
        out_specs=pl.BlockSpec((rows, width)),
        out_shape=jax.ShapeDtypeStruct((rows, width), BF16),
        compiler_params=pltpu.CompilerParams(vmem_limit_bytes=16 * 1024 * 1024),
        cost_estimate=cost(0, 4 * rows * width),
        name="pack",
    )(tokens, cot)


def project_kernel(
    frames_here, scal, oth, own, gain, shift, weight, offset, first, qkv, qfeat, kfeat
):
    step = pl.program_id(0)
    half_blocks = pl.num_programs(0) // 2
    half_rows = half_blocks * BLK
    within = lax.rem(step, half_blocks) * BLK
    rows = pl.ds(pl.multiple_of(within, BLK), BLK)
    values = jnp.where(step < half_blocks, oth[rows, :], own[rows, :]).astype(F32)
    xhat, _ = centre(values)
    low = (xhat * gain[...] + shift[...]).astype(BF16)
    first[...] = low
    out = (nn(low, weight[...]) + offset[...]).astype(BF16)
    for pair in range(out.shape[1] // 384):
        at = pair * 384
        qkv[:, at : at + 128] = out[:, at : at + 128] * jnp.asarray(HEAD_DIM**-0.5, BF16)
        qkv[:, at + 128 : at + 384] = out[:, at + 128 : at + 384]
    core, count = scal[0], scal[2]
    half = jnp.where(step < half_blocks, 1 - core, core)
    edge = clip_edge(count, frames_here, half_rows)
    token = within + lax.broadcasted_iota(jnp.int32, (BLK, 128), 0)
    lane = lax.broadcasted_iota(jnp.int32, (BLK, 128), 1)
    clip = jnp.where(half * half_rows + token >= edge, 1, 0)
    clip = jnp.where(token >= frames_here * FRAME_TOK, 2, clip)
    hit = lane == clip
    qfeat[...] = jnp.where(hit, 1.0, 0.0).astype(BF16)
    kfeat[...] = jnp.where(hit, 0.0, jnp.where(lane < 3, -FAR, 0.0)).astype(BF16)


def clip_edge(count, frames_here, half_rows):
    return jnp.where(
        count <= frames_here,
        count * FRAME_TOK,
        half_rows + (count - frames_here) * FRAME_TOK,
    )


def clip_span(block, edge, blocks):
    low = jnp.where(block * BLK >= edge, edge // BLK, 0)
    high = jnp.where(block * BLK + BLK - 1 < edge, (edge + BLK - 1) // BLK, blocks)
    return low, high


def project(scal, oth, own, gain, shift, weight, offset, frames_here, half_rows):
    width, cols = weight.shape
    steps = 2 * half_rows // BLK
    rows = 2 * half_rows
    return pl.pallas_call(
        functools.partial(project_kernel, frames_here),
        grid_spec=pltpu.PrefetchScalarGridSpec(
            num_scalar_prefetch=1,
            grid=(steps,),
            in_specs=[
                whole(oth.shape),
                whole(own.shape),
                whole((1, width)),
                whole((1, width)),
                whole((width, cols)),
                whole((1, cols)),
            ],
            out_specs=[
                pl.BlockSpec((BLK, width), lambda i, *_: (i, 0)),
                pl.BlockSpec((BLK, cols), lambda i, *_: (i, 0)),
                pl.BlockSpec((BLK, 128), lambda i, *_: (i, 0)),
                pl.BlockSpec((BLK, 128), lambda i, *_: (i, 0)),
            ],
        ),
        out_shape=[
            jax.ShapeDtypeStruct((rows, width), BF16),
            jax.ShapeDtypeStruct((rows, cols), BF16),
            jax.ShapeDtypeStruct((rows, 128), BF16),
            jax.ShapeDtypeStruct((rows, 128), BF16),
        ],
        compiler_params=params(1),
        cost_estimate=cost(2 * rows * width * cols, 4 * rows * width + 2 * rows * cols),
        name="project",
    )(scal, oth, own, gain, shift, weight, offset)


def attend_kernel(
    frames_here,
    bk,
    shift,
    scal,
    q,
    qfeat,
    qkv,
    kfeat,
    mixed,
    wide,
    log_total,
    scores,
    tops,
    acc,
    keys_all,
    values_all,
):
    step = pl.program_id(0)
    half = pl.num_programs(0)
    blocks = 2 * half
    pairs = q.shape[1] // 384
    flip = half * (1 - scal[0])
    edge = clip_edge(scal[2], frames_here, half * BLK)
    low, high = clip_span((step + shift) ^ flip, edge, blocks)
    per = bk // BLK
    low, high = low // per, (high + per - 1) // per
    kflip = flip // per
    lane = lax.broadcasted_iota(jnp.int32, (BLK, 128), 1)
    left = lane < HEAD_DIM
    none = jnp.zeros((BLK, 128), BF16)
    queries = []
    for pair in range(pairs):
        both = q[:, pair * 384 : pair * 384 + 128]
        queries.append(jnp.concatenate([jnp.where(left, both, none), qfeat[...]], axis=1))
        queries.append(jnp.concatenate([jnp.where(left, none, both), qfeat[...]], axis=1))
    @pl.when(step == 0)
    def _():
        def prepare(block, carry):
            rows = pl.ds(pl.multiple_of(block * BLK, BLK), BLK)
            for pair in range(pairs):
                at = pair * 384
                keys_all[pair, rows, :128] = qkv[rows, at + 128 : at + 256]
                keys_all[pair, rows, 128:] = kfeat[rows, :]
                both = qkv[rows, at + 256 : at + 384]
                values_all[2 * pair, rows, :128] = jnp.where(left, both, none)
                values_all[2 * pair, rows, 128:] = jnp.where(lane == 0, 1.0, 0.0).astype(BF16)
                values_all[2 * pair + 1, rows, :128] = jnp.where(left, none, both)
                values_all[2 * pair + 1, rows, 128:] = jnp.where(lane == 1, 1.0, 0.0).astype(BF16)
            return carry

        lax.fori_loop(0, blocks, prepare, 0)

    for head in range(2 * pairs):
        tops[head] = jnp.full((BLK, 128), -3e38, F32)

    def score(block, carry):
        rows = pl.ds(pl.multiple_of((block ^ kflip) * bk, bk), bk)
        for pair in range(pairs):
            keys = keys_all[pair, rows, :]
            for head in (2 * pair, 2 * pair + 1):
                values = nt(queries[head], keys)
                scores[head, block] = values
                top = tops[head]
                for part in range(bk // 128):
                    top = jnp.maximum(top, values[:, part * 128 : (part + 1) * 128])
                tops[head] = top
        return carry

    lax.fori_loop(low, high, score, 0)
    peaks = []
    for head in range(2 * pairs):
        peaks.append(jnp.max(tops[head], axis=1, keepdims=True))
        tops[head] = jnp.broadcast_to(peaks[-1], (BLK, 128))
    acc[...] = jnp.zeros_like(acc)
    def mix(block, carry):
        rows = pl.ds(pl.multiple_of((block ^ kflip) * bk, bk), bk)
        for pair in range(pairs):
            soft = []
            for head in (2 * pair, 2 * pair + 1):
                top = tops[head]
                for part in range(bk // 128):
                    piece = scores[head, block, :, part * 128 : (part + 1) * 128]
                    soft.append(jnp.exp(piece - top).astype(BF16))
            values = jnp.concatenate(
                [values_all[2 * pair, rows, :], values_all[2 * pair + 1, rows, :]], axis=0
            )
            acc[pair] += nn(jnp.concatenate(soft, axis=1), values)
        return carry

    lax.fori_loop(low, high, mix, 0)
    for pair in range(pairs):
        cols = slice(pair * 128, (pair + 1) * 128)
        total_a, total_b = acc[pair, :, 128:129], acc[pair, :, 129:130]
        out = acc[pair, :, :128] / jnp.where(left, total_a, total_b)
        wide[:, cols] = out
        mixed[:, cols] = out.astype(BF16)

        logs = jnp.where(
            lane == 0,
            peaks[2 * pair] + jnp.log(total_a),
            jnp.where(lane == 1, peaks[2 * pair + 1] + jnp.log(total_b), 0.0),
        )
        log_total[pair, 0] = logs.T[:8]


def attend(scal, qkv, qfeat, kfeat, frames_here, own):
    rows, cols = qkv.shape
    width = cols // 3
    pairs = width // 128
    half = rows // BLK // 2
    bk = rows // 2
    shift = half if own else 0
    return pl.pallas_call(
        functools.partial(attend_kernel, frames_here, bk, shift),
        grid_spec=pltpu.PrefetchScalarGridSpec(
            num_scalar_prefetch=1,
            grid=(half,),
            in_specs=[
                pl.BlockSpec((BLK, cols), lambda i, *_: (i + shift, 0)),
                pl.BlockSpec((BLK, 128), lambda i, *_: (i + shift, 0)),
                whole((rows, cols)),
                whole((rows, 128)),
            ],
            out_specs=[
                pl.BlockSpec((BLK, width), lambda i, *_: (i, 0)),
                pl.BlockSpec((BLK, width), lambda i, *_: (i, 0)),
                pl.BlockSpec((pairs, 1, 8, BLK), lambda i, *_: (0, i, 0, 0)),
            ],
            scratch_shapes=[
                pltpu.VMEM((2 * pairs, rows // bk, BLK, bk), F32),
                pltpu.VMEM((2 * pairs, BLK, 128), F32),
                pltpu.VMEM((pairs, BLK, 256), F32),
                pltpu.VMEM((pairs, rows, 256), BF16),
                pltpu.VMEM((2 * pairs, rows, 256), BF16),
            ],
        ),
        out_shape=[
            jax.ShapeDtypeStruct((rows // 2, width), BF16),
            jax.ShapeDtypeStruct((rows // 2, width), F32),
            jax.ShapeDtypeStruct((pairs, half, 8, BLK), F32),
        ],
        compiler_params=params(1),
        cost_estimate=cost(8 * rows * rows * width, 16 * rows * width),
        name="attend",
    )(scal, qkv, qfeat, qkv, kfeat)


def gather_out_weight(scal, own_out, got_a, got_b, out_weight, hid):
    core, plane = scal[0], scal[1]
    share = own_out.shape[0]
    quarter = share // 2
    out_weight[pl.ds(pl.multiple_of(plane * share, 64), share), :] = own_out[...]
    base = (1 - plane) * share
    out_weight[pl.ds(pl.multiple_of(base + core * quarter, 64), quarter), :] = got_a[
        2 * hid : 2 * hid + quarter, :
    ]
    out_weight[pl.ds(pl.multiple_of(base + (1 - core) * quarter, 64), quarter), :] = got_b[
        2 * hid : 2 * hid + quarter, :
    ]


def up_weight(core, own_up, got_a, got_b, chunk):
    hid = got_a.shape[1]
    if chunk < 2:
        return (got_b, got_a)[chunk][hid : 2 * hid, :]
    pick = (1 - core) if chunk == 2 else core
    return own_up[:, pl.ds(pl.multiple_of(pick * hid, 128), hid)]


def down_weight(core, own_down, got_a, got_b, chunk):
    hid = got_a.shape[1]
    if chunk < 2:
        return (got_b, got_a)[chunk][:hid, :]
    pick = (1 - core) if chunk == 2 else core
    return own_down[pl.ds(pl.multiple_of(pick * hid, 128), hid), :]


def ahead_kernel(
    frames_here,
    scal,
    mixed_own,
    mixed_oth,
    tokens,
    cot,
    own_out,
    own_up,
    own_down,
    got_a,
    got_b,
    up_offset,
    gains,
    shifts,
    out_offset,
    down_offset,
    learner,
    learner_offset,
    out_grad_out,
    xhat_out,
    scale_out,
    hidden_out,
    slope_out,
    second_out,
    out_low_out,
    sums,
    pooled,
    learner_sums,
    learner_offset_sums,
    out_weight,
):
    step = pl.program_id(0)
    core, plane = scal[0], scal[1]
    hid = got_a.shape[1]
    share = own_out.shape[0]

    @pl.when(step == 0)
    def _():
        gather_out_weight(scal, own_out, got_a, got_b, out_weight, hid)
        for ref in (sums, pooled, learner_sums, learner_offset_sums):
            ref[...] = jnp.zeros_like(ref)

    def up_bias(chunk):
        side = (1 - plane) if chunk < 2 else plane
        pick = (1 - core) if chunk % 2 == 0 else core
        return up_offset[pl.ds(2 * side + pick, 1), :]

    mine = pl.ds(pl.multiple_of(core * share, 64), share)
    theirs = pl.ds(pl.multiple_of((1 - core) * share, 64), share)
    attended = nn(mixed_own[...], out_weight[mine, :]) + nn(mixed_oth[...], out_weight[theirs, :])
    residual = tokens[...].astype(F32) + attended + out_offset[...]
    xhat_two, scale_two = centre(residual)
    xhat_out[...] = xhat_two
    scale_out[...] = jnp.broadcast_to(scale_two, scale_out.shape)
    second = (xhat_two * gains[1:2, :] + shifts[1:2, :]).astype(BF16)
    second_out[...] = second
    block_out = residual + down_offset[...]
    for chunk in range(4):
        cols = slice(chunk * hid, (chunk + 1) * hid)
        pre = nn(second, up_weight(core, own_up, got_a, got_b, chunk)) + up_bias(chunk)
        square = pre * pre
        bend = jnp.tanh(GELU_C * (pre + GELU_A * (square * pre)))
        half_up = 0.5 * (1.0 + bend)
        hidden = (pre * half_up).astype(BF16)
        slope_out[:, cols] = half_up + (0.5 * pre) * (1.0 - bend * bend) * (
            GELU_C + (3.0 * GELU_A * GELU_C) * square
        )
        hidden_out[:, cols] = hidden
        block_out = block_out + nn(hidden, down_weight(core, own_down, got_a, got_b, chunk))
    xhat_three, scale_three = centre(block_out)
    third = (xhat_three * gains[2:3, :] + shifts[2:3, :]).astype(BF16)
    logits = nt(third, learner[...]) + learner_offset[...]
    sig = 1.0 / (1.0 + jnp.exp(-logits))
    token = step * BLK + lax.broadcasted_iota(jnp.int32, (BLK, 128), 0)
    first_token = (lax.broadcasted_iota(jnp.int32, (BLK, 128), 1) >> 3) * FRAME_TOK
    inside = (token >= first_token) & (token < first_token + FRAME_TOK)
    inside = inside & (first_token < frames_here * FRAME_TOK)
    maps = jnp.where(inside, sig, 0.0).astype(BF16)
    feature = block_out.astype(BF16)
    pooled[...] += tn(maps, feature)
    maps_grad = nt(feature, cot[...])
    pool_grad = nn(maps, cot[...])
    logits_grad = jnp.where(inside, maps_grad * sig * (1.0 - sig), 0.0).astype(BF16)
    learner_sums[...] += tn(logits_grad, third)
    learner_offset_sums[...] += fold8(logits_grad.astype(F32))
    third_grad = nn(logits_grad, learner[...])
    sums[0:8, :] += fold8(third_grad * xhat_three)
    sums[8:16, :] += fold8(third_grad)
    out_grad = pool_grad + norm_back(xhat_three, scale_three, gains[2:3, :], third_grad)
    sums[16:24, :] += fold8(out_grad)
    out_grad_out[...] = out_grad
    out_low_out[...] = out_grad.astype(BF16)


def behind_kernel(
    pooled_rows,
    scal,
    out_grad,
    out_low,
    xhat_two,
    scale_two,
    slope,
    own_out,
    own_up,
    own_down,
    got_a,
    got_b,
    gains,
    pooled,
    residual_grad_out,
    grad_own,
    grad_oth,
    pre_grad_out,
    residual_low_out,
    sums,
    up_sums,
    out_weight,
):
    core = scal[0]
    hid = got_a.shape[1]
    share = own_out.shape[0]

    @pl.when(pl.program_id(0) == 0)
    def _():
        gather_out_weight(scal, own_out, got_a, got_b, out_weight, hid)
        for ref in (sums, up_sums):
            ref[...] = jnp.zeros_like(ref)

    mine = pl.ds(pl.multiple_of(core * share, 64), share)
    theirs = pl.ds(pl.multiple_of((1 - core) * share, 64), share)
    low = out_low[...]
    second_grad = None
    for chunk in range(4):
        cols = slice(chunk * hid, (chunk + 1) * hid)
        hidden_grad = nt(low, down_weight(core, own_down, got_a, got_b, chunk))
        pre_grad = (hidden_grad * slope[:, cols]).astype(BF16)
        pre_grad_out[:, cols] = pre_grad
        up_sums[:, cols] += fold8(pre_grad.astype(F32))
        term = nt(pre_grad, up_weight(core, own_up, got_a, got_b, chunk))
        second_grad = term if second_grad is None else second_grad + term
    xhat = xhat_two[...]
    sums[0:8, :] += fold8(second_grad * xhat)
    sums[8:16, :] += fold8(second_grad)
    residual_grad = out_grad[...] + norm_back(
        xhat, scale_two[:, :1], gains[1:2, :], second_grad
    )
    sums[16:24, :] += fold8(residual_grad)
    residual_grad_out[...] = residual_grad

    @pl.when(pl.program_id(0) == pl.num_programs(0) - 1)
    def _():
        residual_grad_out[BLK - pooled_rows :, :] = pooled[:pooled_rows, :]

    residual_low = residual_grad.astype(BF16)
    residual_low_out[...] = residual_low
    grad_own[...] = nt(residual_low, out_weight[mine, :]).astype(BF16)
    grad_oth[...] = nt(residual_low, out_weight[theirs, :]).astype(BF16)


def row_block(cols):
    return pl.BlockSpec((BLK, cols), lambda i, *_: (i, 0))


def held(shape):
    return pl.BlockSpec(shape, lambda *_: (0,) * len(shape))


def row_call(kernel, name, scal, rowed, wholes, row_outs, held_outs, scratch, flops):
    rows = rowed[0].shape[0]
    nbytes = sum(x.size * x.dtype.itemsize for x in wholes)
    nbytes += rows * sum(c * (2 if t == BF16 else 4) for c, t in row_outs)
    return pl.pallas_call(
        kernel,
        grid_spec=pltpu.PrefetchScalarGridSpec(
            num_scalar_prefetch=1,
            grid=(rows // BLK,),
            in_specs=[row_block(x.shape[1]) for x in rowed] + [whole(x.shape) for x in wholes],
            out_specs=[row_block(cols) for cols, _ in row_outs] + [held(s) for s in held_outs],
            scratch_shapes=scratch,
        ),
        out_shape=[jax.ShapeDtypeStruct((rows, cols), t) for cols, t in row_outs]
        + [jax.ShapeDtypeStruct(s, F32) for s in held_outs],
        compiler_params=params(1),
        cost_estimate=cost(flops, nbytes),
        name=name,
    )(scal, *rowed, *wholes)


def ahead(scal, mixed_own, mixed_oth, packed, cot, weights, up_offset, small, frames_here):
    rows, share = mixed_own.shape
    width = packed.shape[1]
    hidden = up_offset.size
    return row_call(
        functools.partial(ahead_kernel, frames_here),
        "ahead",
        scal,
        [mixed_own, mixed_oth, packed],
        [cot, *weights, up_offset, *small],
        [
            (width, F32),
            (width, F32),
            (128, F32),
            (hidden, BF16),
            (hidden, F32),
            (width, BF16),
            (width, BF16),
        ],
        [(24, width), (128, width), (128, width), (8, 128)],
        [pltpu.VMEM((2 * share, width), BF16)],
        2 * rows * width * (2 * hidden + width),
    )


def behind(scal, out_grad, out_low, xhat_two, scale_two, slope, weights, gains, pooled, maps_all):
    rows, width = out_grad.shape
    share = weights[0].shape[0]
    hidden = slope.shape[1]
    return row_call(
        functools.partial(behind_kernel, maps_all),
        "behind",
        scal,
        [out_grad, out_low, xhat_two, scale_two, slope],
        [*weights, gains, pooled],
        [(width, F32), (share, BF16), (share, BF16), (hidden, BF16), (width, BF16)],
        [(24, width), (8, hidden)],
        [pltpu.VMEM((2 * share, width), BF16)],
        2 * rows * width * (2 * hidden + width),
    )


def down_grad_kernel(hidden, out_low, out):
    out[0] = tn(hidden[...], out_low[...]).astype(BF16)


def down_grad(hidden, out_low, odd):
    rows, width = out_low.shape
    hid = hidden.shape[1] // 4
    return pl.pallas_call(
        down_grad_kernel,
        grid=(2,),
        in_specs=[
            pl.BlockSpec((rows, hid), lambda n: (0, 2 * n + odd)),
            whole((rows, width)),
        ],
        out_specs=pl.BlockSpec((1, hid, width), lambda n: (n, 0, 0)),
        out_shape=jax.ShapeDtypeStruct((2, hid, width), BF16),
        compiler_params=params(1),
        cost_estimate=cost(4 * rows * hid * width, 8 * rows * hid),
        name="down_grad",
    )(hidden, out_low)


def up_grad_kernel(odd, scal, second, pre_grad, mixed_own, mixed_oth, residual_low, out):
    step = pl.program_id(0)
    core, plane = scal[0], scal[1]
    width, hid = second.shape[1], pre_grad.shape[1]
    share = mixed_own.shape[1]
    out[0, :width, :] = tn(second[...], pre_grad[...]).astype(BF16)
    side = jnp.where(step == 0, 1 - plane, plane)
    column = core if odd else 1 - core
    lhs = jnp.where(side == core, mixed_own[...], mixed_oth[...])
    rhs = residual_low[:, pl.ds(pl.multiple_of(column * (width // 2), 128), width // 2)]
    grad = tn(lhs, rhs).astype(BF16)
    out[0, width:, : width // 2] = grad[: share // 2]
    out[0, width:, width // 2 :] = grad[share // 2 :]


def up_grad(scal, second, pre_grad, mixed_own, mixed_oth, residual_low, odd):
    rows, width = second.shape
    hid = pre_grad.shape[1] // 4
    share = mixed_own.shape[1]
    return pl.pallas_call(
        functools.partial(up_grad_kernel, odd),
        grid_spec=pltpu.PrefetchScalarGridSpec(
            num_scalar_prefetch=1,
            grid=(2,),
            in_specs=[
                whole((rows, width)),
                pl.BlockSpec((rows, hid), lambda n, *_: (0, 2 * n + odd)),
                whole((rows, share)),
                whole((rows, share)),
                whole((rows, width)),
            ],
            out_specs=pl.BlockSpec((1, width + share // 2, hid), lambda n, *_: (n, 0, 0)),
        ),
        out_shape=jax.ShapeDtypeStruct((2, width + share // 2, hid), BF16),
        compiler_params=params(1),
        cost_estimate=cost(4 * rows * hid * width * 1.25, 10 * rows * hid),
        name="up_grad",
    )(scal, second, pre_grad, mixed_own, mixed_oth, residual_low)


def attend_back_kernel(
    frames_here,
    scal,
    k,
    v,
    kfeat,
    q,
    qfeat,
    grad_oth,
    grad_own,
    wide_oth,
    wide_own,
    log_oth,
    log_own,
    out_oth,
    out_own,
    queries,
    grads,
    inner,
    logs,
    dq,
    dkv,
):
    step = pl.program_id(0)
    half = grad_oth.shape[0] // BLK
    blocks = 2 * half
    flip = half * (1 - scal[0])
    edge = clip_edge(scal[2], frames_here, half * BLK)
    low, high = clip_span(step ^ flip, edge, blocks)
    bq = half * BLK
    low, high = low // half, (high + half - 1) // half
    qflip = 1 - scal[0]
    lane = lax.broadcasted_iota(jnp.int32, (BLK, 128), 1)
    left = lane < HEAD_DIM
    none = jnp.zeros((BLK, 128), BF16)

    @pl.when(step == 0)
    def _():
        dq[...] = jnp.zeros_like(dq)
        for side, (grad, wide, log_total) in enumerate(
            ((grad_oth, wide_oth, log_oth), (grad_own, wide_own, log_own))
        ):
            for block in range(bq // BLK):
                here = slice(block * BLK, (block + 1) * BLK)
                rows = slice(side * bq + block * BLK, side * bq + (block + 1) * BLK)
                grads[rows, :] = grad[here, :]
                queries[rows, :128] = q[rows, :]
                queries[rows, 128:] = qfeat[rows, :]
                product = (grad[here, :].astype(F32) * wide[here, :]).T
                inner[side, 0:1, here] = jnp.sum(product[:HEAD_DIM], axis=0, keepdims=True)
                inner[side, 1:2, here] = jnp.sum(product[HEAD_DIM:], axis=0, keepdims=True)
                logs[side, :, here] = log_total[0, block]

    ka = jnp.where(left, k[...], none)
    kb = jnp.where(left, none, k[...])
    key_a = jnp.concatenate([ka, kfeat[...]], axis=1)
    key_b = jnp.concatenate([kb, kfeat[...]], axis=1)
    keys = jnp.concatenate([ka, kb], axis=0)
    va = jnp.where(left, v[...], none)
    vb = jnp.where(left, none, v[...])
    dkv[...] = jnp.zeros_like(dkv)

    def pair(block, carry):
        local = block ^ qflip
        rows = pl.ds(pl.multiple_of(local * bq, bq), bq)
        query = queries[rows, :]
        grad = grads[rows, :]
        soft_a = jnp.exp(nt(key_a, query) - logs[local, 0:1])
        soft_b = jnp.exp(nt(key_b, query) - logs[local, 1:2])
        score_a = (soft_a * (nt(va, grad) - inner[local, 0:1])).astype(BF16)
        score_b = (soft_b * (nt(vb, grad) - inner[local, 1:2])).astype(BF16)
        dkv[0] += nn(soft_a.astype(BF16), grad)
        dkv[1] += nn(soft_b.astype(BF16), grad)
        dkv[2] += nn(score_a, query[:, :128])
        dkv[3] += nn(score_b, query[:, :128])
        dq[rows, :] += tn(jnp.concatenate([score_a, score_b], axis=0), keys)
        return carry

    lax.fori_loop(low, high, pair, 0)
    dk = jnp.where(left, dkv[2], dkv[3]).astype(BF16)
    dv = jnp.where(left, dkv[0], dkv[1]).astype(BF16)
    within = pl.ds(pl.multiple_of(lax.rem(step, half) * BLK, BLK), BLK)

    @pl.when(step < half)
    def _():
        out_oth[within, 128:256] = dk
        out_oth[within, 256:] = dv

    @pl.when(step >= half)
    def _():
        out_own[within, 128:256] = dk
        out_own[within, 256:] = dv

    @pl.when(step == blocks - 1)
    def _():
        half_rows = out_oth.shape[0]
        out_oth[:, :128] = (dq[:half_rows, :] * HEAD_DIM**-0.5).astype(BF16)
        out_own[:, :128] = (dq[half_rows:, :] * HEAD_DIM**-0.5).astype(BF16)

def attend_back(scal, qkv, qfeat, kfeat, grad_oth, grad_own, wide, logs, frames_here, pair):
    rows = qkv.shape[0]
    blocks = rows // BLK
    one = pl.Buffered(1)
    half_rows = pl.BlockSpec((rows // 2, 128), lambda j, *_: (0, pair), pipeline_mode=one)
    half_logs = pl.BlockSpec(
        (1, blocks // 2, 8, BLK), lambda j, *_: (pair, 0, 0, 0), pipeline_mode=one
    )
    return pl.pallas_call(
        functools.partial(attend_back_kernel, frames_here),
        grid_spec=pltpu.PrefetchScalarGridSpec(
            num_scalar_prefetch=1,
            grid=(blocks,),
            in_specs=[
                pl.BlockSpec((BLK, 128), lambda j, *_: (j, 3 * pair + 1)),
                pl.BlockSpec((BLK, 128), lambda j, *_: (j, 3 * pair + 2)),
                pl.BlockSpec((BLK, 128), lambda j, *_: (j, 0)),
                pl.BlockSpec((rows, 128), lambda j, *_: (0, 3 * pair), pipeline_mode=one),
                whole((rows, 128)),
                half_rows,
                half_rows,
                half_rows,
                half_rows,
                half_logs,
                half_logs,
            ],
            out_specs=[pl.BlockSpec((rows // 2, 384), lambda j, *_: (0, 0))] * 2,
            scratch_shapes=[
                pltpu.VMEM((rows, 256), BF16),
                pltpu.VMEM((rows, 128), BF16),
                pltpu.VMEM((2, 8, rows // 2), F32),
                pltpu.VMEM((2, 8, rows // 2), F32),
                pltpu.VMEM((rows, 128), F32),
                pltpu.VMEM((4, BLK, 128), F32),
            ],
        ),
        out_shape=[jax.ShapeDtypeStruct((rows // 2, 384), BF16)] * 2,
        compiler_params=params(1),
        cost_estimate=cost(40 * rows * rows * 128, 30 * rows * 128),
        name="attend_back",
    )(scal, qkv, qkv, kfeat, qkv, qfeat, grad_oth, grad_own, *wide, *logs)


def project_grad_kernel(pairs, scal, first, *refs):
    oth, own = refs[:pairs], refs[pairs : 2 * pairs]
    theirs, mine, offsets = refs[2 * pairs :]
    step = pl.program_id(0)
    half = oth[0].shape[0]
    one = jnp.concatenate([x[...] for x in oth], axis=1)
    two = jnp.concatenate([x[...] for x in own], axis=1)
    out = (tn(first[:half, :], one) + tn(first[half:, :], two)).astype(BF16)

    @pl.when(step == 0)
    def _():
        theirs[...] = out
        offsets[...] = fold8(one.astype(F32)) + fold8(two.astype(F32))

    @pl.when(step == 1)
    def _():
        mine[...] = out


def project_grad(scal, first, oth, own):
    pairs = len(oth)
    rows, width = first.shape
    cols = 384 * pairs
    return pl.pallas_call(
        functools.partial(project_grad_kernel, pairs),
        grid_spec=pltpu.PrefetchScalarGridSpec(
            num_scalar_prefetch=1,
            grid=(2,),
            in_specs=[
                pl.BlockSpec((rows, width // 2), lambda n, scal: (0, (1 - scal[0]) ^ n)),
            ]
            + [whole((rows // 2, 384))] * (2 * pairs),
            out_specs=[held((width // 2, cols)), held((width // 2, cols)), held((8, cols))],
        ),
        out_shape=[
            jax.ShapeDtypeStruct((width // 2, cols), BF16),
            jax.ShapeDtypeStruct((width // 2, cols), BF16),
            jax.ShapeDtypeStruct((8, cols), F32),
        ],
        compiler_params=params(1),
        cost_estimate=cost(2 * rows * width * cols, 2 * rows * (width + cols)),
        name="project_grad",
    )(scal, first, *oth, *own)


def first_grad_kernel(pairs, *refs):
    own, got = refs[:pairs], refs[pairs : 2 * pairs]
    mine, theirs, tokens, out, sums = refs[2 * pairs :]
    total = nt(jnp.concatenate([x[...] for x in own], axis=1), mine[...])
    total = total + nt(jnp.concatenate([x[...] for x in got], axis=1), theirs[...])
    out[...] = total.astype(BF16)

    @pl.when(pl.program_id(0) == 0)
    def _():
        sums[...] = jnp.zeros_like(sums)

    xhat, _ = centre(tokens[...].astype(F32))
    sums[0:8, :] += fold8(total * xhat)
    sums[8:16, :] += fold8(total)


def first_grad(own, got, mine, theirs, packed):
    pairs = len(own)
    rows, cols = own[0].shape
    width = mine.shape[0]
    return pl.pallas_call(
        functools.partial(first_grad_kernel, pairs),
        grid=(rows // BLK,),
        in_specs=[pl.BlockSpec((BLK, cols), lambda i: (i, 0))] * (2 * pairs)
        + [whole(mine.shape), whole(theirs.shape), pl.BlockSpec((BLK, width), lambda i: (i, 0))],
        out_specs=[
            pl.BlockSpec((BLK, width), lambda i: (i, 0)),
            pl.BlockSpec((16, width), lambda i: (0, 0)),
        ],
        out_shape=[
            jax.ShapeDtypeStruct((rows, width), BF16),
            jax.ShapeDtypeStruct((16, width), F32),
        ],
        compiler_params=params(1),
        cost_estimate=cost(
            4 * pairs * rows * width * cols, 4 * pairs * rows * cols + 4 * width * cols * pairs
        ),
        name="first_grad",
    )(*own, *got, mine, theirs, packed)


def last_kernel(scal, tokens, grad, grad_got, residual, residual_got, gain, out):
    xhat, scale = centre(tokens[...].astype(F32))
    straight = scal[0] == scal[1]
    wide = jnp.where(straight, grad[...], grad_got[...]).astype(F32)
    base = jnp.where(straight, residual[...], residual_got[...])
    out[...] = base + norm_back(xhat, scale, gain[...], wide)


def last(scal, packed, grad, grad_got, residual, residual_got, gain, tokens_here):
    rows, width = grad.shape
    return pl.pallas_call(
        last_kernel,
        grid_spec=pltpu.PrefetchScalarGridSpec(
            num_scalar_prefetch=1,
            grid=(rows // BLK,),
            in_specs=[row_block(width)] * 5 + [whole((1, width))],
            out_specs=row_block(width),
        ),
        out_shape=jax.ShapeDtypeStruct((tokens_here, width), F32),
        compiler_params=params(1),
        cost_estimate=cost(20 * rows * width, 12 * rows * width),
        name="last",
    )(scal, packed, grad, grad_got, residual, residual_got, gain)


def table_kernel(
    frames_here, scal, ahead_sums, behind_sums, first_sums, learner, learner_offset, up, *refs
):
    offsets, out = refs[:-1], refs[-1]
    core, plane = scal[0], scal[1]
    width = out.shape[1]
    hid = up.shape[1] // 4

    def total(ref, at):
        return jnp.sum(ref[at : at + 8, :], axis=0, keepdims=True)

    out[...] = jnp.zeros_like(out)
    for row, (ref, at) in enumerate(
        (
            (first_sums, 0),
            (behind_sums, 0),
            (ahead_sums, 0),
            (first_sums, 8),
            (behind_sums, 8),
            (ahead_sums, 8),
            (behind_sums, 16),
            (ahead_sums, 16),
        )
    ):
        out[row : row + 1, :] = total(ref, at)
    out[8:16, :] = sum(learner[MAPS * i : MAPS * (i + 1), :] for i in range(frames_here))
    row = total(learner_offset, 0)
    lane = lax.broadcasted_iota(jnp.int32, (1, 128), 1)
    kept = row
    for i in range(1, frames_here):
        kept = kept + pltpu.roll(row, 128 - MAPS * i, 1)
    out[16:17, :128] = jnp.where(lane < MAPS, kept, 0.0)
    for chunk in range(4):
        side = (1 - plane) if chunk < 2 else plane
        pick = (1 - core) if chunk % 2 == 0 else core
        out[pl.ds(17 + 2 * side + pick, 1), :] = jnp.sum(
            up[:, chunk * hid : (chunk + 1) * hid], axis=0, keepdims=True
        )
    pair = 0
    for ref in offsets:
        for at in range(0, ref.shape[1], 384):
            to = pl.ds(pl.multiple_of(core * (width // 2) + pair * 128, 128), 128)
            out[21:22, to] = jnp.sum(ref[:, at : at + 128], axis=0, keepdims=True)
            out[22:23, to] = jnp.sum(ref[:, at + 256 : at + 384], axis=0, keepdims=True)
            pair += 1


def small_table(scal, frames_here, *parts):
    width = parts[0].shape[1]
    return pl.pallas_call(
        functools.partial(table_kernel, frames_here),
        grid_spec=pltpu.PrefetchScalarGridSpec(
            num_scalar_prefetch=1,
            grid=(1,),
            in_specs=[held(x.shape) for x in parts],
            out_specs=held((24, width)),
        ),
        out_shape=jax.ShapeDtypeStruct((24, width), F32),
        compiler_params=pltpu.CompilerParams(vmem_limit_bytes=16 * 1024 * 1024),
        cost_estimate=cost(0, 1 << 20),
        name="small_table",
    )(scal, *parts)


def body(
    tokens,
    frame_counts,
    norm_gains,
    norm_shifts,
    attend_weight,
    attend_offset,
    output_weight,
    output_offset,
    expand_weight,
    expand_offset,
    contract_weight,
    contract_offset,
    learner_weight,
    learner_offset,
    pooled_cotangent,
):
    tokens_here, width = tokens.shape
    frames_here = tokens_here // FRAME_TOK
    half_rows = -(-tokens_here // BLK) * BLK
    share = attend_weight.shape[2]
    hid = contract_weight.shape[0] // 2
    chips = lax.axis_size("chip")
    core, plane = lax.axis_index("core"), lax.axis_index("mp")
    straight = core == plane
    flip2 = [(0, 1), (1, 0)]

    def turn(x):
        return lax.ppermute(x, ("core", "mp"), [(1, 2), (2, 1)])

    def to_core(x):
        return lax.ppermute(x, "core", flip2)

    def to_plane(x):
        return lax.ppermute(x, "mp", flip2)

    chip = lax.axis_index("chip")
    side = chip % 2
    hops = []
    while (2 << len(hops)) < chips:
        hops.append(2 << len(hops))

    def hop(x, step):
        return lax.ppermute(x, "chip", [(i, i ^ step) for i in range(chips)])

    def low(x):
        return x.astype(BF16)

    def plus(a, b):
        return a.astype(F32) + b.astype(F32)

    def pick(x, index):
        return lax.dynamic_index_in_dim(x, index, 0, keepdims=False)

    def halves_of(x):
        rows = x.shape[-2] // 2
        return x.reshape(*x.shape[:-2], 2, rows, x.shape[-1])

    def join(x, other, index, axis):
        return jnp.concatenate(
            [jnp.where(index == 0, x, other), jnp.where(index == 0, other, x)], axis=axis
        )

    pairs = share // 128

    weight_mine = (
        attend_weight.reshape(width, 3, pairs, 128).transpose(0, 2, 1, 3).reshape(width, 3 * share)
    )
    weight_part = turn(lax.dynamic_slice_in_dim(weight_mine, side * (width // 2), width // 2, 0))
    packed = pack(tokens, pooled_cotangent.reshape(frames_here * MAPS, width), half_rows)
    got_packed = turn(after(packed, weight_mine))
    small = jnp.concatenate(
        [
            attend_offset,
            jnp.broadcast_to(frame_counts[0, 0].astype(F32), (2, 128)),
        ],
        axis=1,
    )
    small = jnp.where(straight, small, turn(small))
    expand_got = to_plane(expand_offset)
    weight_rest = lax.ppermute(
        weight_part,
        ("chip", "core", "mp"),
        [(4 * i + j, 4 * (i ^ 1) + j) for i in range(chips) for j in (1, 2)],
    )
    weight_here = jnp.where(straight, weight_mine, join(weight_part, weight_rest, side, 0))
    own = jnp.where(straight, packed, got_packed)
    oth = to_core(own)
    count = small[0, share].astype(jnp.int32)
    scal = jnp.stack([core.astype(jnp.int32), plane.astype(jnp.int32), count])
    offset = jnp.stack([small[0, :share], jnp.zeros((share,), F32), small[1, :share]])
    offset = offset.reshape(3, pairs, 128).transpose(1, 0, 2).reshape(1, 3 * share)

    quarter = jnp.concatenate(
        [
            lax.dynamic_slice_in_dim(contract_weight, core * hid, hid, 0),
            lax.dynamic_slice_in_dim(expand_weight, core * hid, hid, 1),
            lax.dynamic_slice_in_dim(output_weight, core * (share // 2), share // 2, 0),
        ],
        axis=0,
    )
    got_a = to_plane(after(quarter, own, weight_here, small, expand_got))
    up_offset = jnp.where(
        plane == 0,
        jnp.concatenate([expand_offset, expand_got]),
        jnp.concatenate([expand_got, expand_offset]),
    ).reshape(4, hid)

    first, qkv, qfeat, kfeat = project(
        scal,
        oth,
        own,
        norm_gains[0:1],
        norm_shifts[0:1],
        weight_here,
        offset,
        frames_here,
        half_rows,
    )
    mixed_send, wide_oth, logs_oth = attend(scal, qkv, qfeat, kfeat, frames_here, False)
    mixed_oth = to_core(mixed_send)
    weight_there = to_core(after(weight_here, mixed_send))
    mixed_own, wide_own, logs_own = attend(
        after(scal, mixed_send), qkv, qfeat, kfeat, frames_here, True
    )
    got_b = to_core(after(got_a, mixed_own))

    maps_all = frames_here * MAPS
    cot = jnp.pad(own[half_rows:], ((0, 128 - maps_all), (0, 0)))
    learner = jnp.pad(jnp.tile(learner_weight.T, (frames_here, 1)), ((0, 128 - maps_all), (0, 0)))
    learner_bias = jnp.pad(jnp.tile(learner_offset, frames_here), (0, 128 - maps_all))[None]
    weights = (output_weight, expand_weight, contract_weight, got_a, got_b)
    (
        out_grad,
        xhat_two,
        scale_two,
        hidden,
        slope,
        second,
        out_low,
        sums_ahead,
        pooled,
        learner_sums,
        learner_offset_sums,
    ) = ahead(
        scal,
        mixed_own,
        mixed_oth,
        own,
        cot,
        weights,
        up_offset,
        (
            norm_gains,
            norm_shifts,
            output_offset[None],
            contract_offset[None],
            learner,
            learner_bias,
        ),
        frames_here,
    )

    down_theirs = down_grad(hidden, out_low, 0)
    down_got = to_core(down_theirs)
    down_mine = down_grad(hidden, after(out_low, down_theirs), 1)
    down_send = low(plus(down_got[0], down_mine[0]))
    down_keep = plus(down_got[1], down_mine[1])
    down_plane = to_plane(down_send)

    (
        residual_grad,
        grad_own,
        grad_send,
        pre_grad,
        residual_low,
        sums_behind,
        up_sums,
    ) = behind(
        after(scal, down_send),
        out_grad,
        out_low,
        xhat_two,
        scale_two,
        slope,
        weights,
        norm_gains,
        pooled,
        maps_all,
    )
    grad_oth = to_core(grad_send)
    down_half = halves_of(plus(down_keep, after(down_plane, residual_low)))
    down_x_send = low(pick(down_half, 1 - side))
    down_x_keep = pick(down_half, side)
    down_x = hop(down_x_send, 1)
    up_theirs = up_grad(
        after(scal, down_x_send), second, pre_grad, mixed_own, mixed_oth, residual_low, 0
    )
    up_got = to_core(up_theirs)
    up_mine = up_grad(
        after(scal, up_theirs),
        second,
        pre_grad,
        mixed_own,
        mixed_oth,
        residual_low,
        1,
    )
    up_half = halves_of(plus(up_got, up_mine))
    up_x_send = low(lax.dynamic_index_in_dim(up_half, 1 - side, 1, keepdims=False))
    up_x_keep = lax.dynamic_index_in_dim(up_half, side, 1, keepdims=False)
    up_x = hop(up_x_send, 1)

    def back(pair, *gate):
        return attend_back(
            after(scal, *gate),
            qkv,
            qfeat,
            kfeat,
            grad_oth,
            grad_own,
            (wide_oth, wide_own),
            (logs_oth, logs_own),
            frames_here,
            pair,
        )

    def project_fold(their, mine):
        got = to_core(their)
        return jnp.where(straight, got, mine), jnp.where(straight, mine, got)

    bit = (chip // 2) % 2

    def split(x):
        parts = halves_of(x)
        return low(pick(parts, 1 - bit)), pick(parts, bit)

    residual_got = turn(after(residual_grad, up_mine))
    oth_0, own_0 = back(0, up_x_send)
    got_0 = to_core(oth_0)
    down_send, down_keep = split(plus(down_x_keep, after(down_x, oth_0)))
    down_z = hop(down_send, hops[0])
    up_y = plus(up_x_keep, after(up_x, oth_0))
    up_y_send = low(up_y[0])
    up_y_got = to_plane(up_y_send)

    residual_got = after(residual_got, oth_0)
    oth_1, own_1 = back(1, down_send, up_y_send, residual_got)
    got_1 = to_core(oth_1)
    down_sum = plus(down_keep, after(down_z, oth_1))
    down_low = low(down_sum)
    down_z = hop(down_low, hops[1])
    up_send, up_keep = split(plus(up_y[1], after(up_y_got, oth_1)))
    up_z = hop(up_send, hops[0])
    their_0, mine_0, offsets_0 = project_grad(
        after(scal, down_low, up_send), first, (oth_0, oth_1), (own_0, own_1)
    )
    early_send, early_keep = project_fold(their_0, mine_0)
    early_got = to_plane(early_send)
    up_sum = plus(up_keep, after(up_z, mine_0))
    up_low = low(up_sum)
    up_z = hop(up_low, hops[1])

    oth_2, own_2 = back(2, early_send, up_low)
    got_2 = to_core(oth_2)

    def rest(total, got, steps):
        total = plus(total, got)
        for step in steps:
            total = plus(total, hop(low(total), step))
        return low(total)

    down_sum = rest(down_sum, after(down_z, oth_2), hops[2:])
    down_z = hop(down_sum, hops[0])
    up_sum = rest(up_sum, after(up_z, oth_2), hops[2:])
    up_z = hop(up_sum, hops[0])
    early_half = halves_of(plus(early_keep, after(early_got, oth_2)))
    early_send = low(pick(early_half, 1 - side))
    early_keep = pick(early_half, side)
    early_x = hop(early_send, 1)
    their_2, mine_2, offsets_2 = project_grad(
        after(scal, down_sum, up_sum, early_send), first, (oth_2,), (own_2,)
    )
    late_send, late_keep = project_fold(their_2, mine_2)
    late_got = to_plane(late_send)
    down_sum = join(down_sum, after(down_z, mine_2), bit, 0)
    down_x = hop(down_sum, 1)
    up_sum = join(up_sum, after(up_z, mine_2), bit, 0)
    up_x = hop(up_sum, 1)
    early_sum = plus(early_keep, after(early_x, mine_2))
    early_low = low(early_sum)
    early_z = hop(early_low, hops[0])
    first_low, first_sums = first_grad(
        (own_0, own_1, own_2),
        (got_0, got_1, got_2),
        weight_here,
        weight_there,
        after(own, late_send, down_sum, up_sum, early_low),
    )
    first_got = turn(first_low)
    table = small_table(
        scal,
        frames_here,
        sums_ahead,
        sums_behind,
        first_sums,
        learner_sums,
        learner_offset_sums,
        up_sums,
        offsets_0,
        offsets_2,
    )
    table = table + to_core(table)
    table = table + to_plane(table)
    for step in [1, *hops]:
        table = table + hop(table, step)

    def around(x):
        return join(x, hop(x, 1), side, 0)

    late_half = halves_of(plus(late_keep, after(late_got, first_low)))
    late_x_send = low(pick(late_half, 1 - side))
    late_sum = around(rest(pick(late_half, side), hop(late_x_send, 1), hops))
    early_sum = around(rest(early_sum, after(early_z, first_low), hops[1:]))
    up_sum = join(up_sum, after(up_x, first_low), side, 0)
    down_sum = join(down_sum, after(down_x, first_low), side, 0)

    tokens_gradient = last(
        scal, packed, first_low, first_got, residual_grad, residual_got, norm_gains[0:1], tokens_here
    )

    def two(x):
        other = to_core(x)
        return jnp.where(core == 0, x, other), jnp.where(core == 0, other, x)

    def out_block(x):
        return jnp.concatenate([x[width:, : width // 2], x[width:, width // 2 :]], axis=0)

    down_first, down_second = two(down_sum)
    up_first, up_second = two(up_sum)
    contract_gradient = jnp.concatenate([down_first, down_second], axis=0).astype(F32)
    expand_gradient = jnp.concatenate([up_first[:width], up_second[:width]], axis=1).astype(F32)
    output_gradient = jnp.concatenate([out_block(up_first), out_block(up_second)], axis=1).astype(F32)

    attend_gradient = jnp.concatenate(
        [jnp.concatenate(two(early_sum), axis=0), jnp.concatenate(two(late_sum), axis=0)], axis=1
    )
    attend_gradient = (
        attend_gradient.reshape(width, pairs, 3, 128).transpose(0, 2, 1, 3).astype(F32)
    )
    return (
        jnp.where(straight, pooled[:maps_all], residual_got[half_rows - maps_all :]).reshape(
            frames_here, MAPS, width
        ),
        tokens_gradient,
        table[0:3],
        table[3:6],
        attend_gradient.reshape(width, 3, share),
        lax.dynamic_slice_in_dim(table[21:23], plane * share, share, 1),
        output_gradient,
        table[6],
        expand_gradient,
        lax.dynamic_slice_in_dim(table[17:21], 2 * plane, 2, 0).reshape(2 * hid),
        contract_gradient,
        table[7],
        table[8:16].T,
        table[16, :MAPS],
    )


def solution(mesh):
    groups, sides = mesh.devices.shape
    fine = Mesh(mesh.devices.reshape(groups // 2, 2, sides), ("chip", "core", "mp"))
    dp = ("chip", "core")
    every = ("chip", "core", "mp")
    return jax.shard_map(
        body,
        mesh=fine,
        in_specs=(
            P(every, None),
            P(dp, None),
            P(),
            P(),
            P(None, None, "mp"),
            P(None, "mp"),
            P("mp", None),
            P(),
            P(None, "mp"),
            P("mp"),
            P("mp", None),
            P(),
            P(),
            P(),
            P(every, None, None),
        ),
        out_specs=(
            P(every, None, None),
            P(every, None),
            P(),
            P(),
            P(None, None, "mp"),
            P(None, "mp"),
            P("mp", None),
            P(),
            P(None, "mp"),
            P("mp"),
            P("mp", None),
            P(),
            P(),
            P(),
        ),
        check_vma=False,
    )
```

```python
import functools

import jax
import jax.numpy as jnp
from jax import lax
from jax.experimental import pallas as pl
from jax.experimental.pallas import tpu as pltpu
from jax.sharding import Mesh, PartitionSpec as P

HEAD_DIM = 64
MAPS = 8
FRAME_TOK = 196
EPS = 1e-06
BLK = 256
COST = 20.0
FAR = 1e30
GELU_C = 0.7978845608028654
GELU_A = 0.044715

F32 = jnp.float32
BF16 = jnp.bfloat16


def nn(a, b):
    return lax.dot_general(a, b, (((1,), (0,)), ((), ())), preferred_element_type=F32)


def nt(a, b):
    return lax.dot_general(a, b, (((1,), (1,)), ((), ())), preferred_element_type=F32)


def tn(a, b):
    return lax.dot_general(a, b, (((0,), (0,)), ((), ())), preferred_element_type=F32)


def fold8(values):
    rows, width = values.shape
    return jnp.sum(values.reshape(rows // 8, 8, width), axis=0)


def centre(values):
    average = jnp.mean(values, axis=-1, keepdims=True)
    centred = values - average
    spread = jnp.mean(centred * centred, axis=-1, keepdims=True)
    scale = lax.rsqrt(spread + EPS)
    return centred * scale, scale


def norm_back(xhat, scale, gain, grad):
    scaled = grad * gain
    along = jnp.mean(scaled * xhat, axis=-1, keepdims=True)
    return scale * (scaled - jnp.mean(scaled, axis=-1, keepdims=True) - xhat * along)


def cost(flops, nbytes):
    return pl.CostEstimate(
        flops=int(flops * COST), bytes_accessed=int(nbytes * COST), transcendentals=0
    )


def params(n, mib=60):
    return pltpu.CompilerParams(
        dimension_semantics=("arbitrary",) * n, vmem_limit_bytes=mib * 1024 * 1024
    )


def whole(shape):
    return pl.BlockSpec(shape, lambda *_: (0,) * len(shape), pipeline_mode=pl.Buffered(1))


def after(value, *others):
    return lax.optimization_barrier((value, others))[0]


NOTE = 4


def pack_kernel(tokens, cot, offset, count, out):
    here = tokens.shape[0]
    rows = out.shape[0] - cot.shape[0]
    edge = here // 16 * 16
    width = out.shape[1]
    out[:here, :] = tokens[...]
    left = offset[...]
    lines = []
    for _ in range(3):
        line = left.astype(BF16)
        lines.append(line.astype(F32))
        left = left - lines[-1]
    lines.append(jnp.broadcast_to(count[...], (1, width)))
    tail = rows - here
    row = lax.broadcasted_iota(jnp.int32, (tail, width), 0)
    block = jnp.zeros((tail, width), F32)
    for i, line in enumerate(lines):
        block = jnp.where(row == NOTE + i, line, block)
    out[here:rows, :] = block.astype(BF16)
    out[rows:, :] = cot[...]


def pack(tokens, cot, offset, count, half_rows):
    rows, width = half_rows + cot.shape[0], tokens.shape[1]
    return pl.pallas_call(
        pack_kernel,
        in_specs=[pl.BlockSpec(x.shape) for x in (tokens, cot, offset, count)],
        out_specs=pl.BlockSpec((rows, width)),
        out_shape=jax.ShapeDtypeStruct((rows, width), BF16),
        compiler_params=pltpu.CompilerParams(vmem_limit_bytes=16 * 1024 * 1024),
        cost_estimate=cost(0, 4 * rows * width),
        name="pack",
    )(tokens, cot, offset, count)


def relay_kernel(scal, mine, first, second, out):
    straight = scal[0] == scal[1]
    rows = first.shape[0]
    swap = scal[2] == 1
    for half in range(2):
        here = slice(half * rows, (half + 1) * rows)
        one, two = (first, second) if half == 0 else (second, first)
        got = jnp.where(swap, two[...], one[...])
        kept = jnp.where(straight, mine[here, :], got)
        share = kept.shape[1] // 3
        for pair in range(share // 128):
            for item in range(3):
                to = pair * 384 + item * 128
                at = item * share + pair * 128
                out[here, to : to + 128] = kept[:, at : at + 128]


def relay(scal, mine, first, second):
    return pl.pallas_call(
        relay_kernel,
        grid_spec=pltpu.PrefetchScalarGridSpec(
            num_scalar_prefetch=1,
            grid=(1,),
            in_specs=[held(mine.shape), held(first.shape), held(first.shape)],
            out_specs=held(mine.shape),
        ),
        out_shape=jax.ShapeDtypeStruct(mine.shape, BF16),
        compiler_params=params(1, 24),
        cost_estimate=cost(0, 0),
        name="relay",
    )(scal, mine, first, second)


def project_kernel(
    frames_here, scal, oth, own, gain, shift, weight, first, qkv, qfeat, kfeat, offset
):
    step = pl.program_id(0)
    half_blocks = pl.num_programs(0) // 2
    half_rows = half_blocks * BLK
    within = lax.rem(step, half_blocks) * BLK
    rows = pl.ds(pl.multiple_of(within, BLK), BLK)

    @pl.when(step == 0)
    def _():
        start = frames_here * FRAME_TOK // 16 * 16
        at = frames_here * FRAME_TOK + NOTE - start
        block = own[start : start + 32, :].astype(F32)
        note = block[at : at + 1, :] + block[at + 1 : at + 2, :] + block[at + 2 : at + 3, :]
        share = weight.shape[1] // 3
        offset[...] = jnp.zeros_like(offset)
        for pair in range(share // 128):
            here = pair * 128
            offset[:, 3 * here : 3 * here + 128] = note[:, here : here + 128]
            offset[:, 3 * here + 256 : 3 * here + 384] = note[:, share + here : share + here + 128]

    values = jnp.where(step < half_blocks, oth[rows, :], own[rows, :]).astype(F32)
    xhat, _ = centre(values)
    low = (xhat * gain[...] + shift[...]).astype(BF16)
    first[...] = low
    out = (nn(low, weight[...]) + offset[...]).astype(BF16)
    for pair in range(out.shape[1] // 384):
        at = pair * 384
        qkv[:, at : at + 128] = out[:, at : at + 128] * jnp.asarray(HEAD_DIM**-0.5, BF16)
        qkv[:, at + 128 : at + 384] = out[:, at + 128 : at + 384]
    core, count = scal[0], scal[2]
    half = jnp.where(step < half_blocks, 1 - core, core)
    edge = clip_edge(count, frames_here, half_rows)
    token = within + lax.broadcasted_iota(jnp.int32, (BLK, 128), 0)
    lane = lax.broadcasted_iota(jnp.int32, (BLK, 128), 1)
    clip = jnp.where(half * half_rows + token >= edge, 1, 0)
    clip = jnp.where(token >= frames_here * FRAME_TOK, 2, clip)
    hit = lane == clip
    qfeat[...] = jnp.where(hit, 1.0, 0.0).astype(BF16)
    kfeat[...] = jnp.where(hit, 0.0, jnp.where(lane < 3, -FAR, 0.0)).astype(BF16)


def clip_edge(count, frames_here, half_rows):
    return jnp.where(
        count <= frames_here,
        count * FRAME_TOK,
        half_rows + (count - frames_here) * FRAME_TOK,
    )


def clip_span(block, edge, blocks):
    low = jnp.where(block * BLK >= edge, edge // BLK, 0)
    high = jnp.where(block * BLK + BLK - 1 < edge, (edge + BLK - 1) // BLK, blocks)
    return low, high


def project(scal, oth, own, gain, shift, weight, frames_here, half_rows):
    width, cols = weight.shape
    steps = 2 * half_rows // BLK
    rows = 2 * half_rows
    return pl.pallas_call(
        functools.partial(project_kernel, frames_here),
        grid_spec=pltpu.PrefetchScalarGridSpec(
            num_scalar_prefetch=1,
            grid=(steps,),
            in_specs=[
                whole(oth.shape),
                whole(own.shape),
                whole((1, width)),
                whole((1, width)),
                whole((width, cols)),
            ],
            out_specs=[
                pl.BlockSpec((BLK, width), lambda i, *_: (i, 0)),
                pl.BlockSpec((BLK, cols), lambda i, *_: (i, 0)),
                pl.BlockSpec((BLK, 128), lambda i, *_: (i, 0)),
                pl.BlockSpec((BLK, 128), lambda i, *_: (i, 0)),
            ],
            scratch_shapes=[pltpu.VMEM((1, cols), F32)],
        ),
        out_shape=[
            jax.ShapeDtypeStruct((rows, width), BF16),
            jax.ShapeDtypeStruct((rows, cols), BF16),
            jax.ShapeDtypeStruct((rows, 128), BF16),
            jax.ShapeDtypeStruct((rows, 128), BF16),
        ],
        compiler_params=params(1, 22),
        cost_estimate=cost(2 * rows * width * cols, 4 * rows * width + 2 * rows * cols),
        name="project",
    )(scal, oth, own, gain, shift, weight)


def attend_kernel(
    frames_here,
    bk,
    scal,
    q,
    qfeat,
    qkv,
    kfeat,
    mixed,
    wide,
    log_total,
    scores,
    tops,
    acc,
    keys_all,
    values_all,
):
    step = pl.program_id(0)
    half = pl.num_programs(0)
    blocks = 2 * half
    pairs = q.shape[1] // 384
    flip = half * (1 - scal[0])
    edge = clip_edge(scal[2], frames_here, half * BLK)
    low, high = clip_span((step + half * scal[3]) ^ flip, edge, blocks)
    per = bk // BLK
    low, high = low // per, (high + per - 1) // per
    kflip = flip // per
    lane = lax.broadcasted_iota(jnp.int32, (BLK, 128), 1)
    left = lane < HEAD_DIM
    none = jnp.zeros((BLK, 128), BF16)
    queries = []
    for pair in range(pairs):
        both = q[:, pair * 384 : pair * 384 + 128]
        queries.append(jnp.concatenate([jnp.where(left, both, none), qfeat[...]], axis=1))
        queries.append(jnp.concatenate([jnp.where(left, none, both), qfeat[...]], axis=1))
    @pl.when(step == 0)
    def _():
        def prepare(block, carry):
            rows = pl.ds(pl.multiple_of(block * BLK, BLK), BLK)
            for pair in range(pairs):
                at = pair * 384
                keys_all[pair, rows, :128] = qkv[rows, at + 128 : at + 256]
                keys_all[pair, rows, 128:] = kfeat[rows, :]
                both = qkv[rows, at + 256 : at + 384]
                values_all[2 * pair, rows, :128] = jnp.where(left, both, none)
                values_all[2 * pair, rows, 128:] = jnp.where(left, 1.0, 0.0).astype(BF16)
                values_all[2 * pair + 1, rows, :128] = jnp.where(left, none, both)
                values_all[2 * pair + 1, rows, 128:] = jnp.where(left, 0.0, 1.0).astype(BF16)
            return carry

        lax.fori_loop(0, blocks, prepare, 0)

    for head in range(2 * pairs):
        tops[head] = jnp.full((BLK, 128), -3e38, F32)

    def score(block, carry):
        rows = pl.ds(pl.multiple_of((block ^ kflip) * bk, bk), bk)
        for pair in range(pairs):
            keys = keys_all[pair, rows, :]
            for head in (2 * pair, 2 * pair + 1):
                values = nt(queries[head], keys)
                scores[head, block] = values
                top = tops[head]
                for part in range(bk // 128):
                    top = jnp.maximum(top, values[:, part * 128 : (part + 1) * 128])
                tops[head] = top
        return carry

    lax.fori_loop(low, high, score, 0)
    for head in range(2 * pairs):
        tops[head] = jnp.broadcast_to(jnp.max(tops[head], axis=1, keepdims=True), (BLK, 128))
    acc[...] = jnp.zeros_like(acc)
    def mix(block, carry):
        rows = pl.ds(pl.multiple_of((block ^ kflip) * bk, bk), bk)
        for pair in range(pairs):
            soft = []
            for head in (2 * pair, 2 * pair + 1):
                top = tops[head]
                for part in range(bk // 128):
                    piece = scores[head, block, :, part * 128 : (part + 1) * 128]
                    soft.append(jnp.exp(piece - top).astype(BF16))
            values = jnp.concatenate(
                [values_all[2 * pair, rows, :], values_all[2 * pair + 1, rows, :]], axis=0
            )
            acc[pair] += nn(jnp.concatenate(soft, axis=1), values)
        return carry

    lax.fori_loop(low, high, mix, 0)
    for pair in range(pairs):
        cols = slice(pair * 128, (pair + 1) * 128)
        totals = acc[pair, :, 128:]
        out = acc[pair, :, :128] / totals
        wide[:, cols] = out
        mixed[:, cols] = out.astype(BF16)
        logs = (jnp.where(left, tops[2 * pair], tops[2 * pair + 1]) + jnp.log(totals)).T
        log_total[pair, 0, 0:1] = logs[0:1]
        log_total[pair, 0, 1:2] = logs[HEAD_DIM : HEAD_DIM + 1]


def attend(scal, qkv, qfeat, kfeat, frames_here):
    rows, cols = qkv.shape
    width = cols // 3
    pairs = width // 128
    half = rows // BLK // 2
    bk = rows // 2
    return pl.pallas_call(
        functools.partial(attend_kernel, frames_here, bk),
        grid_spec=pltpu.PrefetchScalarGridSpec(
            num_scalar_prefetch=1,
            grid=(half,),
            in_specs=[
                pl.BlockSpec((BLK, cols), lambda i, scal: (i + half * scal[3], 0)),
                pl.BlockSpec((BLK, 128), lambda i, scal: (i + half * scal[3], 0)),
                whole((rows, cols)),
                whole((rows, 128)),
            ],
            out_specs=[
                pl.BlockSpec((BLK, width), lambda i, *_: (i, 0)),
                pl.BlockSpec((BLK, width), lambda i, *_: (i, 0)),
                pl.BlockSpec((pairs, 1, 8, BLK), lambda i, *_: (0, i, 0, 0)),
            ],
            scratch_shapes=[
                pltpu.VMEM((2 * pairs, rows // bk, BLK, bk), F32),
                pltpu.VMEM((2 * pairs, BLK, 128), F32),
                pltpu.VMEM((pairs, BLK, 256), F32),
                pltpu.VMEM((pairs, rows, 256), BF16),
                pltpu.VMEM((2 * pairs, rows, 256), BF16),
            ],
        ),
        out_shape=[
            jax.ShapeDtypeStruct((rows // 2, width), BF16),
            jax.ShapeDtypeStruct((rows // 2, width), F32),
            jax.ShapeDtypeStruct((pairs, half, 8, BLK), F32),
        ],
        compiler_params=params(1, 40),
        cost_estimate=cost(8 * rows * rows * width, 16 * rows * width),
        name="attend",
    )(scal, qkv, qfeat, qkv, kfeat)


def gather_out_weight(scal, own_out, got_a, got_b, out_weight, hid):
    core, plane = scal[0], scal[1]
    share = own_out.shape[0]
    quarter = share // 2
    out_weight[pl.ds(pl.multiple_of(plane * share, 64), share), :] = own_out[...]
    base = (1 - plane) * share
    out_weight[pl.ds(pl.multiple_of(base + core * quarter, 64), quarter), :] = got_a[
        2 * hid : 2 * hid + quarter, :
    ]
    out_weight[pl.ds(pl.multiple_of(base + (1 - core) * quarter, 64), quarter), :] = got_b[
        2 * hid : 2 * hid + quarter, :
    ]


def up_weight(core, own_up, got_a, got_b, chunk):
    hid = got_a.shape[1]
    if chunk < 2:
        return (got_b, got_a)[chunk][hid : 2 * hid, :]
    pick = (1 - core) if chunk == 2 else core
    return own_up[:, pl.ds(pl.multiple_of(pick * hid, 128), hid)]


def down_weight(core, own_down, got_a, got_b, chunk):
    hid = got_a.shape[1]
    if chunk < 2:
        return (got_b, got_a)[chunk][:hid, :]
    pick = (1 - core) if chunk == 2 else core
    return own_down[pl.ds(pl.multiple_of(pick * hid, 128), hid), :]


def ahead_kernel(
    frames_here,
    scal,
    mixed_own,
    mixed_oth,
    tokens,
    cot,
    own_out,
    own_up,
    own_down,
    got_a,
    got_b,
    up_offset,
    gains,
    shifts,
    out_offset,
    down_offset,
    learner,
    learner_offset,
    out_grad_out,
    xhat_out,
    scale_out,
    hidden_out,
    slope_out,
    second_out,
    out_low_out,
    sums,
    pooled,
    learner_sums,
    learner_offset_sums,
    out_weight,
):
    step = pl.program_id(0)
    core, plane = scal[0], scal[1]
    hid = got_a.shape[1]
    share = own_out.shape[0]

    @pl.when(step == 0)
    def _():
        gather_out_weight(scal, own_out, got_a, got_b, out_weight, hid)
        for ref in (sums, pooled, learner_sums, learner_offset_sums):
            ref[...] = jnp.zeros_like(ref)

    def up_bias(chunk):
        side = (1 - plane) if chunk < 2 else plane
        pick = (1 - core) if chunk % 2 == 0 else core
        return up_offset[pl.ds(2 * side + pick, 1), :]

    mine = pl.ds(pl.multiple_of(core * share, 64), share)
    theirs = pl.ds(pl.multiple_of((1 - core) * share, 64), share)
    attended = nn(mixed_own[...], out_weight[mine, :]) + nn(mixed_oth[...], out_weight[theirs, :])
    residual = tokens[...].astype(F32) + attended + out_offset[...]
    xhat_two, scale_two = centre(residual)
    xhat_out[...] = xhat_two
    scale_out[...] = jnp.broadcast_to(scale_two, scale_out.shape)
    second = (xhat_two * gains[1:2, :] + shifts[1:2, :]).astype(BF16)
    second_out[...] = second
    block_out = residual + down_offset[...]
    for chunk in range(4):
        cols = slice(chunk * hid, (chunk + 1) * hid)
        pre = nn(second, up_weight(core, own_up, got_a, got_b, chunk)) + up_bias(chunk)
        square = pre * pre
        gate = 0.5 + 0.5 * jnp.tanh(pre * (GELU_C + (GELU_A * GELU_C) * square))
        product = pre * gate
        hidden = product.astype(BF16)
        bend = (1.0 - gate) * (2.0 * GELU_C + (6.0 * GELU_A * GELU_C) * square)
        slope_out[:, cols] = (gate + product * bend).astype(BF16)
        hidden_out[:, cols] = hidden
        block_out = block_out + nn(hidden, down_weight(core, own_down, got_a, got_b, chunk))
    xhat_three, scale_three = centre(block_out)
    third = (xhat_three * gains[2:3, :] + shifts[2:3, :]).astype(BF16)
    logits = nt(third, learner[...]) + learner_offset[...]
    sig = 1.0 / (1.0 + jnp.exp(-logits))
    token = step * BLK + lax.broadcasted_iota(jnp.int32, (BLK, 128), 0)
    first_token = (lax.broadcasted_iota(jnp.int32, (BLK, 128), 1) >> 3) * FRAME_TOK
    inside = (token >= first_token) & (token < first_token + FRAME_TOK)
    inside = inside & (first_token < frames_here * FRAME_TOK)
    maps = jnp.where(inside, sig, 0.0).astype(BF16)
    feature = block_out.astype(BF16)
    pooled[...] += tn(maps, feature)
    maps_grad = nt(feature, cot[...])
    pool_grad = nn(maps, cot[...])
    logits_grad = jnp.where(inside, maps_grad * sig * (1.0 - sig), 0.0).astype(BF16)
    learner_sums[...] += tn(logits_grad, third)
    learner_offset_sums[...] += fold8(logits_grad.astype(F32))
    third_grad = nn(logits_grad, learner[...])
    sums[0:8, :] += fold8(third_grad * xhat_three)
    sums[8:16, :] += fold8(third_grad)
    out_grad = pool_grad + norm_back(xhat_three, scale_three, gains[2:3, :], third_grad)
    sums[16:24, :] += fold8(out_grad)
    out_grad_out[...] = out_grad
    out_low_out[...] = out_grad.astype(BF16)


def behind_kernel(
    pooled_rows,
    scal,
    out_grad,
    out_low,
    xhat_two,
    scale_two,
    slope,
    own_out,
    own_up,
    own_down,
    got_a,
    got_b,
    gains,
    pooled,
    residual_grad_out,
    grad_own,
    grad_oth,
    pre_grad_out,
    residual_low_out,
    sums,
    up_sums,
    out_weight,
):
    core = scal[0]
    hid = got_a.shape[1]
    share = own_out.shape[0]

    @pl.when(pl.program_id(0) == 0)
    def _():
        gather_out_weight(scal, own_out, got_a, got_b, out_weight, hid)
        for ref in (sums, up_sums):
            ref[...] = jnp.zeros_like(ref)

    mine = pl.ds(pl.multiple_of(core * share, 64), share)
    theirs = pl.ds(pl.multiple_of((1 - core) * share, 64), share)
    low = out_low[...]
    second_grad = None
    for chunk in range(4):
        cols = slice(chunk * hid, (chunk + 1) * hid)
        hidden_grad = nt(low, down_weight(core, own_down, got_a, got_b, chunk))
        pre_grad = (hidden_grad * slope[:, cols].astype(F32)).astype(BF16)
        pre_grad_out[:, cols] = pre_grad
        up_sums[:, cols] += fold8(pre_grad.astype(F32))
        term = nt(pre_grad, up_weight(core, own_up, got_a, got_b, chunk))
        second_grad = term if second_grad is None else second_grad + term
    xhat = xhat_two[...]
    sums[0:8, :] += fold8(second_grad * xhat)
    sums[8:16, :] += fold8(second_grad)
    residual_grad = out_grad[...] + norm_back(
        xhat, scale_two[:, :1], gains[1:2, :], second_grad
    )
    sums[16:24, :] += fold8(residual_grad)
    residual_grad_out[...] = residual_grad

    @pl.when(pl.program_id(0) == pl.num_programs(0) - 1)
    def _():
        residual_grad_out[BLK - pooled_rows :, :] = pooled[:pooled_rows, :]

    residual_low = residual_grad.astype(BF16)
    residual_low_out[...] = residual_low
    grad_own[...] = nt(residual_low, out_weight[mine, :]).astype(BF16)
    grad_oth[...] = nt(residual_low, out_weight[theirs, :]).astype(BF16)


def row_block(cols):
    return pl.BlockSpec((BLK, cols), lambda i, *_: (i, 0))


def held(shape):
    return pl.BlockSpec(shape, lambda *_: (0,) * len(shape))


def row_call(kernel, name, scal, rowed, wholes, row_outs, held_outs, scratch, flops, mib):
    rows = rowed[0].shape[0]
    nbytes = sum(x.size * x.dtype.itemsize for x in wholes)
    nbytes += rows * sum(c * (2 if t == BF16 else 4) for c, t in row_outs)
    return pl.pallas_call(
        kernel,
        grid_spec=pltpu.PrefetchScalarGridSpec(
            num_scalar_prefetch=1,
            grid=(rows // BLK,),
            in_specs=[row_block(x.shape[1]) for x in rowed] + [whole(x.shape) for x in wholes],
            out_specs=[row_block(cols) for cols, _ in row_outs] + [held(s) for s in held_outs],
            scratch_shapes=scratch,
        ),
        out_shape=[jax.ShapeDtypeStruct((rows, cols), t) for cols, t in row_outs]
        + [jax.ShapeDtypeStruct(s, F32) for s in held_outs],
        compiler_params=params(1, mib),
        cost_estimate=cost(flops, nbytes),
        name=name,
    )(scal, *rowed, *wholes)


def ahead(scal, mixed_own, mixed_oth, packed, cot, weights, up_offset, small, frames_here):
    rows, share = mixed_own.shape
    width = packed.shape[1]
    hidden = up_offset.size
    return row_call(
        functools.partial(ahead_kernel, frames_here),
        "ahead",
        scal,
        [mixed_own, mixed_oth, packed],
        [cot, *weights, up_offset, *small],
        [
            (width, F32),
            (width, F32),
            (128, F32),
            (hidden, BF16),
            (hidden, BF16),
            (width, BF16),
            (width, BF16),
        ],
        [(24, width), (128, width), (128, width), (8, 128)],
        [pltpu.VMEM((2 * share, width), BF16)],
        2 * rows * width * (2 * hidden + width),
        40,
    )


def behind(scal, out_grad, out_low, xhat_two, scale_two, slope, weights, gains, pooled, maps_all):
    rows, width = out_grad.shape
    share = weights[0].shape[0]
    hidden = slope.shape[1]
    return row_call(
        functools.partial(behind_kernel, maps_all),
        "behind",
        scal,
        [out_grad, out_low, xhat_two, scale_two, slope],
        [*weights, gains, pooled],
        [(width, F32), (share, BF16), (share, BF16), (hidden, BF16), (width, BF16)],
        [(24, width), (8, hidden)],
        [pltpu.VMEM((2 * share, width), BF16)],
        2 * rows * width * (2 * hidden + width),
        40,
    )


def down_grad_kernel(scal, hidden, out_low, out):
    out[0] = tn(hidden[...], out_low[...]).astype(BF16)


def down_grad(scal, hidden, out_low):
    rows, width = out_low.shape
    hid = hidden.shape[1] // 4
    return pl.pallas_call(
        down_grad_kernel,
        grid_spec=pltpu.PrefetchScalarGridSpec(
            num_scalar_prefetch=1,
            grid=(2,),
            in_specs=[
                pl.BlockSpec((rows, hid), lambda n, scal: (0, 2 * n + scal[3])),
                whole((rows, width)),
            ],
            out_specs=pl.BlockSpec((1, hid, width), lambda n, *_: (n, 0, 0)),
        ),
        out_shape=jax.ShapeDtypeStruct((2, hid, width), BF16),
        compiler_params=params(1, 14),
        cost_estimate=cost(4 * rows * hid * width, 8 * rows * hid),
        name="down_grad",
    )(scal, hidden, out_low)


def up_grad_kernel(scal, second, pre_grad, mixed_own, mixed_oth, residual_low, out):
    step = pl.program_id(0)
    core, plane = scal[0], scal[1]
    width, hid = second.shape[1], pre_grad.shape[1]
    share = mixed_own.shape[1]
    out[0, :width, :] = tn(second[...], pre_grad[...]).astype(BF16)
    side = jnp.where(step == 0, 1 - plane, plane)
    column = jnp.where(scal[3] == 1, core, 1 - core)
    lhs = jnp.where(side == core, mixed_own[...], mixed_oth[...])
    rhs = residual_low[:, pl.ds(pl.multiple_of(column * (width // 2), 128), width // 2)]
    grad = tn(lhs, rhs).astype(BF16)
    out[0, width:, : width // 2] = grad[: share // 2]
    out[0, width:, width // 2 :] = grad[share // 2 :]


def up_grad(scal, second, pre_grad, mixed_own, mixed_oth, residual_low):
    rows, width = second.shape
    hid = pre_grad.shape[1] // 4
    share = mixed_own.shape[1]
    return pl.pallas_call(
        up_grad_kernel,
        grid_spec=pltpu.PrefetchScalarGridSpec(
            num_scalar_prefetch=1,
            grid=(2,),
            in_specs=[
                whole((rows, width)),
                pl.BlockSpec((rows, hid), lambda n, scal: (0, 2 * n + scal[3])),
                whole((rows, share)),
                whole((rows, share)),
                whole((rows, width)),
            ],
            out_specs=pl.BlockSpec((1, width + share // 2, hid), lambda n, *_: (n, 0, 0)),
        ),
        out_shape=jax.ShapeDtypeStruct((2, width + share // 2, hid), BF16),
        compiler_params=params(1, 18),
        cost_estimate=cost(4 * rows * hid * width * 1.25, 10 * rows * hid),
        name="up_grad",
    )(scal, second, pre_grad, mixed_own, mixed_oth, residual_low)


def attend_back_kernel(
    frames_here,
    scal,
    k,
    v,
    kfeat,
    q,
    qfeat,
    grad_oth,
    grad_own,
    wide_oth,
    wide_own,
    log_oth,
    log_own,
    out_oth,
    out_own,
    queries,
    grads,
    inner,
    logs,
    dq,
    dkv,
):
    step = pl.program_id(0)
    half = grad_oth.shape[0] // BLK
    blocks = 2 * half
    flip = half * (1 - scal[0])
    edge = clip_edge(scal[2], frames_here, half * BLK)
    low, high = clip_span(step ^ flip, edge, blocks)
    bq = half * BLK
    low, high = low // half, (high + half - 1) // half
    qflip = 1 - scal[0]
    lane = lax.broadcasted_iota(jnp.int32, (BLK, 128), 1)
    left = lane < HEAD_DIM
    none = jnp.zeros((BLK, 128), BF16)

    @pl.when(step == 0)
    def _():
        dq[...] = jnp.zeros_like(dq)
        for side, (grad, wide, log_total) in enumerate(
            ((grad_oth, wide_oth, log_oth), (grad_own, wide_own, log_own))
        ):
            for block in range(bq // BLK):
                here = slice(block * BLK, (block + 1) * BLK)
                rows = slice(side * bq + block * BLK, side * bq + (block + 1) * BLK)
                grads[rows, :] = grad[here, :]
                queries[rows, :128] = q[rows, :]
                queries[rows, 128:] = qfeat[rows, :]
                product = (grad[here, :].astype(F32) * wide[here, :]).T
                inner[side, 0:1, here] = jnp.sum(product[:HEAD_DIM], axis=0, keepdims=True)
                inner[side, 1:2, here] = jnp.sum(product[HEAD_DIM:], axis=0, keepdims=True)
                logs[side, :, here] = log_total[0, block]

    ka = jnp.where(left, k[...], none)
    kb = jnp.where(left, none, k[...])
    key_a = jnp.concatenate([ka, kfeat[...]], axis=1)
    key_b = jnp.concatenate([kb, kfeat[...]], axis=1)
    keys = jnp.concatenate([ka, kb], axis=0)
    va = jnp.where(left, v[...], none)
    vb = jnp.where(left, none, v[...])
    dkv[...] = jnp.zeros_like(dkv)

    def pair(block, carry):
        local = block ^ qflip
        rows = pl.ds(pl.multiple_of(local * bq, bq), bq)
        query = queries[rows, :]
        grad = grads[rows, :]
        soft_a = jnp.exp(nt(key_a, query) - logs[local, 0:1])
        soft_b = jnp.exp(nt(key_b, query) - logs[local, 1:2])
        score_a = (soft_a * (nt(va, grad) - inner[local, 0:1])).astype(BF16)
        score_b = (soft_b * (nt(vb, grad) - inner[local, 1:2])).astype(BF16)
        dkv[0] += nn(soft_a.astype(BF16), grad)
        dkv[1] += nn(soft_b.astype(BF16), grad)
        dkv[2] += nn(score_a, query[:, :128])
        dkv[3] += nn(score_b, query[:, :128])
        dq[rows, :] += tn(jnp.concatenate([score_a, score_b], axis=0), keys)
        return carry

    lax.fori_loop(low, high, pair, 0)
    dk = jnp.where(left, dkv[2], dkv[3]).astype(BF16)
    dv = jnp.where(left, dkv[0], dkv[1]).astype(BF16)
    within = pl.ds(pl.multiple_of(lax.rem(step, half) * BLK, BLK), BLK)

    @pl.when(step < half)
    def _():
        out_oth[within, 128:256] = dk
        out_oth[within, 256:] = dv

    @pl.when(step >= half)
    def _():
        out_own[within, 128:256] = dk
        out_own[within, 256:] = dv

    @pl.when(step == blocks - 1)
    def _():
        half_rows = out_oth.shape[0]
        out_oth[:, :128] = (dq[:half_rows, :] * HEAD_DIM**-0.5).astype(BF16)
        out_own[:, :128] = (dq[half_rows:, :] * HEAD_DIM**-0.5).astype(BF16)

def attend_back(scal, qkv, qfeat, kfeat, grad_oth, grad_own, wide, logs, frames_here):
    rows = qkv.shape[0]
    blocks = rows // BLK
    one = pl.Buffered(1)
    half_rows = pl.BlockSpec((rows // 2, 128), lambda j, scal: (0, scal[3]), pipeline_mode=one)
    half_logs = pl.BlockSpec(
        (1, blocks // 2, 8, BLK), lambda j, scal: (scal[3], 0, 0, 0), pipeline_mode=one
    )
    return pl.pallas_call(
        functools.partial(attend_back_kernel, frames_here),
        grid_spec=pltpu.PrefetchScalarGridSpec(
            num_scalar_prefetch=1,
            grid=(blocks,),
            in_specs=[
                pl.BlockSpec((BLK, 128), lambda j, scal: (j, 3 * scal[3] + 1)),
                pl.BlockSpec((BLK, 128), lambda j, scal: (j, 3 * scal[3] + 2)),
                pl.BlockSpec((BLK, 128), lambda j, *_: (j, 0)),
                pl.BlockSpec((rows, 128), lambda j, scal: (0, 3 * scal[3]), pipeline_mode=one),
                whole((rows, 128)),
                half_rows,
                half_rows,
                half_rows,
                half_rows,
                half_logs,
                half_logs,
            ],
            out_specs=[pl.BlockSpec((rows // 2, 384), lambda j, *_: (0, 0))] * 2,
            scratch_shapes=[
                pltpu.VMEM((rows, 256), BF16),
                pltpu.VMEM((rows, 128), BF16),
                pltpu.VMEM((2, 8, rows // 2), F32),
                pltpu.VMEM((2, 8, rows // 2), F32),
                pltpu.VMEM((rows, 128), F32),
                pltpu.VMEM((4, BLK, 128), F32),
            ],
        ),
        out_shape=[jax.ShapeDtypeStruct((rows // 2, 384), BF16)] * 2,
        compiler_params=params(1, 20),
        cost_estimate=cost(40 * rows * rows * 128, 30 * rows * 128),
        name="attend_back",
    )(scal, qkv, qkv, kfeat, qkv, qfeat, grad_oth, grad_own, *wide, *logs)


def project_grad_kernel(pairs, scal, first, *refs):
    oth, own = refs[:pairs], refs[pairs : 2 * pairs]
    theirs, mine, offsets = refs[2 * pairs :]
    step = pl.program_id(0)
    half = oth[0].shape[0]
    one = jnp.concatenate([x[...] for x in oth], axis=1)
    two = jnp.concatenate([x[...] for x in own], axis=1)
    out = (tn(first[:half, :], one) + tn(first[half:, :], two)).astype(BF16)

    @pl.when(step == 0)
    def _():
        theirs[...] = out
        offsets[...] = fold8(one.astype(F32)) + fold8(two.astype(F32))

    @pl.when(step == 1)
    def _():
        mine[...] = out


def project_grad(scal, first, oth, own):
    pairs = len(oth)
    rows, width = first.shape
    cols = 384 * pairs
    return pl.pallas_call(
        functools.partial(project_grad_kernel, pairs),
        grid_spec=pltpu.PrefetchScalarGridSpec(
            num_scalar_prefetch=1,
            grid=(2,),
            in_specs=[
                pl.BlockSpec((rows, width // 2), lambda n, scal: (0, (1 - scal[0]) ^ n)),
            ]
            + [whole((rows // 2, 384))] * (2 * pairs),
            out_specs=[held((width // 2, cols)), held((width // 2, cols)), held((8, cols))],
        ),
        out_shape=[
            jax.ShapeDtypeStruct((width // 2, cols), BF16),
            jax.ShapeDtypeStruct((width // 2, cols), BF16),
            jax.ShapeDtypeStruct((8, cols), F32),
        ],
        compiler_params=params(1, 18),
        cost_estimate=cost(2 * rows * width * cols, 2 * rows * (width + cols)),
        name="project_grad",
    )(scal, first, *oth, *own)


def first_grad_kernel(pairs, *refs):
    own, got = refs[:pairs], refs[pairs : 2 * pairs]
    mine, theirs, tokens, out, sums = refs[2 * pairs :]
    total = nt(jnp.concatenate([x[...] for x in own], axis=1), mine[...])
    total = total + nt(jnp.concatenate([x[...] for x in got], axis=1), theirs[...])
    out[...] = total.astype(BF16)

    @pl.when(pl.program_id(0) == 0)
    def _():
        sums[...] = jnp.zeros_like(sums)

    xhat, _ = centre(tokens[...].astype(F32))
    sums[0:8, :] += fold8(total * xhat)
    sums[8:16, :] += fold8(total)


def first_grad(own, got, mine, theirs, packed):
    pairs = len(own)
    rows, cols = own[0].shape
    width = mine.shape[0]
    return pl.pallas_call(
        functools.partial(first_grad_kernel, pairs),
        grid=(rows // BLK,),
        in_specs=[pl.BlockSpec((BLK, cols), lambda i: (i, 0))] * (2 * pairs)
        + [whole(mine.shape), whole(theirs.shape), pl.BlockSpec((BLK, width), lambda i: (i, 0))],
        out_specs=[
            pl.BlockSpec((BLK, width), lambda i: (i, 0)),
            pl.BlockSpec((16, width), lambda i: (0, 0)),
        ],
        out_shape=[
            jax.ShapeDtypeStruct((rows, width), BF16),
            jax.ShapeDtypeStruct((16, width), F32),
        ],
        compiler_params=params(1, 18),
        cost_estimate=cost(
            4 * pairs * rows * width * cols, 4 * pairs * rows * cols + 4 * width * cols * pairs
        ),
        name="first_grad",
    )(*own, *got, mine, theirs, packed)


def last_kernel(scal, tokens, grad, grad_got, residual, residual_got, gain, out):
    xhat, scale = centre(tokens[...].astype(F32))
    straight = scal[0] == scal[1]
    wide = jnp.where(straight, grad[...], grad_got[...]).astype(F32)
    base = jnp.where(straight, residual[...], residual_got[...])
    out[...] = base + norm_back(xhat, scale, gain[...], wide)


def last(scal, packed, grad, grad_got, residual, residual_got, gain, tokens_here):
    rows, width = grad.shape
    return pl.pallas_call(
        last_kernel,
        grid_spec=pltpu.PrefetchScalarGridSpec(
            num_scalar_prefetch=1,
            grid=(rows // BLK,),
            in_specs=[row_block(width)] * 5 + [whole((1, width))],
            out_specs=row_block(width),
        ),
        out_shape=jax.ShapeDtypeStruct((tokens_here, width), F32),
        compiler_params=params(1, 20),
        cost_estimate=cost(20 * rows * width, 12 * rows * width),
        name="last",
    )(scal, packed, grad, grad_got, residual, residual_got, gain)


def table_kernel(
    frames_here, scal, ahead_sums, behind_sums, first_sums, learner, learner_offset, up, *refs
):
    offsets, out = refs[:-1], refs[-1]
    core, plane = scal[0], scal[1]
    width = out.shape[1]
    hid = up.shape[1] // 4

    def total(ref, at):
        return jnp.sum(ref[at : at + 8, :], axis=0, keepdims=True)

    out[...] = jnp.zeros_like(out)
    for row, (ref, at) in enumerate(
        (
            (first_sums, 0),
            (behind_sums, 0),
            (ahead_sums, 0),
            (first_sums, 8),
            (behind_sums, 8),
            (ahead_sums, 8),
            (behind_sums, 16),
            (ahead_sums, 16),
        )
    ):
        out[row : row + 1, :] = total(ref, at)
    out[8:16, :] = sum(learner[MAPS * i : MAPS * (i + 1), :] for i in range(frames_here))
    row = total(learner_offset, 0)
    lane = lax.broadcasted_iota(jnp.int32, (1, 128), 1)
    kept = row
    for i in range(1, frames_here):
        kept = kept + pltpu.roll(row, 128 - MAPS * i, 1)
    out[16:17, :128] = jnp.where(lane < MAPS, kept, 0.0)
    for chunk in range(4):
        side = (1 - plane) if chunk < 2 else plane
        pick = (1 - core) if chunk % 2 == 0 else core
        out[pl.ds(17 + 2 * side + pick, 1), :] = jnp.sum(
            up[:, chunk * hid : (chunk + 1) * hid], axis=0, keepdims=True
        )
    pair = 0
    for ref in offsets:
        for at in range(0, ref.shape[1], 384):
            to = pl.ds(pl.multiple_of(core * (width // 2) + pair * 128, 128), 128)
            out[21:22, to] = jnp.sum(ref[:, at : at + 128], axis=0, keepdims=True)
            out[22:23, to] = jnp.sum(ref[:, at + 256 : at + 384], axis=0, keepdims=True)
            pair += 1


def small_table(scal, frames_here, *parts):
    width = parts[0].shape[1]
    return pl.pallas_call(
        functools.partial(table_kernel, frames_here),
        grid_spec=pltpu.PrefetchScalarGridSpec(
            num_scalar_prefetch=1,
            grid=(1,),
            in_specs=[held(x.shape) for x in parts],
            out_specs=held((24, width)),
        ),
        out_shape=jax.ShapeDtypeStruct((24, width), F32),
        compiler_params=pltpu.CompilerParams(vmem_limit_bytes=16 * 1024 * 1024),
        cost_estimate=cost(0, 1 << 20),
        name="small_table",
    )(scal, *parts)


def body(
    tokens,
    frame_counts,
    norm_gains,
    norm_shifts,
    attend_weight,
    attend_offset,
    output_weight,
    output_offset,
    expand_weight,
    expand_offset,
    contract_weight,
    contract_offset,
    learner_weight,
    learner_offset,
    pooled_cotangent,
):
    tokens_here, width = tokens.shape
    frames_here = tokens_here // FRAME_TOK
    half_rows = -(-tokens_here // BLK) * BLK
    share = attend_weight.shape[2]
    hid = contract_weight.shape[0] // 2
    chips = lax.axis_size("chip")
    core, plane = lax.axis_index("core"), lax.axis_index("mp")
    straight = core == plane
    flip2 = [(0, 1), (1, 0)]

    def turn(x):
        return lax.ppermute(x, ("core", "mp"), [(1, 2), (2, 1)])

    def to_core(x):
        return lax.ppermute(x, "core", flip2)

    def to_plane(x):
        return lax.ppermute(x, "mp", flip2)

    chip = lax.axis_index("chip")
    side = chip % 2
    hops = []
    while (2 << len(hops)) < chips:
        hops.append(2 << len(hops))

    def hop(x, step):
        return lax.ppermute(x, "chip", [(i, i ^ step) for i in range(chips)])

    def low(x):
        return x.astype(BF16)

    def plus(a, b):
        return a.astype(F32) + b.astype(F32)

    def pick(x, index):
        return lax.dynamic_index_in_dim(x, index, 0, keepdims=False)

    def halves_of(x):
        rows = x.shape[-2] // 2
        return x.reshape(*x.shape[:-2], 2, rows, x.shape[-1])

    def join(x, other, index, axis):
        return jnp.concatenate(
            [jnp.where(index == 0, x, other), jnp.where(index == 0, other, x)], axis=axis
        )

    pairs = share // 128

    weight_mine = attend_weight.reshape(width, 3 * share)
    weight_part = lax.dynamic_slice_in_dim(weight_mine, side * (width // 2), width // 2, 0)
    weight_got = turn(weight_part)
    packed = pack(
        after(tokens, weight_part),
        pooled_cotangent.reshape(frames_here * MAPS, width),
        attend_offset.reshape(1, 2 * share),
        frame_counts[:, :1].astype(F32),
        half_rows,
    )
    got_packed = turn(packed)
    expand_got = to_plane(after(expand_offset, packed))
    weight_rest = lax.ppermute(
        weight_got,
        ("chip", "core", "mp"),
        [(4 * i + j, 4 * (i ^ 1) + j) for i in range(chips) for j in (1, 2)],
    )
    weight_here = relay(
        jnp.stack([core, plane, side]).astype(jnp.int32), weight_mine, weight_got, weight_rest
    )
    own = jnp.where(straight, packed, after(got_packed, weight_here))
    oth = to_core(own)
    count = own[tokens_here + NOTE + 3, 0].astype(jnp.int32)
    numbered = [
        jnp.stack([core.astype(jnp.int32), plane.astype(jnp.int32), count, jnp.int32(i)])
        for i in range(pairs)
    ]
    scal = numbered[0]

    quarter = jnp.concatenate(
        [
            lax.dynamic_slice_in_dim(contract_weight, core * hid, hid, 0),
            lax.dynamic_slice_in_dim(expand_weight, core * hid, hid, 1),
            lax.dynamic_slice_in_dim(output_weight, core * (share // 2), share // 2, 0),
        ],
        axis=0,
    )
    got_a = to_plane(after(quarter, own, weight_here))
    up_offset = jnp.where(
        plane == 0,
        jnp.concatenate([expand_offset, expand_got]),
        jnp.concatenate([expand_got, expand_offset]),
    ).reshape(4, hid)

    first, qkv, qfeat, kfeat = project(
        scal,
        oth,
        own,
        norm_gains[0:1],
        norm_shifts[0:1],
        weight_here,
        frames_here,
        half_rows,
    )
    mixed_send, wide_oth, logs_oth = attend(numbered[0], qkv, qfeat, kfeat, frames_here)
    mixed_oth = to_core(mixed_send)
    weight_there = to_core(after(weight_here, mixed_send))
    mixed_own, wide_own, logs_own = attend(
        after(numbered[1], mixed_send), qkv, qfeat, kfeat, frames_here
    )
    got_b = to_core(after(got_a, mixed_own))

    maps_all = frames_here * MAPS
    cot = jnp.pad(own[half_rows:], ((0, 128 - maps_all), (0, 0)))
    learner = jnp.pad(jnp.tile(learner_weight.T, (frames_here, 1)), ((0, 128 - maps_all), (0, 0)))
    learner_bias = jnp.pad(jnp.tile(learner_offset, frames_here), (0, 128 - maps_all))[None]
    weights = (output_weight, expand_weight, contract_weight, got_a, got_b)
    (
        out_grad,
        xhat_two,
        scale_two,
        hidden,
        slope,
        second,
        out_low,
        sums_ahead,
        pooled,
        learner_sums,
        learner_offset_sums,
    ) = ahead(
        after(scal, weight_there),
        mixed_own,
        mixed_oth,
        own,
        cot,
        weights,
        up_offset,
        (
            norm_gains,
            norm_shifts,
            output_offset[None],
            contract_offset[None],
            learner,
            learner_bias,
        ),
        frames_here,
    )

    down_theirs = down_grad(numbered[0], hidden, out_low)
    down_got = to_core(down_theirs)
    down_mine = down_grad(after(numbered[1], down_theirs), hidden, out_low)
    down_send = low(plus(down_got[0], down_mine[0]))
    down_keep = plus(down_got[1], down_mine[1])
    down_plane = to_plane(down_send)

    (
        residual_grad,
        grad_own,
        grad_send,
        pre_grad,
        residual_low,
        sums_behind,
        up_sums,
    ) = behind(
        after(scal, down_send),
        out_grad,
        out_low,
        xhat_two,
        scale_two,
        slope,
        weights,
        norm_gains,
        pooled,
        maps_all,
    )
    grad_oth = to_core(grad_send)
    down_half = halves_of(plus(down_keep, after(down_plane, residual_low)))
    down_x_send = low(pick(down_half, 1 - side))
    down_x_keep = pick(down_half, side)
    down_x = hop(down_x_send, 1)
    up_theirs = up_grad(
        after(numbered[0], down_x_send), second, pre_grad, mixed_own, mixed_oth, residual_low
    )
    up_got = to_core(up_theirs)
    up_mine = up_grad(
        after(numbered[1], up_theirs), second, pre_grad, mixed_own, mixed_oth, residual_low
    )
    up_half = halves_of(plus(up_got, up_mine))
    up_x_send = low(lax.dynamic_index_in_dim(up_half, 1 - side, 1, keepdims=False))
    up_x_keep = lax.dynamic_index_in_dim(up_half, side, 1, keepdims=False)
    up_x = hop(up_x_send, 1)

    def back(pair, *gate):
        return attend_back(
            after(numbered[pair], *gate),
            qkv,
            qfeat,
            kfeat,
            grad_oth,
            grad_own,
            (wide_oth, wide_own),
            (logs_oth, logs_own),
            frames_here,
        )

    def project_fold(their, mine):
        got = to_core(their)
        return jnp.where(straight, got, mine), jnp.where(straight, mine, got)

    bit = (chip // 2) % 2

    def split(x):
        parts = halves_of(x)
        return low(pick(parts, 1 - bit)), pick(parts, bit)

    residual_got = turn(after(residual_grad, up_mine))
    down_send, down_keep = split(plus(down_x_keep, after(down_x, up_x_send)))
    down_z = hop(down_send, hops[0])
    oth_0, own_0 = back(0, down_send)
    got_0 = to_core(oth_0)
    down_sum = plus(down_keep, after(down_z, oth_0))
    down_low = low(down_sum)
    down_z = hop(down_low, hops[1])
    up_y = plus(up_x_keep, after(up_x, oth_0))
    up_y_send = low(up_y[0])
    up_y_got = to_plane(up_y_send)

    residual_got = after(residual_got, oth_0)
    oth_1, own_1 = back(1, down_low, up_y_send, residual_got, got_0)
    got_1 = to_core(oth_1)

    def rest(total, got, steps):
        total = plus(total, got)
        for step in steps:
            total = plus(total, hop(low(total), step))
        return low(total)

    down_sum = rest(down_sum, after(down_z, oth_1), hops[2:])
    down_z = hop(down_sum, hops[0])
    up_send, up_keep = split(plus(up_y[1], after(up_y_got, oth_1)))
    up_z = hop(up_send, hops[0])
    their_0, mine_0, offsets_0 = project_grad(
        after(scal, down_sum, up_send), first, (oth_0, oth_1), (own_0, own_1)
    )
    early_send, early_keep = project_fold(their_0, mine_0)
    early_got = to_plane(early_send)
    up_sum = plus(up_keep, after(up_z, mine_0))
    up_low = low(up_sum)
    up_z = hop(up_low, hops[1])

    down_sum = join(down_sum, after(down_z, mine_0), bit, 0)
    down_x = hop(down_sum, 1)

    oth_2, own_2 = back(2, early_send, up_low, down_sum, got_1)
    got_2 = to_core(oth_2)
    up_sum = rest(up_sum, after(up_z, oth_2), hops[2:])
    up_z = hop(up_sum, hops[0])
    early_half = halves_of(plus(early_keep, after(early_got, oth_2)))
    early_send = low(pick(early_half, 1 - side))
    early_keep = pick(early_half, side)
    early_x = hop(early_send, 1)
    their_2, mine_2, offsets_2 = project_grad(
        after(scal, up_sum, early_send), first, (oth_2,), (own_2,)
    )
    late_send, late_keep = project_fold(their_2, mine_2)
    late_got = to_plane(late_send)
    up_sum = join(up_sum, after(up_z, mine_2), bit, 0)
    down_sum = join(down_sum, after(down_x, mine_2), side, 0)
    down_got = to_core(down_sum)
    early_sum = plus(early_keep, after(early_x, mine_2))
    early_low = low(early_sum)
    early_z = hop(early_low, hops[0])
    first_low, first_sums = first_grad(
        (own_0, own_1, own_2),
        (got_0, got_1, got_2),
        weight_here,
        weight_there,
        after(own, late_send, up_sum, early_low),
    )
    first_got = turn(first_low)
    table = small_table(
        scal,
        frames_here,
        sums_ahead,
        sums_behind,
        first_sums,
        learner_sums,
        learner_offset_sums,
        up_sums,
        offsets_0,
        offsets_2,
    )

    late_half = halves_of(plus(late_keep, after(late_got, table)))
    late_send = low(pick(late_half, 1 - side))
    late_keep = pick(late_half, side)
    late_x = hop(late_send, 1)
    early_sum = plus(early_sum, after(early_z, late_send))
    early_low = low(early_sum)
    early_z = hop(early_low, hops[1])
    up_x = hop(after(up_sum, early_low), 1)
    table = table + after(to_core(table), early_low)
    table_got = to_plane(table)
    late_sum = plus(late_keep, after(late_x, table))
    late_low = low(late_sum)
    late_z = hop(late_low, hops[0])
    table = table + after(table_got, late_low)
    table_got = hop(table, hops[0])
    late_sum = plus(late_sum, after(late_z, table))
    late_low = low(late_sum)
    late_z = hop(late_low, hops[1])
    table = table + after(table_got, late_low)
    table_got = hop(table, hops[1])
    up_sum = join(up_sum, after(up_x, table), side, 0)
    up_got = to_core(up_sum)
    early_sum = rest(early_sum, after(early_z, up_sum), hops[2:])
    early_x = hop(early_sum, 1)
    tokens_gradient = last(
        after(scal, early_sum),
        packed,
        first_low,
        first_got,
        residual_grad,
        residual_got,
        norm_gains[0:1],
        tokens_here,
    )
    late_sum = rest(late_sum, after(late_z, tokens_gradient), hops[2:])
    late_x = hop(late_sum, 1)
    table = table + after(table_got, late_sum)
    for step in [*hops[2:], 1]:
        table = table + hop(table, step)
    early_sum = join(early_sum, after(early_x, late_sum), side, 0)
    early_got = to_core(early_sum)
    late_sum = join(late_sum, after(late_x, early_sum), side, 0)
    late_got = to_core(late_sum)

    def two(x, other):
        return jnp.where(core == 0, x, other), jnp.where(core == 0, other, x)

    def out_block(x):
        return jnp.concatenate([x[width:, : width // 2], x[width:, width // 2 :]], axis=0)

    down_first, down_second = two(down_sum, down_got)
    up_first, up_second = two(up_sum, up_got)
    contract_gradient = jnp.concatenate([down_first, down_second], axis=0).astype(F32)
    expand_gradient = jnp.concatenate([up_first[:width], up_second[:width]], axis=1).astype(F32)
    output_gradient = jnp.concatenate([out_block(up_first), out_block(up_second)], axis=1).astype(F32)

    early_two, late_two = two(early_sum, early_got), two(late_sum, late_got)

    def column(pair, part):
        halves, at = (early_two, pair) if pair < pairs - 1 else (late_two, 0)
        at = at * 384 + part * 128
        return jnp.concatenate([x[:, at : at + 128] for x in halves], axis=0)

    attend_gradient = jnp.stack(
        [
            jnp.concatenate([column(pair, part) for pair in range(pairs)], axis=1)
            for part in range(3)
        ],
        axis=1,
    ).astype(F32)
    return (
        jnp.where(straight, pooled[:maps_all], residual_got[half_rows - maps_all :]).reshape(
            frames_here, MAPS, width
        ),
        tokens_gradient,
        table[0:3],
        table[3:6],
        attend_gradient,
        lax.dynamic_slice_in_dim(table[21:23], plane * share, share, 1),
        output_gradient,
        table[6],
        expand_gradient,
        lax.dynamic_slice_in_dim(table[17:21], 2 * plane, 2, 0).reshape(2 * hid),
        contract_gradient,
        table[7],
        table[8:16].T,
        table[16, :MAPS],
    )


def solution(mesh):
    groups, sides = mesh.devices.shape
    fine = Mesh(mesh.devices.reshape(groups // 2, 2, sides), ("chip", "core", "mp"))
    dp = ("chip", "core")
    every = ("chip", "core", "mp")
    return jax.shard_map(
        body,
        mesh=fine,
        in_specs=(
            P(every, None),
            P(dp, None),
            P(),
            P(),
            P(None, None, "mp"),
            P(None, "mp"),
            P("mp", None),
            P(),
            P(None, "mp"),
            P("mp"),
            P("mp", None),
            P(),
            P(),
            P(),
            P(every, None, None),
        ),
        out_specs=(
            P(every, None, None),
            P(every, None),
            P(),
            P(),
            P(None, None, "mp"),
            P(None, "mp"),
            P("mp", None),
            P(),
            P(None, "mp"),
            P("mp"),
            P("mp", None),
            P(),
            P(),
            P(),
        ),
        check_vma=False,
    )
```

```python
import functools

import jax
import jax.numpy as jnp
from jax import lax
from jax.experimental import pallas as pl
from jax.experimental.pallas import tpu as pltpu
from jax.sharding import Mesh, PartitionSpec as P

HEAD_DIM = 64
MAPS = 8
FRAME_TOK = 196
EPS = 1e-06
BLK = 256
COST = 20.0
FAR = 1e30
GELU_C = 0.7978845608028654
GELU_A = 0.044715

F32 = jnp.float32
BF16 = jnp.bfloat16


def nn(a, b):
    return lax.dot_general(a, b, (((1,), (0,)), ((), ())), preferred_element_type=F32)


def nt(a, b):
    return lax.dot_general(a, b, (((1,), (1,)), ((), ())), preferred_element_type=F32)


def tn(a, b):
    return lax.dot_general(a, b, (((0,), (0,)), ((), ())), preferred_element_type=F32)


def fold8(values):
    rows, width = values.shape
    return jnp.sum(values.reshape(rows // 8, 8, width), axis=0)


def centre(values):
    average = jnp.mean(values, axis=-1, keepdims=True)
    centred = values - average
    spread = jnp.mean(centred * centred, axis=-1, keepdims=True)
    scale = lax.rsqrt(spread + EPS)
    return centred * scale, scale


def norm_back(xhat, scale, gain, grad):
    scaled = grad * gain
    along = jnp.mean(scaled * xhat, axis=-1, keepdims=True)
    return scale * (scaled - jnp.mean(scaled, axis=-1, keepdims=True) - xhat * along)


def cost(flops, nbytes):
    return pl.CostEstimate(
        flops=int(flops * COST), bytes_accessed=int(nbytes * COST), transcendentals=0
    )


def params(n, mib=60):
    return pltpu.CompilerParams(
        dimension_semantics=("arbitrary",) * n, vmem_limit_bytes=mib * 1024 * 1024
    )


def whole(shape):
    return pl.BlockSpec(shape, lambda *_: (0,) * len(shape), pipeline_mode=pl.Buffered(1))


def after(value, *others):
    return lax.optimization_barrier((value, others))[0]


NOTE = 4


def pack_kernel(tokens, cot, offset, count, out):
    here = tokens.shape[0]
    rows = out.shape[0] - cot.shape[0]
    edge = here // 16 * 16
    width = out.shape[1]
    out[:here, :] = tokens[...]
    left = offset[...]
    lines = []
    for _ in range(3):
        line = left.astype(BF16)
        lines.append(line.astype(F32))
        left = left - lines[-1]
    lines.append(jnp.broadcast_to(count[...], (1, width)))
    tail = rows - here
    row = lax.broadcasted_iota(jnp.int32, (tail, width), 0)
    block = jnp.zeros((tail, width), F32)
    for i, line in enumerate(lines):
        block = jnp.where(row == NOTE + i, line, block)
    out[here:rows, :] = block.astype(BF16)
    out[rows:, :] = cot[...]


def pack(tokens, cot, offset, count, half_rows):
    rows, width = half_rows + cot.shape[0], tokens.shape[1]
    return pl.pallas_call(
        pack_kernel,
        in_specs=[pl.BlockSpec(x.shape) for x in (tokens, cot, offset, count)],
        out_specs=pl.BlockSpec((rows, width)),
        out_shape=jax.ShapeDtypeStruct((rows, width), BF16),
        compiler_params=pltpu.CompilerParams(vmem_limit_bytes=8 * 1024 * 1024),
        cost_estimate=cost(0, 4 * rows * width),
        name="pack",
    )(tokens, cot, offset, count)


def relay_kernel(scal, mine, first, second, out):
    straight = scal[0] == scal[1]
    rows = first.shape[0]
    swap = scal[2] == 1
    for half in range(2):
        here = slice(half * rows, (half + 1) * rows)
        one, two = (first, second) if half == 0 else (second, first)
        got = jnp.where(swap, two[...], one[...])
        kept = jnp.where(straight, mine[here, :], got)
        share = kept.shape[1] // 3
        for pair in range(share // 128):
            for item in range(3):
                to = pair * 384 + item * 128
                at = item * share + pair * 128
                out[here, to : to + 128] = kept[:, at : at + 128]


def relay(scal, mine, first, second):
    return pl.pallas_call(
        relay_kernel,
        grid_spec=pltpu.PrefetchScalarGridSpec(
            num_scalar_prefetch=1,
            grid=(1,),
            in_specs=[held(mine.shape), held(first.shape), held(first.shape)],
            out_specs=held(mine.shape),
        ),
        out_shape=jax.ShapeDtypeStruct(mine.shape, BF16),
        compiler_params=params(1, 10),
        cost_estimate=cost(0, 0),
        name="relay",
    )(scal, mine, first, second)


def project_kernel(
    frames_here, scal, oth, own, gain, shift, weight, first, qkv, qfeat, kfeat, offset
):
    step = pl.program_id(0)
    half_blocks = pl.num_programs(0) // 2
    half_rows = half_blocks * BLK
    within = lax.rem(step, half_blocks) * BLK
    rows = pl.ds(pl.multiple_of(within, BLK), BLK)

    @pl.when(step == 0)
    def _():
        start = frames_here * FRAME_TOK // 16 * 16
        at = frames_here * FRAME_TOK + NOTE - start
        block = own[start : start + 32, :].astype(F32)
        note = block[at : at + 1, :] + block[at + 1 : at + 2, :] + block[at + 2 : at + 3, :]
        share = weight.shape[1] // 3
        offset[...] = jnp.zeros_like(offset)
        for pair in range(share // 128):
            here = pair * 128
            offset[:, 3 * here : 3 * here + 128] = note[:, here : here + 128]
            offset[:, 3 * here + 256 : 3 * here + 384] = note[:, share + here : share + here + 128]

    values = jnp.where(step < half_blocks, oth[rows, :], own[rows, :]).astype(F32)
    xhat, _ = centre(values)
    low = (xhat * gain[...] + shift[...]).astype(BF16)
    first[...] = low
    out = (nn(low, weight[...]) + offset[...]).astype(BF16)
    for pair in range(out.shape[1] // 384):
        at = pair * 384
        qkv[:, at : at + 128] = out[:, at : at + 128] * jnp.asarray(HEAD_DIM**-0.5, BF16)
        qkv[:, at + 128 : at + 384] = out[:, at + 128 : at + 384]
    core, count = scal[0], scal[2]
    half = jnp.where(step < half_blocks, 1 - core, core)
    edge = clip_edge(count, frames_here, half_rows)
    token = within + lax.broadcasted_iota(jnp.int32, (BLK, 128), 0)
    lane = lax.broadcasted_iota(jnp.int32, (BLK, 128), 1)
    clip = jnp.where(half * half_rows + token >= edge, 1, 0)
    clip = jnp.where(token >= frames_here * FRAME_TOK, 2, clip)
    hit = lane == clip
    qfeat[...] = jnp.where(hit, 1.0, 0.0).astype(BF16)
    kfeat[...] = jnp.where(hit, 0.0, jnp.where(lane < 3, -FAR, 0.0)).astype(BF16)


def clip_edge(count, frames_here, half_rows):
    return jnp.where(
        count < frames_here,
        count * FRAME_TOK,
        half_rows + (count - frames_here) * FRAME_TOK,
    )


def clip_span(block, edge, blocks):
    low = jnp.where(block * BLK >= edge, edge // BLK, 0)
    high = jnp.where(block * BLK + BLK - 1 < edge, (edge + BLK - 1) // BLK, blocks)
    return low, high


def project(scal, oth, own, gain, shift, weight, frames_here, half_rows):
    width, cols = weight.shape
    steps = 2 * half_rows // BLK
    rows = 2 * half_rows
    return pl.pallas_call(
        functools.partial(project_kernel, frames_here),
        grid_spec=pltpu.PrefetchScalarGridSpec(
            num_scalar_prefetch=1,
            grid=(steps,),
            in_specs=[
                whole(oth.shape),
                whole(own.shape),
                whole((1, width)),
                whole((1, width)),
                whole((width, cols)),
            ],
            out_specs=[
                pl.BlockSpec((BLK, width), lambda i, *_: (i, 0)),
                pl.BlockSpec((BLK, cols), lambda i, *_: (i, 0)),
                pl.BlockSpec((BLK, 128), lambda i, *_: (i, 0)),
                pl.BlockSpec((BLK, 128), lambda i, *_: (i, 0)),
            ],
            scratch_shapes=[pltpu.VMEM((1, cols), F32)],
        ),
        out_shape=[
            jax.ShapeDtypeStruct((rows, width), BF16),
            jax.ShapeDtypeStruct((rows, cols), BF16),
            jax.ShapeDtypeStruct((rows, 128), BF16),
            jax.ShapeDtypeStruct((rows, 128), BF16),
        ],
        compiler_params=params(1, 10),
        cost_estimate=cost(2 * rows * width * cols, 4 * rows * width + 2 * rows * cols),
        name="project",
    )(scal, oth, own, gain, shift, weight)


def attend_kernel(
    frames_here,
    bk,
    scal,
    q,
    qfeat,
    qkv,
    kfeat,
    mixed,
    wide,
    log_total,
    scores,
    tops,
    acc,
    keys_all,
    values_all,
):
    step = pl.program_id(0)
    half = pl.num_programs(0)
    blocks = 2 * half
    pairs = q.shape[1] // 384
    flip = half * (1 - scal[0])
    edge = clip_edge(scal[2], frames_here, half * BLK)
    low, high = clip_span((step + half * scal[3]) ^ flip, edge, blocks)
    per = bk // BLK
    low, high = low // per, (high + per - 1) // per
    kflip = flip // per
    lane = lax.broadcasted_iota(jnp.int32, (BLK, 128), 1)
    left = lane < HEAD_DIM
    none = jnp.zeros((BLK, 128), BF16)
    queries = []
    for pair in range(pairs):
        both = q[:, pair * 384 : pair * 384 + 128]
        queries.append(jnp.concatenate([jnp.where(left, both, none), qfeat[...]], axis=1))
        queries.append(jnp.concatenate([jnp.where(left, none, both), qfeat[...]], axis=1))
    @pl.when(step == 0)
    def _():
        def prepare(block, carry):
            rows = pl.ds(pl.multiple_of(block * BLK, BLK), BLK)
            for pair in range(pairs):
                at = pair * 384
                keys_all[pair, rows, :128] = qkv[rows, at + 128 : at + 256]
                keys_all[pair, rows, 128:] = kfeat[rows, :]
                both = qkv[rows, at + 256 : at + 384]
                values_all[2 * pair, rows, :128] = jnp.where(left, both, none)
                values_all[2 * pair, rows, 128:] = jnp.where(left, 1.0, 0.0).astype(BF16)
                values_all[2 * pair + 1, rows, :128] = jnp.where(left, none, both)
                values_all[2 * pair + 1, rows, 128:] = jnp.where(left, 0.0, 1.0).astype(BF16)
            return carry

        lax.fori_loop(0, blocks, prepare, 0)

    for head in range(2 * pairs):
        tops[head] = jnp.full((BLK, 128), -3e38, F32)

    def score(block, carry):
        rows = pl.ds(pl.multiple_of((block ^ kflip) * bk, bk), bk)
        for pair in range(pairs):
            keys = keys_all[pair, rows, :]
            for head in (2 * pair, 2 * pair + 1):
                values = nt(queries[head], keys)
                scores[head, block] = values
                top = tops[head]
                for part in range(bk // 128):
                    top = jnp.maximum(top, values[:, part * 128 : (part + 1) * 128])
                tops[head] = top
        return carry

    lax.fori_loop(low, high, score, 0)
    for head in range(2 * pairs):
        tops[head] = jnp.broadcast_to(jnp.max(tops[head], axis=1, keepdims=True), (BLK, 128))
    acc[...] = jnp.zeros_like(acc)
    def mix(block, carry):
        rows = pl.ds(pl.multiple_of((block ^ kflip) * bk, bk), bk)
        for pair in range(pairs):
            soft = []
            for head in (2 * pair, 2 * pair + 1):
                top = tops[head]
                for part in range(bk // 128):
                    piece = scores[head, block, :, part * 128 : (part + 1) * 128]
                    soft.append(jnp.exp(piece - top).astype(BF16))
            values = jnp.concatenate(
                [values_all[2 * pair, rows, :], values_all[2 * pair + 1, rows, :]], axis=0
            )
            acc[pair] += nn(jnp.concatenate(soft, axis=1), values)
        return carry

    lax.fori_loop(low, high, mix, 0)
    for pair in range(pairs):
        cols = slice(pair * 128, (pair + 1) * 128)
        totals = acc[pair, :, 128:]
        out = acc[pair, :, :128] / totals
        wide[:, cols] = out
        mixed[:, cols] = out.astype(BF16)
        logs = (jnp.where(left, tops[2 * pair], tops[2 * pair + 1]) + jnp.log(totals)).T
        log_total[pair, 0, 0:1] = logs[0:1]
        log_total[pair, 0, 1:2] = logs[HEAD_DIM : HEAD_DIM + 1]


def attend(scal, qkv, qfeat, kfeat, frames_here):
    rows, cols = qkv.shape
    width = cols // 3
    pairs = width // 128
    half = rows // BLK // 2
    bk = rows // 2
    return pl.pallas_call(
        functools.partial(attend_kernel, frames_here, bk),
        grid_spec=pltpu.PrefetchScalarGridSpec(
            num_scalar_prefetch=1,
            grid=(half,),
            in_specs=[
                pl.BlockSpec((BLK, cols), lambda i, scal: (i + half * scal[3], 0)),
                pl.BlockSpec((BLK, 128), lambda i, scal: (i + half * scal[3], 0)),
                whole((rows, cols)),
                whole((rows, 128)),
            ],
            out_specs=[
                pl.BlockSpec((BLK, width), lambda i, *_: (i, 0)),
                pl.BlockSpec((BLK, width), lambda i, *_: (i, 0)),
                pl.BlockSpec((pairs, 1, 8, BLK), lambda i, *_: (0, i, 0, 0)),
            ],
            scratch_shapes=[
                pltpu.VMEM((2 * pairs, rows // bk, BLK, bk), F32),
                pltpu.VMEM((2 * pairs, BLK, 128), F32),
                pltpu.VMEM((pairs, BLK, 256), F32),
                pltpu.VMEM((pairs, rows, 256), BF16),
                pltpu.VMEM((2 * pairs, rows, 256), BF16),
            ],
        ),
        out_shape=[
            jax.ShapeDtypeStruct((rows // 2, width), BF16),
            jax.ShapeDtypeStruct((rows // 2, width), F32),
            jax.ShapeDtypeStruct((pairs, half, 8, BLK), F32),
        ],
        compiler_params=params(1, 28),
        cost_estimate=cost(8 * rows * rows * width, 16 * rows * width),
        name="attend",
    )(scal, qkv, qfeat, qkv, kfeat)


def gather_out_weight(scal, own_out, got_up, more_up, out_weight, hid):
    core, plane = scal[0], scal[1]
    share = own_out.shape[0]
    quarter = share // 2
    out_weight[pl.ds(pl.multiple_of(plane * share, 64), share), :] = own_out[...]
    base = (1 - plane) * share
    out_weight[pl.ds(pl.multiple_of(base + core * quarter, 64), quarter), :] = got_up[
        hid : hid + quarter, :
    ]
    out_weight[pl.ds(pl.multiple_of(base + (1 - core) * quarter, 64), quarter), :] = more_up[
        hid : hid + quarter, :
    ]


def up_weight(core, own_up, got_up, more_up, chunk):
    hid = got_up.shape[1]
    if chunk < 2:
        return (more_up, got_up)[chunk][:hid, :]
    pick = (1 - core) if chunk == 2 else core
    return own_up[:, pl.ds(pl.multiple_of(pick * hid, 128), hid)]


def down_weight(core, own_down, got_down, more_down, chunk):
    hid = got_down.shape[1]
    if chunk < 2:
        return (more_down, got_down)[chunk][...]
    pick = (1 - core) if chunk == 2 else core
    return own_down[pl.ds(pl.multiple_of(pick * hid, 128), hid), :]


def ahead_kernel(
    frames_here,
    scal,
    mixed_own,
    mixed_oth,
    tokens,
    cot,
    own_out,
    own_up,
    own_down,
    got_up,
    got_down,
    more_up,
    more_down,
    up_offset,
    gains,
    shifts,
    out_offset,
    down_offset,
    learner,
    learner_offset,
    out_grad_out,
    xhat_out,
    scale_out,
    slope_out,
    second_out,
    out_low_out,
    sums,
    pooled,
    learner_sums,
    learner_offset_sums,
    theirs_out,
    mine_out,
    out_weight,
    hidden_kept,
    down_total,
):
    step = pl.program_id(0)
    core, plane = scal[0], scal[1]
    hid = got_up.shape[1]
    share = own_out.shape[0]

    @pl.when(step == 0)
    def _():
        gather_out_weight(scal, own_out, got_up, more_up, out_weight, hid)
        for ref in (sums, pooled, learner_sums, learner_offset_sums, down_total):
            ref[...] = jnp.zeros_like(ref)

    def up_bias(chunk):
        pick = (1 - core) if chunk % 2 == 0 else core
        if chunk >= 2:
            return up_offset[pl.ds(pick, 1), :]
        note = got_up[hid + share // 2 :, :].astype(F32)
        sums = [
            note[3 * i : 3 * i + 1] + note[3 * i + 1 : 3 * i + 2] + note[3 * i + 2 : 3 * i + 3]
            for i in range(2)
        ]
        return jnp.where(pick == 0, sums[0], sums[1])

    mine = pl.ds(pl.multiple_of(core * share, 64), share)
    theirs = pl.ds(pl.multiple_of((1 - core) * share, 64), share)
    attended = nn(mixed_own[...], out_weight[mine, :]) + nn(mixed_oth[...], out_weight[theirs, :])
    residual = tokens[...].astype(F32) + attended + out_offset[...]
    xhat_two, scale_two = centre(residual)
    xhat_out[...] = xhat_two
    scale_out[...] = jnp.broadcast_to(scale_two, scale_out.shape)
    second = (xhat_two * gains[1:2, :] + shifts[1:2, :]).astype(BF16)
    second_out[...] = second
    block_out = residual + down_offset[...]
    for chunk in range(4):
        cols = slice(chunk * hid, (chunk + 1) * hid)
        pre = nn(second, up_weight(core, own_up, got_up, more_up, chunk)) + up_bias(chunk)
        square = pre * pre
        gate = 0.5 + 0.5 * jnp.tanh(pre * (GELU_C + (GELU_A * GELU_C) * square))
        product = pre * gate
        hidden = product.astype(BF16)
        bend = (1.0 - gate) * (2.0 * GELU_C + (6.0 * GELU_A * GELU_C) * square)
        slope_out[:, cols] = (gate + product * bend).astype(BF16)
        hidden_kept[:, cols] = hidden
        block_out = block_out + nn(hidden, down_weight(core, own_down, got_down, more_down, chunk))
    xhat_three, scale_three = centre(block_out)
    third = (xhat_three * gains[2:3, :] + shifts[2:3, :]).astype(BF16)
    logits = nt(third, learner[...]) + learner_offset[...]
    sig = 1.0 / (1.0 + jnp.exp(-logits))
    token = step * BLK + lax.broadcasted_iota(jnp.int32, (BLK, 128), 0)
    first_token = (lax.broadcasted_iota(jnp.int32, (BLK, 128), 1) >> 3) * FRAME_TOK
    inside = (token >= first_token) & (token < first_token + FRAME_TOK)
    inside = inside & (first_token < frames_here * FRAME_TOK)
    maps = jnp.where(inside, sig, 0.0).astype(BF16)
    feature = block_out.astype(BF16)
    pooled[...] += tn(maps, feature)
    maps_grad = nt(feature, cot[...])
    pool_grad = nn(maps, cot[...])
    logits_grad = jnp.where(inside, maps_grad * sig * (1.0 - sig), 0.0).astype(BF16)
    learner_sums[...] += tn(logits_grad, third)
    learner_offset_sums[...] += fold8(logits_grad.astype(F32))
    third_grad = nn(logits_grad, learner[...])
    sums[0:8, :] += fold8(third_grad * xhat_three)
    sums[8:16, :] += fold8(third_grad)
    out_grad = pool_grad + norm_back(xhat_three, scale_three, gains[2:3, :], third_grad)
    sums[16:24, :] += fold8(out_grad)
    out_grad_out[...] = out_grad
    out_low = out_grad.astype(BF16)
    out_low_out[...] = out_low
    for chunk in range(4):
        down_total[chunk] += tn(hidden_kept[:, chunk * hid : (chunk + 1) * hid], out_low)

    @pl.when(step == pl.num_programs(0) - 1)
    def _():
        for n in range(2):
            theirs_out[n] = down_total[2 * n].astype(BF16)
            mine_out[n] = down_total[2 * n + 1].astype(BF16)


def behind_kernel(
    pooled_rows,
    scal,
    out_grad,
    out_low,
    xhat_two,
    scale_two,
    slope,
    second,
    mixed_own,
    mixed_oth,
    own_out,
    own_up,
    own_down,
    got_up,
    got_down,
    more_up,
    more_down,
    gains,
    pooled,
    residual_grad_out,
    grad_own,
    grad_oth,
    sums,
    up_sums,
    theirs_out,
    mine_out,
    out_weight,
    up_total,
    out_total,
):
    core, plane = scal[0], scal[1]
    hid = got_up.shape[1]
    share = own_out.shape[0]

    @pl.when(pl.program_id(0) == 0)
    def _():
        gather_out_weight(scal, own_out, got_up, more_up, out_weight, hid)
        for ref in (sums, up_sums, up_total, out_total):
            ref[...] = jnp.zeros_like(ref)

    mine = pl.ds(pl.multiple_of(core * share, 64), share)
    theirs = pl.ds(pl.multiple_of((1 - core) * share, 64), share)
    low = out_low[...]
    second_turned = second[...].T
    second_grad = None
    for chunk in range(4):
        cols = slice(chunk * hid, (chunk + 1) * hid)
        hidden_grad = nt(low, down_weight(core, own_down, got_down, more_down, chunk))
        pre_grad = (hidden_grad * slope[:, cols].astype(F32)).astype(BF16)
        up_total[chunk] += nn(second_turned, pre_grad)
        up_sums[:, cols] += fold8(pre_grad.astype(F32))
        term = nt(pre_grad, up_weight(core, own_up, got_up, more_up, chunk))
        second_grad = term if second_grad is None else second_grad + term
    xhat = xhat_two[...]
    sums[0:8, :] += fold8(second_grad * xhat)
    sums[8:16, :] += fold8(second_grad)
    residual_grad = out_grad[...] + norm_back(
        xhat, scale_two[:, :1], gains[1:2, :], second_grad
    )
    sums[16:24, :] += fold8(residual_grad)
    residual_grad_out[...] = residual_grad

    @pl.when(pl.program_id(0) == pl.num_programs(0) - 1)
    def _():
        residual_grad_out[BLK - pooled_rows :, :] = pooled[:pooled_rows, :]

    residual_low = residual_grad.astype(BF16)
    grad_own[...] = nt(residual_low, out_weight[mine, :]).astype(BF16)
    grad_oth[...] = nt(residual_low, out_weight[theirs, :]).astype(BF16)
    out_total[0] += tn(mixed_own[...], residual_low)
    out_total[1] += tn(mixed_oth[...], residual_low)

    @pl.when(pl.program_id(0) == pl.num_programs(0) - 1)
    def _():
        width = second.shape[1]
        half = width // 2
        for odd, (out, column) in enumerate(((theirs_out, 1 - core), (mine_out, core))):
            for n in range(2):
                out[n, :width, :] = up_total[2 * n + odd].astype(BF16)
                side = (1 - plane) if n == 0 else plane
                at = pl.ds(pl.multiple_of(column * half, 128), half)
                grad = out_total[jnp.where(side == core, 0, 1), :, at].astype(BF16)
                out[n, width:, :half] = grad[: share // 2]
                out[n, width:, half:] = grad[share // 2 :]


def row_block(cols):
    return pl.BlockSpec((BLK, cols), lambda i, *_: (i, 0))


def held(shape):
    return pl.BlockSpec(shape, lambda *_: (0,) * len(shape))


def row_call(kernel, name, scal, rowed, wholes, row_outs, held_outs, scratch, flops, mib, low_outs=()):
    rows = rowed[0].shape[0]
    nbytes = sum(x.size * x.dtype.itemsize for x in wholes)
    nbytes += rows * sum(c * (2 if t == BF16 else 4) for c, t in row_outs)
    return pl.pallas_call(
        kernel,
        grid_spec=pltpu.PrefetchScalarGridSpec(
            num_scalar_prefetch=1,
            grid=(rows // BLK,),
            in_specs=[row_block(x.shape[1]) for x in rowed] + [whole(x.shape) for x in wholes],
            out_specs=[row_block(cols) for cols, _ in row_outs]
            + [held(s) for s in held_outs]
            + [whole(s) for s in low_outs],
            scratch_shapes=scratch,
        ),
        out_shape=[jax.ShapeDtypeStruct((rows, cols), t) for cols, t in row_outs]
        + [jax.ShapeDtypeStruct(s, F32) for s in held_outs]
        + [jax.ShapeDtypeStruct(s, BF16) for s in low_outs],
        compiler_params=params(1, mib),
        cost_estimate=cost(flops, nbytes),
        name=name,
    )(scal, *rowed, *wholes)


def ahead(scal, mixed_own, mixed_oth, packed, cot, weights, up_offset, small, frames_here):
    rows, share = mixed_own.shape
    width = packed.shape[1]
    hidden = 2 * up_offset.size
    return row_call(
        functools.partial(ahead_kernel, frames_here),
        "ahead",
        scal,
        [mixed_own, mixed_oth, packed],
        [cot, *weights, up_offset, *small],
        [
            (width, F32),
            (width, F32),
            (128, F32),
            (hidden, BF16),
            (width, BF16),
            (width, BF16),
        ],
        [(24, width), (128, width), (128, width), (8, 128)],
        [
            pltpu.VMEM((2 * share, width), BF16),
            pltpu.VMEM((BLK, hidden), BF16),
            pltpu.VMEM((4, hidden // 4, width), F32),
        ],
        2 * rows * width * (3 * hidden + width),
        42,
        [(2, hidden // 4, width)] * 2,
    )


def behind(scal, rowed, weights, gains, pooled, maps_all):
    rows, width = rowed[0].shape
    share = weights[0].shape[0]
    hidden = rowed[4].shape[1]
    hid = hidden // 4
    return row_call(
        functools.partial(behind_kernel, maps_all),
        "behind",
        scal,
        rowed,
        [*weights, gains, pooled],
        [(width, F32), (share, BF16), (share, BF16)],
        [(24, width), (8, hidden)],
        [
            pltpu.VMEM((2 * share, width), BF16),
            pltpu.VMEM((4, width, hid), F32),
            pltpu.VMEM((2, share, width), F32),
        ],
        2 * rows * width * (3 * hidden + 2 * width),
        44,
        [(2, width + share // 2, hid)] * 2,
    )


def attend_back_kernel(
    frames_here,
    scal,
    k,
    v,
    kfeat,
    q,
    qfeat,
    grad_oth,
    grad_own,
    wide_oth,
    wide_own,
    log_oth,
    log_own,
    out_oth,
    out_own,
    queries,
    grads,
    inner,
    logs,
    dq,
    dkv,
):
    step = pl.program_id(0)
    half = grad_oth.shape[0] // BLK
    blocks = 2 * half
    flip = half * (1 - scal[0])
    edge = clip_edge(scal[2], frames_here, half * BLK)
    low, high = clip_span(step ^ flip, edge, blocks)
    bq = half * BLK
    low, high = low // half, (high + half - 1) // half
    qflip = 1 - scal[0]
    lane = lax.broadcasted_iota(jnp.int32, (BLK, 128), 1)
    left = lane < HEAD_DIM
    none = jnp.zeros((BLK, 128), BF16)

    @pl.when(step == 0)
    def _():
        dq[...] = jnp.zeros_like(dq)
        for side, (grad, wide, log_total) in enumerate(
            ((grad_oth, wide_oth, log_oth), (grad_own, wide_own, log_own))
        ):
            for block in range(bq // BLK):
                here = slice(block * BLK, (block + 1) * BLK)
                rows = slice(side * bq + block * BLK, side * bq + (block + 1) * BLK)
                grads[rows, :] = grad[here, :]
                queries[rows, :128] = q[rows, :]
                queries[rows, 128:] = qfeat[rows, :]
                product = (grad[here, :].astype(F32) * wide[here, :]).T
                inner[side, 0:1, here] = jnp.sum(product[:HEAD_DIM], axis=0, keepdims=True)
                inner[side, 1:2, here] = jnp.sum(product[HEAD_DIM:], axis=0, keepdims=True)
                logs[side, :, here] = log_total[0, block]

    ka = jnp.where(left, k[...], none)
    kb = jnp.where(left, none, k[...])
    key_a = jnp.concatenate([ka, kfeat[...]], axis=1)
    key_b = jnp.concatenate([kb, kfeat[...]], axis=1)
    keys = jnp.concatenate([ka, kb], axis=0)
    va = jnp.where(left, v[...], none)
    vb = jnp.where(left, none, v[...])
    dkv[...] = jnp.zeros_like(dkv)

    def pair(block, carry):
        local = block ^ qflip
        rows = pl.ds(pl.multiple_of(local * bq, bq), bq)
        query = queries[rows, :]
        grad = grads[rows, :]
        soft_a = jnp.exp(nt(key_a, query) - logs[local, 0:1])
        soft_b = jnp.exp(nt(key_b, query) - logs[local, 1:2])
        score_a = (soft_a * (nt(va, grad) - inner[local, 0:1])).astype(BF16)
        score_b = (soft_b * (nt(vb, grad) - inner[local, 1:2])).astype(BF16)
        dkv[0] += nn(soft_a.astype(BF16), grad)
        dkv[1] += nn(soft_b.astype(BF16), grad)
        dkv[2] += nn(score_a, query[:, :128])
        dkv[3] += nn(score_b, query[:, :128])
        dq[rows, :] += tn(jnp.concatenate([score_a, score_b], axis=0), keys)
        return carry

    lax.fori_loop(low, high, pair, 0)
    dk = jnp.where(left, dkv[2], dkv[3]).astype(BF16)
    dv = jnp.where(left, dkv[0], dkv[1]).astype(BF16)
    within = pl.ds(pl.multiple_of(lax.rem(step, half) * BLK, BLK), BLK)

    @pl.when(step < half)
    def _():
        out_oth[within, 128:256] = dk
        out_oth[within, 256:] = dv

    @pl.when(step >= half)
    def _():
        out_own[within, 128:256] = dk
        out_own[within, 256:] = dv

    @pl.when(step == blocks - 1)
    def _():
        half_rows = out_oth.shape[0]
        out_oth[:, :128] = (dq[:half_rows, :] * HEAD_DIM**-0.5).astype(BF16)
        out_own[:, :128] = (dq[half_rows:, :] * HEAD_DIM**-0.5).astype(BF16)

def attend_back(scal, qkv, qfeat, kfeat, grad_oth, grad_own, wide, logs, frames_here):
    rows = qkv.shape[0]
    blocks = rows // BLK
    one = pl.Buffered(1)
    half_rows = pl.BlockSpec((rows // 2, 128), lambda j, scal: (0, scal[3]), pipeline_mode=one)
    half_logs = pl.BlockSpec(
        (1, blocks // 2, 8, BLK), lambda j, scal: (scal[3], 0, 0, 0), pipeline_mode=one
    )
    return pl.pallas_call(
        functools.partial(attend_back_kernel, frames_here),
        grid_spec=pltpu.PrefetchScalarGridSpec(
            num_scalar_prefetch=1,
            grid=(blocks,),
            in_specs=[
                pl.BlockSpec((BLK, 128), lambda j, scal: (j, 3 * scal[3] + 1)),
                pl.BlockSpec((BLK, 128), lambda j, scal: (j, 3 * scal[3] + 2)),
                pl.BlockSpec((BLK, 128), lambda j, *_: (j, 0)),
                pl.BlockSpec((rows, 128), lambda j, scal: (0, 3 * scal[3]), pipeline_mode=one),
                whole((rows, 128)),
                half_rows,
                half_rows,
                half_rows,
                half_rows,
                half_logs,
                half_logs,
            ],
            out_specs=[pl.BlockSpec((rows // 2, 384), lambda j, *_: (0, 0))] * 2,
            scratch_shapes=[
                pltpu.VMEM((rows, 256), BF16),
                pltpu.VMEM((rows, 128), BF16),
                pltpu.VMEM((2, 8, rows // 2), F32),
                pltpu.VMEM((2, 8, rows // 2), F32),
                pltpu.VMEM((rows, 128), F32),
                pltpu.VMEM((4, BLK, 128), F32),
            ],
        ),
        out_shape=[jax.ShapeDtypeStruct((rows // 2, 384), BF16)] * 2,
        compiler_params=params(1, 14),
        cost_estimate=cost(40 * rows * rows * 128, 30 * rows * 128),
        name="attend_back",
    )(scal, qkv, qkv, kfeat, qkv, qfeat, grad_oth, grad_own, *wide, *logs)


def project_grad_kernel(pairs, scal, first, *refs):
    oth, own = refs[:pairs], refs[pairs : 2 * pairs]
    theirs, mine, offsets = refs[2 * pairs :]
    step = pl.program_id(0)
    half = oth[0].shape[0]
    one = jnp.concatenate([x[...] for x in oth], axis=1)
    two = jnp.concatenate([x[...] for x in own], axis=1)
    out = (tn(first[:half, :], one) + tn(first[half:, :], two)).astype(BF16)

    @pl.when(step == 0)
    def _():
        theirs[...] = out
        offsets[...] = fold8(one.astype(F32)) + fold8(two.astype(F32))

    @pl.when(step == 1)
    def _():
        mine[...] = out


def project_grad(scal, first, oth, own):
    pairs = len(oth)
    rows, width = first.shape
    cols = 384 * pairs
    return pl.pallas_call(
        functools.partial(project_grad_kernel, pairs),
        grid_spec=pltpu.PrefetchScalarGridSpec(
            num_scalar_prefetch=1,
            grid=(2,),
            in_specs=[
                pl.BlockSpec((rows, width // 2), lambda n, scal: (0, (1 - scal[0]) ^ n)),
            ]
            + [whole((rows // 2, 384))] * (2 * pairs),
            out_specs=[held((width // 2, cols)), held((width // 2, cols)), held((8, cols))],
        ),
        out_shape=[
            jax.ShapeDtypeStruct((width // 2, cols), BF16),
            jax.ShapeDtypeStruct((width // 2, cols), BF16),
            jax.ShapeDtypeStruct((8, cols), F32),
        ],
        compiler_params=params(1, 12),
        cost_estimate=cost(2 * rows * width * cols, 2 * rows * (width + cols)),
        name="project_grad",
    )(scal, first, *oth, *own)


def first_grad_kernel(pairs, *refs):
    own, got = refs[:pairs], refs[pairs : 2 * pairs]
    mine, theirs, tokens, out, sums = refs[2 * pairs :]
    total = nt(jnp.concatenate([x[...] for x in own], axis=1), mine[...])
    total = total + nt(jnp.concatenate([x[...] for x in got], axis=1), theirs[...])
    out[...] = total.astype(BF16)

    @pl.when(pl.program_id(0) == 0)
    def _():
        sums[...] = jnp.zeros_like(sums)

    xhat, _ = centre(tokens[...].astype(F32))
    sums[0:8, :] += fold8(total * xhat)
    sums[8:16, :] += fold8(total)


def first_grad(own, got, mine, theirs, packed):
    pairs = len(own)
    rows, cols = own[0].shape
    width = mine.shape[0]
    return pl.pallas_call(
        functools.partial(first_grad_kernel, pairs),
        grid=(rows // BLK,),
        in_specs=[pl.BlockSpec((BLK, cols), lambda i: (i, 0))] * (2 * pairs)
        + [whole(mine.shape), whole(theirs.shape), pl.BlockSpec((BLK, width), lambda i: (i, 0))],
        out_specs=[
            pl.BlockSpec((BLK, width), lambda i: (i, 0)),
            pl.BlockSpec((16, width), lambda i: (0, 0)),
        ],
        out_shape=[
            jax.ShapeDtypeStruct((rows, width), BF16),
            jax.ShapeDtypeStruct((16, width), F32),
        ],
        compiler_params=params(1, 12),
        cost_estimate=cost(
            4 * pairs * rows * width * cols, 4 * pairs * rows * cols + 4 * width * cols * pairs
        ),
        name="first_grad",
    )(*own, *got, mine, theirs, packed)


def last_kernel(scal, tokens, grad, grad_got, residual, residual_got, gain, out):
    xhat, scale = centre(tokens[...].astype(F32))
    straight = scal[0] == scal[1]
    wide = jnp.where(straight, grad[...], grad_got[...]).astype(F32)
    base = jnp.where(straight, residual[...], residual_got[...])
    out[...] = base + norm_back(xhat, scale, gain[...], wide)


def last(scal, packed, grad, grad_got, residual, residual_got, gain, tokens_here):
    rows, width = grad.shape
    return pl.pallas_call(
        last_kernel,
        grid_spec=pltpu.PrefetchScalarGridSpec(
            num_scalar_prefetch=1,
            grid=(rows // BLK,),
            in_specs=[row_block(width)] * 5 + [whole((1, width))],
            out_specs=row_block(width),
        ),
        out_shape=jax.ShapeDtypeStruct((tokens_here, width), F32),
        compiler_params=params(1, 12),
        cost_estimate=cost(20 * rows * width, 12 * rows * width),
        name="last",
    )(scal, packed, grad, grad_got, residual, residual_got, gain)


def table_kernel(
    frames_here, scal, ahead_sums, behind_sums, first_sums, learner, learner_offset, up, *refs
):
    offsets, out = refs[:-1], refs[-1]
    core, plane = scal[0], scal[1]
    width = out.shape[1]
    hid = up.shape[1] // 4

    def total(ref, at):
        return jnp.sum(ref[at : at + 8, :], axis=0, keepdims=True)

    out[...] = jnp.zeros_like(out)
    for row, (ref, at) in enumerate(
        (
            (first_sums, 0),
            (behind_sums, 0),
            (ahead_sums, 0),
            (first_sums, 8),
            (behind_sums, 8),
            (ahead_sums, 8),
            (behind_sums, 16),
            (ahead_sums, 16),
        )
    ):
        out[row : row + 1, :] = total(ref, at)
    out[8:16, :] = sum(learner[MAPS * i : MAPS * (i + 1), :] for i in range(frames_here))
    row = total(learner_offset, 0)
    lane = lax.broadcasted_iota(jnp.int32, (1, 128), 1)
    kept = row
    for i in range(1, frames_here):
        kept = kept + pltpu.roll(row, 128 - MAPS * i, 1)
    out[16:17, :128] = jnp.where(lane < MAPS, kept, 0.0)
    for chunk in range(4):
        side = (1 - plane) if chunk < 2 else plane
        pick = (1 - core) if chunk % 2 == 0 else core
        out[pl.ds(17 + 2 * side + pick, 1), :] = jnp.sum(
            up[:, chunk * hid : (chunk + 1) * hid], axis=0, keepdims=True
        )
    pair = 0
    for ref in offsets:
        for at in range(0, ref.shape[1], 384):
            to = pl.ds(pl.multiple_of(core * (width // 2) + pair * 128, 128), 128)
            out[21:22, to] = jnp.sum(ref[:, at : at + 128], axis=0, keepdims=True)
            out[22:23, to] = jnp.sum(ref[:, at + 256 : at + 384], axis=0, keepdims=True)
            pair += 1


def small_table(scal, frames_here, *parts):
    width = parts[0].shape[1]
    return pl.pallas_call(
        functools.partial(table_kernel, frames_here),
        grid_spec=pltpu.PrefetchScalarGridSpec(
            num_scalar_prefetch=1,
            grid=(1,),
            in_specs=[held(x.shape) for x in parts],
            out_specs=held((24, width)),
        ),
        out_shape=jax.ShapeDtypeStruct((24, width), F32),
        compiler_params=pltpu.CompilerParams(vmem_limit_bytes=6 * 1024 * 1024),
        cost_estimate=cost(0, 1 << 20),
        name="small_table",
    )(scal, *parts)


def body(
    tokens,
    frame_counts,
    norm_gains,
    norm_shifts,
    attend_weight,
    attend_offset,
    output_weight,
    output_offset,
    expand_weight,
    expand_offset,
    contract_weight,
    contract_offset,
    learner_weight,
    learner_offset,
    pooled_cotangent,
):
    tokens_here, width = tokens.shape
    frames_here = tokens_here // FRAME_TOK
    half_rows = -(-tokens_here // BLK) * BLK
    share = attend_weight.shape[2]
    hid = contract_weight.shape[0] // 2
    chips = lax.axis_size("chip")
    core, plane = lax.axis_index("core"), lax.axis_index("mp")
    straight = core == plane
    flip2 = [(0, 1), (1, 0)]

    def turn(x):
        return lax.ppermute(x, ("core", "mp"), [(1, 2), (2, 1)])

    def to_core(x):
        return lax.ppermute(x, "core", flip2)

    def to_plane(x):
        return lax.ppermute(x, "mp", flip2)

    chip = lax.axis_index("chip")
    side = chip % 2
    hops = []
    while (2 << len(hops)) < chips:
        hops.append(2 << len(hops))

    def hop(x, step):
        return lax.ppermute(x, "chip", [(i, i ^ step) for i in range(chips)])

    def low(x):
        return x.astype(BF16)

    def plus(a, b):
        return a.astype(F32) + b.astype(F32)

    def pick(x, index):
        return lax.dynamic_index_in_dim(x, index, 0, keepdims=False)

    def halves_of(x):
        rows = x.shape[-2] // 2
        return x.reshape(*x.shape[:-2], 2, rows, x.shape[-1])

    def join(x, other, index, axis):
        return jnp.concatenate(
            [jnp.where(index == 0, x, other), jnp.where(index == 0, other, x)], axis=axis
        )

    pairs = share // 128

    weight_mine = attend_weight.reshape(width, 3 * share)
    weight_part = lax.dynamic_slice_in_dim(attend_weight, side * (width // 2), width // 2, 0)
    weight_part = weight_part.reshape(width // 2, 3 * share)
    weight_got = turn(weight_part)
    packed = pack(
        after(tokens, weight_part),
        pooled_cotangent.reshape(frames_here * MAPS, width),
        attend_offset.reshape(1, 2 * share),
        frame_counts[:, :1].astype(F32),
        half_rows,
    )
    got_packed = turn(packed)
    weight_rest = lax.ppermute(
        weight_got,
        ("chip", "core", "mp"),
        [(4 * i + j, 4 * (i ^ 1) + j) for i in range(chips) for j in (1, 2)],
    )
    weight_here = relay(
        jnp.stack([core, plane, side]).astype(jnp.int32), weight_mine, weight_got, weight_rest
    )
    left, notes = expand_offset.reshape(2, hid), []
    for _ in range(3):
        notes.append(lax.reduce_precision(left, 8, 7))
        left = left - notes[-1]
    notes = jnp.stack(notes, axis=1).reshape(6, hid)
    up_quarter = jnp.concatenate(
        [
            lax.dynamic_slice_in_dim(expand_weight, core * hid, hid, 1),
            lax.dynamic_slice_in_dim(output_weight, core * (share // 2), share // 2, 0),
            jnp.pad(notes, ((0, 10), (0, 0))).astype(BF16),
        ],
        axis=0,
    )
    down_quarter = lax.dynamic_slice_in_dim(contract_weight, core * hid, hid, 0)
    own = jnp.where(
        straight, packed, after(got_packed, weight_here, up_quarter, down_quarter)
    )
    oth = to_core(own)
    count = own[tokens_here + NOTE + 3, 0].astype(jnp.int32)
    numbered = [
        jnp.stack([core.astype(jnp.int32), plane.astype(jnp.int32), count, jnp.int32(i)])
        for i in range(pairs)
    ]
    scal = numbered[0]

    up_got_a = to_plane(after(up_quarter, own, weight_here))
    down_got_a = to_plane(after(down_quarter, oth))

    first, qkv, qfeat, kfeat = project(
        scal,
        oth,
        own,
        norm_gains[0:1],
        norm_shifts[0:1],
        weight_here,
        frames_here,
        half_rows,
    )
    weight_there = to_core(after(weight_here, qkv))
    mixed_send, wide_oth, logs_oth = attend(numbered[0], qkv, qfeat, kfeat, frames_here)
    mixed_oth = to_core(mixed_send)
    up_got_b = to_core(after(up_got_a, mixed_send))
    mixed_own, wide_own, logs_own = attend(
        after(numbered[1], mixed_send, weight_there), qkv, qfeat, kfeat, frames_here
    )
    down_got_b = to_core(after(down_got_a, mixed_own))

    maps_all = frames_here * MAPS
    cot = jnp.pad(own[half_rows:], ((0, 128 - maps_all), (0, 0)))
    learner = jnp.pad(jnp.tile(learner_weight.T, (frames_here, 1)), ((0, 128 - maps_all), (0, 0)))
    learner_bias = jnp.pad(jnp.tile(learner_offset, frames_here), (0, 128 - maps_all))[None]
    weights = (
        *(
            pltpu.with_memory_space_constraint(x, pltpu.HBM)
            for x in (output_weight, expand_weight, contract_weight)
        ),
        up_got_a,
        down_got_a,
        up_got_b,
        down_got_b,
    )
    (
        out_grad,
        xhat_two,
        scale_two,
        slope,
        second,
        out_low,
        sums_ahead,
        pooled,
        learner_sums,
        learner_offset_sums,
        down_theirs,
        down_mine,
    ) = ahead(
        scal,
        mixed_own,
        mixed_oth,
        own,
        cot,
        weights,
        expand_offset.reshape(2, hid),
        (
            norm_gains,
            norm_shifts,
            output_offset[None],
            contract_offset[None],
            learner,
            learner_bias,
        ),
        frames_here,
    )

    down_got = to_core(down_theirs)
    down_send = low(plus(down_got[0], down_mine[0]))
    down_keep = plus(down_got[1], down_mine[1])
    down_plane = to_plane(down_send)

    (
        residual_grad,
        grad_own,
        grad_send,
        sums_behind,
        up_sums,
        up_theirs,
        up_mine,
    ) = behind(
        after(scal, down_send),
        [out_grad, out_low, xhat_two, scale_two, slope, second, mixed_own, mixed_oth],
        weights,
        norm_gains,
        pooled,
        maps_all,
    )
    down_half = halves_of(plus(down_keep, after(down_plane, residual_grad)))
    down_x_send = low(pick(down_half, 1 - side))
    down_x_keep = pick(down_half, side)
    down_x = hop(down_x_send, 1)
    up_got = to_core(after(up_theirs, down_x_send))
    grad_oth = to_core(after(grad_send, down_x_send))
    up_half = halves_of(plus(up_got, after(up_mine, down_x_send)))
    up_x_send = low(lax.dynamic_index_in_dim(up_half, 1 - side, 1, keepdims=False))
    up_x_keep = lax.dynamic_index_in_dim(up_half, side, 1, keepdims=False)
    up_x = hop(up_x_send, 1)

    def back(pair, *gate):
        return attend_back(
            after(numbered[pair], *gate),
            qkv,
            qfeat,
            kfeat,
            grad_oth,
            grad_own,
            (wide_oth, wide_own),
            (logs_oth, logs_own),
            frames_here,
        )

    def project_fold(their, mine):
        got = to_core(their)
        return jnp.where(straight, got, mine), jnp.where(straight, mine, got)

    bit = (chip // 2) % 2

    def split(x):
        parts = halves_of(x)
        return low(pick(parts, 1 - bit)), pick(parts, bit)

    residual_got = turn(after(residual_grad, up_x_send))
    down_send, down_keep = split(plus(down_x_keep, after(down_x, up_x_send)))
    down_z = hop(down_send, hops[0])
    oth_0, own_0 = back(0, down_send)
    got_0 = to_core(oth_0)
    down_sum = plus(down_keep, after(down_z, oth_0))
    down_low = low(down_sum)
    down_z = hop(down_low, hops[1])
    up_y = plus(up_x_keep, after(up_x, oth_0))
    up_y_send = low(up_y[0])
    up_y_got = to_plane(up_y_send)

    residual_got = after(residual_got, oth_0)
    oth_1, own_1 = back(1, down_low, up_y_send, residual_got, got_0)
    got_1 = to_core(oth_1)

    def rest(total, got, steps):
        total = plus(total, got)
        for step in steps:
            total = plus(total, hop(low(total), step))
        return low(total)

    down_sum = rest(down_sum, after(down_z, oth_1), hops[2:])
    down_z = hop(down_sum, hops[0])
    up_send, up_keep = split(plus(up_y[1], after(up_y_got, oth_1)))
    up_z = hop(up_send, hops[0])
    their_0, mine_0, offsets_0 = project_grad(
        after(scal, down_sum, up_send), first, (oth_0, oth_1), (own_0, own_1)
    )
    early_send, early_keep = project_fold(their_0, mine_0)
    early_got = to_plane(early_send)
    up_sum = plus(up_keep, after(up_z, mine_0))
    up_low = low(up_sum)
    up_z = hop(up_low, hops[1])

    down_sum = join(down_sum, after(down_z, mine_0), bit, 0)
    down_x = hop(down_sum, 1)

    oth_2, own_2 = back(2, early_send, up_low, down_sum, got_1)
    got_2 = to_core(oth_2)
    up_sum = rest(up_sum, after(up_z, oth_2), hops[2:])
    up_z = hop(up_sum, hops[0])
    early_half = halves_of(plus(early_keep, after(early_got, oth_2)))
    early_send = low(pick(early_half, 1 - side))
    early_keep = pick(early_half, side)
    early_x = hop(early_send, 1)
    their_2, mine_2, offsets_2 = project_grad(
        after(scal, up_sum, early_send), first, (oth_2,), (own_2,)
    )
    late_send, late_keep = project_fold(their_2, mine_2)
    late_got = to_plane(late_send)
    up_sum = join(up_sum, after(up_z, mine_2), bit, 0)
    down_sum = join(down_sum, after(down_x, mine_2), side, 0)
    down_got = to_core(down_sum)
    early_sum = plus(early_keep, after(early_x, mine_2))
    early_low = low(early_sum)
    early_z = hop(early_low, hops[0])
    first_low, first_sums = first_grad(
        (own_0, own_1, own_2),
        (got_0, got_1, got_2),
        weight_here,
        weight_there,
        after(own, late_send, up_sum, early_low),
    )
    first_got = turn(first_low)
    table = small_table(
        scal,
        frames_here,
        sums_ahead,
        sums_behind,
        first_sums,
        learner_sums,
        learner_offset_sums,
        up_sums,
        offsets_0,
        offsets_2,
    )

    early_sum = plus(early_sum, after(early_z, table))
    early_low = low(early_sum)
    early_z = hop(early_low, hops[1])
    late_half = halves_of(plus(late_keep, after(late_got, early_low)))
    late_send = low(pick(late_half, 1 - side))
    late_keep = pick(late_half, side)
    late_x = hop(late_send, 1)
    table = table + after(to_core(table), late_send)
    table_got = to_plane(table)
    up_x = hop(after(up_sum, table), 1)
    late_sum = plus(late_keep, after(late_x, table))
    late_low = low(late_sum)
    late_z = hop(late_low, hops[0])
    table = table + after(table_got, late_low)
    late_sum = plus(late_sum, after(late_z, table))
    late_low = low(late_sum)
    late_z = hop(late_low, hops[1])
    table_got = hop(after(table, late_low), hops[0])
    early_sum = rest(early_sum, after(early_z, late_low), hops[2:])
    early_x = hop(early_sum, 1)
    table = table + after(table_got, early_sum)
    table_got = hop(table, hops[1])
    up_sum = join(up_sum, after(up_x, table), side, 0)
    up_got = to_core(up_sum)
    late_sum = rest(late_sum, after(late_z, up_sum), hops[2:])
    late_x = hop(late_sum, 1)
    table = table + after(table_got, late_sum)
    for step in hops[2:]:
        table = table + hop(table, step)
    table_got = hop(table, 1)
    tokens_gradient = last(
        after(scal, table),
        packed,
        first_low,
        first_got,
        residual_grad,
        residual_got,
        norm_gains[0:1],
        tokens_here,
    )
    table = table + after(table_got, tokens_gradient)
    early_sum = join(early_sum, after(early_x, tokens_gradient), side, 0)
    early_got = to_core(early_sum)
    late_sum = join(late_sum, after(late_x, early_sum), side, 0)
    late_got = to_core(late_sum)

    def two(x, other):
        return jnp.where(core == 0, x, other), jnp.where(core == 0, other, x)

    def out_block(x):
        return jnp.concatenate([x[width:, : width // 2], x[width:, width // 2 :]], axis=0)

    down_first, down_second = two(down_sum, down_got)
    up_first, up_second = two(up_sum, up_got)
    contract_gradient = jnp.concatenate([down_first, down_second], axis=0).astype(F32)
    expand_gradient = jnp.concatenate([up_first[:width], up_second[:width]], axis=1).astype(F32)
    output_gradient = jnp.concatenate([out_block(up_first), out_block(up_second)], axis=1).astype(F32)

    early_two, late_two = two(early_sum, early_got), two(late_sum, late_got)

    def column(pair, part):
        halves, at = (early_two, pair) if pair < pairs - 1 else (late_two, 0)
        at = at * 384 + part * 128
        return jnp.concatenate([x[:, at : at + 128] for x in halves], axis=0)

    attend_gradient = jnp.stack(
        [
            jnp.concatenate([column(pair, part) for pair in range(pairs)], axis=1)
            for part in range(3)
        ],
        axis=1,
    ).astype(F32)
    return (
        jnp.where(straight, pooled[:maps_all], residual_got[half_rows - maps_all :]).reshape(
            frames_here, MAPS, width
        ),
        tokens_gradient,
        table[0:3],
        table[3:6],
        attend_gradient,
        lax.dynamic_slice_in_dim(table[21:23], plane * share, share, 1),
        output_gradient,
        table[6],
        expand_gradient,
        lax.dynamic_slice_in_dim(table[17:21], 2 * plane, 2, 0).reshape(2 * hid),
        contract_gradient,
        table[7],
        table[8:16].T,
        table[16, :MAPS],
    )


def solution(mesh):
    groups, sides = mesh.devices.shape
    fine = Mesh(mesh.devices.reshape(groups // 2, 2, sides), ("chip", "core", "mp"))
    dp = ("chip", "core")
    every = ("chip", "core", "mp")
    return jax.shard_map(
        body,
        mesh=fine,
        in_specs=(
            P(every, None),
            P(dp, None),
            P(),
            P(),
            P(None, None, "mp"),
            P(None, "mp"),
            P("mp", None),
            P(),
            P(None, "mp"),
            P("mp"),
            P("mp", None),
            P(),
            P(),
            P(),
            P(every, None, None),
        ),
        out_specs=(
            P(every, None, None),
            P(every, None),
            P(),
            P(),
            P(None, None, "mp"),
            P(None, "mp"),
            P("mp", None),
            P(),
            P(None, "mp"),
            P("mp"),
            P("mp", None),
            P(),
            P(),
            P(),
        ),
        check_vma=False,
    )
```

```python
import functools

import jax
import jax.numpy as jnp
from jax import lax
from jax.experimental import pallas as pl
from jax.experimental.pallas import tpu as pltpu
from jax.sharding import Mesh, PartitionSpec as P

HEAD_DIM = 64
MAPS = 8
FRAME_TOK = 196
EPS = 1e-06
BLK = 256
COST = 20.0
FAR = 1e30
GELU_C = 0.7978845608028654
GELU_A = 0.044715

F32 = jnp.float32
BF16 = jnp.bfloat16


def nn(a, b):
    return lax.dot_general(a, b, (((1,), (0,)), ((), ())), preferred_element_type=F32)


def nt(a, b):
    return lax.dot_general(a, b, (((1,), (1,)), ((), ())), preferred_element_type=F32)


def tn(a, b):
    return lax.dot_general(a, b, (((0,), (0,)), ((), ())), preferred_element_type=F32)


def fold8(values):
    rows, width = values.shape
    return jnp.sum(values.reshape(rows // 8, 8, width), axis=0)


def centre(values):
    average = jnp.mean(values, axis=-1, keepdims=True)
    centred = values - average
    spread = jnp.mean(centred * centred, axis=-1, keepdims=True)
    scale = lax.rsqrt(spread + EPS)
    return centred * scale, scale


def norm_back(xhat, scale, gain, grad):
    scaled = grad * gain
    along = jnp.mean(scaled * xhat, axis=-1, keepdims=True)
    return scale * (scaled - jnp.mean(scaled, axis=-1, keepdims=True) - xhat * along)


STRIP = 96


def clear(ref):
    def strip(index, carry):
        rows = pl.ds(pl.multiple_of(index * STRIP, 32), STRIP)
        for part in range(ref.shape[0]):
            ref[part, rows, :] = jnp.zeros((STRIP, ref.shape[2]), ref.dtype)
        return carry

    lax.fori_loop(0, ref.shape[1] // STRIP, strip, 0)


def cost(flops, nbytes):
    return pl.CostEstimate(
        flops=int(flops * COST), bytes_accessed=int(nbytes * COST), transcendentals=0
    )


def params(n, mib=60):
    return pltpu.CompilerParams(
        dimension_semantics=("arbitrary",) * n, vmem_limit_bytes=mib * 1024 * 1024
    )


def whole(shape):
    return pl.BlockSpec(shape, lambda *_: (0,) * len(shape), pipeline_mode=pl.Buffered(1))


def after(value, *others):
    return lax.optimization_barrier((value, others))[0]


NOTE = 4


def pack_kernel(tokens, cot, offset, count, out):
    here = tokens.shape[0]
    rows = out.shape[0] - cot.shape[0]
    edge = here // 16 * 16
    width = out.shape[1]
    out[:here, :] = tokens[...]
    left = offset[...]
    lines = []
    for _ in range(3):
        line = left.astype(BF16)
        lines.append(line.astype(F32))
        left = left - lines[-1]
    lines.append(jnp.broadcast_to(count[...], (1, width)))
    tail = rows - here
    row = lax.broadcasted_iota(jnp.int32, (tail, width), 0)
    block = jnp.zeros((tail, width), F32)
    for i, line in enumerate(lines):
        block = jnp.where(row == NOTE + i, line, block)
    out[here:rows, :] = block.astype(BF16)
    out[rows:, :] = cot[...]


def pack(tokens, cot, offset, count, half_rows):
    rows, width = half_rows + cot.shape[0], tokens.shape[1]
    return pl.pallas_call(
        pack_kernel,
        in_specs=[pl.BlockSpec(x.shape) for x in (tokens, cot, offset, count)],
        out_specs=pl.BlockSpec((rows, width)),
        out_shape=jax.ShapeDtypeStruct((rows, width), BF16),
        compiler_params=pltpu.CompilerParams(vmem_limit_bytes=8 * 1024 * 1024),
        cost_estimate=cost(0, 4 * rows * width),
        name="pack",
    )(tokens, cot, offset, count)


def relay_kernel(scal, mine, first, second, out):
    straight = scal[0] == scal[1]
    rows = first.shape[0]
    swap = scal[2] == 1
    for half in range(2):
        here = slice(half * rows, (half + 1) * rows)
        one, two = (first, second) if half == 0 else (second, first)
        got = jnp.where(swap, two[...], one[...])
        kept = jnp.where(straight, mine[here, :], got)
        share = kept.shape[1] // 3
        for pair in range(share // 128):
            for item in range(3):
                to = pair * 384 + item * 128
                at = item * share + pair * 128
                out[here, to : to + 128] = kept[:, at : at + 128]


def relay(scal, mine, first, second):
    return pl.pallas_call(
        relay_kernel,
        grid_spec=pltpu.PrefetchScalarGridSpec(
            num_scalar_prefetch=1,
            grid=(1,),
            in_specs=[held(mine.shape), held(first.shape), held(first.shape)],
            out_specs=held(mine.shape),
        ),
        out_shape=jax.ShapeDtypeStruct(mine.shape, BF16),
        compiler_params=params(1, 10),
        cost_estimate=cost(0, 0),
        name="relay",
    )(scal, mine, first, second)


def project_kernel(
    frames_here, scal, oth, own, gain, shift, weight, first, qkv, qfeat, kfeat, offset
):
    step = pl.program_id(0)
    half_blocks = pl.num_programs(0) // 2
    half_rows = half_blocks * BLK
    within = lax.rem(step, half_blocks) * BLK
    rows = pl.ds(pl.multiple_of(within, BLK), BLK)

    @pl.when(step == 0)
    def _():
        start = frames_here * FRAME_TOK // 16 * 16
        at = frames_here * FRAME_TOK + NOTE - start
        block = own[start : start + 32, :].astype(F32)
        note = block[at : at + 1, :] + block[at + 1 : at + 2, :] + block[at + 2 : at + 3, :]
        share = weight.shape[1] // 3
        offset[...] = jnp.zeros_like(offset)
        for pair in range(share // 128):
            here = pair * 128
            offset[:, 3 * here : 3 * here + 128] = note[:, here : here + 128]
            offset[:, 3 * here + 256 : 3 * here + 384] = note[:, share + here : share + here + 128]

    values = jnp.where(step < half_blocks, oth[rows, :], own[rows, :]).astype(F32)
    xhat, _ = centre(values)
    low = (xhat * gain[...] + shift[...]).astype(BF16)
    first[...] = low
    out = (nn(low, weight[...]) + offset[...]).astype(BF16)
    for pair in range(out.shape[1] // 384):
        at = pair * 384
        qkv[:, at : at + 128] = out[:, at : at + 128] * jnp.asarray(HEAD_DIM**-0.5, BF16)
        qkv[:, at + 128 : at + 384] = out[:, at + 128 : at + 384]
    core, count = scal[0], scal[2]
    half = jnp.where(step < half_blocks, 1 - core, core)
    edge = clip_edge(count, frames_here, half_rows)
    token = within + lax.broadcasted_iota(jnp.int32, (BLK, 128), 0)
    lane = lax.broadcasted_iota(jnp.int32, (BLK, 128), 1)
    clip = jnp.where(half * half_rows + token >= edge, 1, 0)
    clip = jnp.where(token >= frames_here * FRAME_TOK, 2, clip)
    hit = lane == clip
    qfeat[...] = jnp.where(hit, 1.0, 0.0).astype(BF16)
    kfeat[...] = jnp.where(hit, 0.0, jnp.where(lane < 3, -FAR, 0.0)).astype(BF16)


def clip_edge(count, frames_here, half_rows):
    return jnp.where(
        count < frames_here,
        count * FRAME_TOK,
        half_rows + (count - frames_here) * FRAME_TOK,
    )


def clip_span(block, edge, blocks):
    low = jnp.where(block * BLK >= edge, edge // BLK, 0)
    high = jnp.where(block * BLK + BLK - 1 < edge, (edge + BLK - 1) // BLK, blocks)
    return low, high


def project(scal, oth, own, gain, shift, weight, frames_here, half_rows):
    width, cols = weight.shape
    steps = 2 * half_rows // BLK
    rows = 2 * half_rows
    return pl.pallas_call(
        functools.partial(project_kernel, frames_here),
        grid_spec=pltpu.PrefetchScalarGridSpec(
            num_scalar_prefetch=1,
            grid=(steps,),
            in_specs=[
                whole(oth.shape),
                whole(own.shape),
                whole((1, width)),
                whole((1, width)),
                whole((width, cols)),
            ],
            out_specs=[
                pl.BlockSpec((BLK, width), lambda i, *_: (i, 0)),
                pl.BlockSpec((BLK, cols), lambda i, *_: (i, 0)),
                pl.BlockSpec((BLK, 128), lambda i, *_: (i, 0)),
                pl.BlockSpec((BLK, 128), lambda i, *_: (i, 0)),
            ],
            scratch_shapes=[pltpu.VMEM((1, cols), F32)],
        ),
        out_shape=[
            jax.ShapeDtypeStruct((rows, width), BF16),
            jax.ShapeDtypeStruct((rows, cols), BF16),
            jax.ShapeDtypeStruct((rows, 128), BF16),
            jax.ShapeDtypeStruct((rows, 128), BF16),
        ],
        compiler_params=params(1, 10),
        cost_estimate=cost(2 * rows * width * cols, 4 * rows * width + 2 * rows * cols),
        name="project",
    )(scal, oth, own, gain, shift, weight)


def attend_kernel(
    frames_here,
    bk,
    scal,
    q,
    qfeat,
    qkv,
    kfeat,
    mixed,
    wide,
    log_total,
    scores,
    tops,
    acc,
    keys_all,
    values_all,
):
    step = pl.program_id(0)
    half = pl.num_programs(0)
    blocks = 2 * half
    pairs = q.shape[1] // 384
    flip = half * (1 - scal[0])
    edge = clip_edge(scal[2], frames_here, half * BLK)
    low, high = clip_span((step + half * scal[3]) ^ flip, edge, blocks)
    per = bk // BLK
    low, high = low // per, (high + per - 1) // per
    kflip = flip // per
    lane = lax.broadcasted_iota(jnp.int32, (BLK, 128), 1)
    left = lane < HEAD_DIM
    none = jnp.zeros((BLK, 128), BF16)
    queries = []
    for pair in range(pairs):
        both = q[:, pair * 384 : pair * 384 + 128]
        queries.append(jnp.concatenate([jnp.where(left, both, none), qfeat[...]], axis=1))
        queries.append(jnp.concatenate([jnp.where(left, none, both), qfeat[...]], axis=1))
    @pl.when(step == 0)
    def _():
        def prepare(block, carry):
            rows = pl.ds(pl.multiple_of(block * BLK, BLK), BLK)
            for pair in range(pairs):
                at = pair * 384
                keys_all[pair, rows, :128] = qkv[rows, at + 128 : at + 256]
                keys_all[pair, rows, 128:] = kfeat[rows, :]
                both = qkv[rows, at + 256 : at + 384]
                values_all[2 * pair, rows, :128] = jnp.where(left, both, none)
                values_all[2 * pair, rows, 128:] = jnp.where(left, 1.0, 0.0).astype(BF16)
                values_all[2 * pair + 1, rows, :128] = jnp.where(left, none, both)
                values_all[2 * pair + 1, rows, 128:] = jnp.where(left, 0.0, 1.0).astype(BF16)
            return carry

        lax.fori_loop(0, blocks, prepare, 0)

    for head in range(2 * pairs):
        tops[head] = jnp.full((BLK, 128), -3e38, F32)

    def score(block, carry):
        rows = pl.ds(pl.multiple_of((block ^ kflip) * bk, bk), bk)
        for pair in range(pairs):
            keys = keys_all[pair, rows, :]
            for head in (2 * pair, 2 * pair + 1):
                values = nt(queries[head], keys)
                scores[head, block] = values
                top = tops[head]
                for part in range(bk // 128):
                    top = jnp.maximum(top, values[:, part * 128 : (part + 1) * 128])
                tops[head] = top
        return carry

    lax.fori_loop(low, high, score, 0)
    for head in range(2 * pairs):
        tops[head] = jnp.broadcast_to(jnp.max(tops[head], axis=1, keepdims=True), (BLK, 128))
    acc[...] = jnp.zeros_like(acc)
    def mix(block, carry):
        rows = pl.ds(pl.multiple_of((block ^ kflip) * bk, bk), bk)
        for pair in range(pairs):
            soft = []
            for head in (2 * pair, 2 * pair + 1):
                top = tops[head]
                for part in range(bk // 128):
                    piece = scores[head, block, :, part * 128 : (part + 1) * 128]
                    soft.append(jnp.exp(piece - top).astype(BF16))
            values = jnp.concatenate(
                [values_all[2 * pair, rows, :], values_all[2 * pair + 1, rows, :]], axis=0
            )
            acc[pair] += nn(jnp.concatenate(soft, axis=1), values)
        return carry

    lax.fori_loop(low, high, mix, 0)
    for pair in range(pairs):
        cols = slice(pair * 128, (pair + 1) * 128)
        totals = acc[pair, :, 128:]
        out = acc[pair, :, :128] / totals
        wide[:, cols] = out
        mixed[:, cols] = out.astype(BF16)
        logs = (jnp.where(left, tops[2 * pair], tops[2 * pair + 1]) + jnp.log(totals)).T
        log_total[pair, 0, 0:1] = logs[0:1]
        log_total[pair, 0, 1:2] = logs[HEAD_DIM : HEAD_DIM + 1]


def attend(scal, qkv, qfeat, kfeat, frames_here):
    rows, cols = qkv.shape
    width = cols // 3
    pairs = width // 128
    half = rows // BLK // 2
    bk = rows // 2
    return pl.pallas_call(
        functools.partial(attend_kernel, frames_here, bk),
        grid_spec=pltpu.PrefetchScalarGridSpec(
            num_scalar_prefetch=1,
            grid=(half,),
            in_specs=[
                pl.BlockSpec((BLK, cols), lambda i, scal: (i + half * scal[3], 0)),
                pl.BlockSpec((BLK, 128), lambda i, scal: (i + half * scal[3], 0)),
                whole((rows, cols)),
                whole((rows, 128)),
            ],
            out_specs=[
                pl.BlockSpec((BLK, width), lambda i, *_: (i, 0)),
                pl.BlockSpec((BLK, width), lambda i, *_: (i, 0)),
                pl.BlockSpec((pairs, 1, 8, BLK), lambda i, *_: (0, i, 0, 0)),
            ],
            scratch_shapes=[
                pltpu.VMEM((2 * pairs, rows // bk, BLK, bk), F32),
                pltpu.VMEM((2 * pairs, BLK, 128), F32),
                pltpu.VMEM((pairs, BLK, 256), F32),
                pltpu.VMEM((pairs, rows, 256), BF16),
                pltpu.VMEM((2 * pairs, rows, 256), BF16),
            ],
        ),
        out_shape=[
            jax.ShapeDtypeStruct((rows // 2, width), BF16),
            jax.ShapeDtypeStruct((rows // 2, width), F32),
            jax.ShapeDtypeStruct((pairs, half, 8, BLK), F32),
        ],
        compiler_params=params(1, 28),
        cost_estimate=cost(8 * rows * rows * width, 16 * rows * width),
        name="attend",
    )(scal, qkv, qfeat, qkv, kfeat)


def gather_out_weight(scal, own_out, got_up, more_up, out_weight, hid):
    core, plane = scal[0], scal[1]
    share = own_out.shape[0]
    quarter = share // 2
    out_weight[pl.ds(pl.multiple_of(plane * share, 64), share), :] = own_out[...]
    base = (1 - plane) * share
    out_weight[pl.ds(pl.multiple_of(base + core * quarter, 64), quarter), :] = got_up[
        hid : hid + quarter, :
    ]
    out_weight[pl.ds(pl.multiple_of(base + (1 - core) * quarter, 64), quarter), :] = more_up[
        hid : hid + quarter, :
    ]


def up_weight(core, own_up, got_up, more_up, chunk):
    hid = got_up.shape[1]
    if chunk < 2:
        return (more_up, got_up)[chunk][:hid, :]
    pick = (1 - core) if chunk == 2 else core
    return own_up[:, pl.ds(pl.multiple_of(pick * hid, 128), hid)]


def down_weight(core, own_down, got_down, more_down, chunk):
    hid = got_down.shape[1]
    if chunk < 2:
        return (more_down, got_down)[chunk][...]
    pick = (1 - core) if chunk == 2 else core
    return own_down[pl.ds(pl.multiple_of(pick * hid, 128), hid), :]


def ahead_kernel(
    frames_here,
    scal,
    mixed_own,
    mixed_oth,
    tokens,
    cot,
    own_out,
    own_up,
    own_down,
    got_up,
    got_down,
    more_up,
    more_down,
    up_offset,
    gains,
    shifts,
    out_offset,
    down_offset,
    learner,
    learner_offset,
    out_grad_out,
    xhat_out,
    scale_out,
    slope_out,
    second_out,
    out_low_out,
    sums,
    pooled,
    learner_sums,
    learner_offset_sums,
    theirs_out,
    mine_out,
    out_weight,
    hidden_kept,
    down_total,
):
    step = pl.program_id(0)
    core, plane = scal[0], scal[1]
    hid = got_up.shape[1]
    share = own_out.shape[0]

    @pl.when(step == 0)
    def _():
        gather_out_weight(scal, own_out, got_up, more_up, out_weight, hid)
        for ref in (sums, pooled, learner_sums, learner_offset_sums):
            ref[...] = jnp.zeros_like(ref)
        clear(down_total)

    def up_bias(chunk):
        pick = (1 - core) if chunk % 2 == 0 else core
        if chunk >= 2:
            return up_offset[pl.ds(pick, 1), :]
        note = got_up[hid + share // 2 :, :].astype(F32)
        sums = [
            note[3 * i : 3 * i + 1] + note[3 * i + 1 : 3 * i + 2] + note[3 * i + 2 : 3 * i + 3]
            for i in range(2)
        ]
        return jnp.where(pick == 0, sums[0], sums[1])

    mine = pl.ds(pl.multiple_of(core * share, 64), share)
    theirs = pl.ds(pl.multiple_of((1 - core) * share, 64), share)
    attended = nn(mixed_own[...], out_weight[mine, :]) + nn(mixed_oth[...], out_weight[theirs, :])
    residual = tokens[...].astype(F32) + attended + out_offset[...]
    xhat_two, scale_two = centre(residual)
    xhat_out[...] = xhat_two
    scale_out[...] = jnp.broadcast_to(scale_two, scale_out.shape)
    second = (xhat_two * gains[1:2, :] + shifts[1:2, :]).astype(BF16)
    second_out[...] = second
    block_out = residual + down_offset[...]
    for chunk in range(4):
        cols = slice(chunk * hid, (chunk + 1) * hid)
        pre = nn(second, up_weight(core, own_up, got_up, more_up, chunk)) + up_bias(chunk)
        square = pre * pre
        gate = 0.5 + 0.5 * jnp.tanh(pre * (GELU_C + (GELU_A * GELU_C) * square))
        product = pre * gate
        hidden = product.astype(BF16)
        bend = (1.0 - gate) * (2.0 * GELU_C + (6.0 * GELU_A * GELU_C) * square)
        slope_out[:, cols] = (gate + product * bend).astype(BF16)
        hidden_kept[:, cols] = hidden
        block_out = block_out + nn(hidden, down_weight(core, own_down, got_down, more_down, chunk))
    xhat_three, scale_three = centre(block_out)
    third = (xhat_three * gains[2:3, :] + shifts[2:3, :]).astype(BF16)
    logits = nt(third, learner[...]) + learner_offset[...]
    sig = 1.0 / (1.0 + jnp.exp(-logits))
    token = step * BLK + lax.broadcasted_iota(jnp.int32, (BLK, 128), 0)
    first_token = (lax.broadcasted_iota(jnp.int32, (BLK, 128), 1) >> 3) * FRAME_TOK
    inside = (token >= first_token) & (token < first_token + FRAME_TOK)
    inside = inside & (first_token < frames_here * FRAME_TOK)
    maps = jnp.where(inside, sig, 0.0).astype(BF16)
    feature = block_out.astype(BF16)
    pooled[...] += tn(maps, feature)
    maps_grad = nt(feature, cot[...])
    pool_grad = nn(maps, cot[...])
    logits_grad = jnp.where(inside, maps_grad * sig * (1.0 - sig), 0.0).astype(BF16)
    learner_sums[...] += tn(logits_grad, third)
    learner_offset_sums[...] += fold8(logits_grad.astype(F32))
    third_grad = nn(logits_grad, learner[...])
    sums[0:8, :] += fold8(third_grad * xhat_three)
    sums[8:16, :] += fold8(third_grad)
    out_grad = pool_grad + norm_back(xhat_three, scale_three, gains[2:3, :], third_grad)
    sums[16:24, :] += fold8(out_grad)
    out_grad_out[...] = out_grad
    out_low = out_grad.astype(BF16)
    out_low_out[...] = out_low
    for chunk in range(4):
        down_total[chunk] += tn(hidden_kept[:, chunk * hid : (chunk + 1) * hid], out_low)

    @pl.when(step == pl.num_programs(0) - 1)
    def _():
        def strip(index, carry):
            rows = pl.ds(pl.multiple_of(index * STRIP, 32), STRIP)
            for n in range(2):
                theirs_out[n, rows, :] = down_total[2 * n, rows, :].astype(BF16)
                mine_out[n, rows, :] = down_total[2 * n + 1, rows, :].astype(BF16)
            return carry

        lax.fori_loop(0, hid // STRIP, strip, 0)


def behind_kernel(
    pooled_rows,
    scal,
    out_grad,
    out_low,
    xhat_two,
    scale_two,
    slope,
    second,
    mixed_own,
    mixed_oth,
    own_out,
    own_up,
    own_down,
    got_up,
    got_down,
    more_up,
    more_down,
    gains,
    pooled,
    residual_grad_out,
    grad_own,
    grad_oth,
    sums,
    up_sums,
    theirs_out,
    mine_out,
    out_weight,
    up_total,
    out_total,
):
    core, plane = scal[0], scal[1]
    hid = got_up.shape[1]
    share = own_out.shape[0]

    @pl.when(pl.program_id(0) == 0)
    def _():
        gather_out_weight(scal, own_out, got_up, more_up, out_weight, hid)
        for ref in (sums, up_sums):
            ref[...] = jnp.zeros_like(ref)
        clear(up_total)
        clear(out_total)

    mine = pl.ds(pl.multiple_of(core * share, 64), share)
    theirs = pl.ds(pl.multiple_of((1 - core) * share, 64), share)
    low = out_low[...]
    second_turned = second[...].T
    second_grad = None
    for chunk in range(4):
        cols = slice(chunk * hid, (chunk + 1) * hid)
        hidden_grad = nt(low, down_weight(core, own_down, got_down, more_down, chunk))
        pre_grad = (hidden_grad * slope[:, cols].astype(F32)).astype(BF16)
        up_total[chunk] += nn(second_turned, pre_grad)
        up_sums[:, cols] += fold8(pre_grad.astype(F32))
        term = nt(pre_grad, up_weight(core, own_up, got_up, more_up, chunk))
        second_grad = term if second_grad is None else second_grad + term
    xhat = xhat_two[...]
    sums[0:8, :] += fold8(second_grad * xhat)
    sums[8:16, :] += fold8(second_grad)
    residual_grad = out_grad[...] + norm_back(
        xhat, scale_two[:, :1], gains[1:2, :], second_grad
    )
    sums[16:24, :] += fold8(residual_grad)
    residual_grad_out[...] = residual_grad

    @pl.when(pl.program_id(0) == pl.num_programs(0) - 1)
    def _():
        residual_grad_out[BLK - pooled_rows :, :] = pooled[:pooled_rows, :]

    residual_low = residual_grad.astype(BF16)
    grad_own[...] = nt(residual_low, out_weight[mine, :]).astype(BF16)
    grad_oth[...] = nt(residual_low, out_weight[theirs, :]).astype(BF16)
    out_total[0] += tn(mixed_own[...], residual_low)
    out_total[1] += tn(mixed_oth[...], residual_low)

    @pl.when(pl.program_id(0) == pl.num_programs(0) - 1)
    def _():
        width = second.shape[1]
        half = width // 2

        def strip(index, carry):
            rows = pl.ds(pl.multiple_of(index * STRIP, 32), STRIP)
            for n in range(2):
                theirs_out[n, rows, :] = up_total[2 * n, rows, :].astype(BF16)
                mine_out[n, rows, :] = up_total[2 * n + 1, rows, :].astype(BF16)
            return carry

        lax.fori_loop(0, width // STRIP, strip, 0)
        for out, column in ((theirs_out, 1 - core), (mine_out, core)):
            for n in range(2):
                side = (1 - plane) if n == 0 else plane
                at = pl.ds(pl.multiple_of(column * half, 128), half)
                grad = out_total[jnp.where(side == core, 0, 1), :, at].astype(BF16)
                out[n, width:, :half] = grad[: share // 2]
                out[n, width:, half:] = grad[share // 2 :]


def row_block(cols):
    return pl.BlockSpec((BLK, cols), lambda i, *_: (i, 0))


def held(shape):
    return pl.BlockSpec(shape, lambda *_: (0,) * len(shape))


def row_call(kernel, name, scal, rowed, wholes, row_outs, held_outs, scratch, flops, mib, low_outs=()):
    rows = rowed[0].shape[0]
    nbytes = sum(x.size * x.dtype.itemsize for x in wholes)
    nbytes += rows * sum(c * (2 if t == BF16 else 4) for c, t in row_outs)
    return pl.pallas_call(
        kernel,
        grid_spec=pltpu.PrefetchScalarGridSpec(
            num_scalar_prefetch=1,
            grid=(rows // BLK,),
            in_specs=[row_block(x.shape[1]) for x in rowed] + [whole(x.shape) for x in wholes],
            out_specs=[row_block(cols) for cols, _ in row_outs]
            + [held(s) for s in held_outs]
            + [whole(s) for s in low_outs],
            scratch_shapes=scratch,
        ),
        out_shape=[jax.ShapeDtypeStruct((rows, cols), t) for cols, t in row_outs]
        + [jax.ShapeDtypeStruct(s, F32) for s in held_outs]
        + [jax.ShapeDtypeStruct(s, BF16) for s in low_outs],
        compiler_params=params(1, mib),
        cost_estimate=cost(flops, nbytes),
        name=name,
    )(scal, *rowed, *wholes)


def ahead(scal, mixed_own, mixed_oth, packed, cot, weights, up_offset, small, frames_here):
    rows, share = mixed_own.shape
    width = packed.shape[1]
    hidden = 2 * up_offset.size
    return row_call(
        functools.partial(ahead_kernel, frames_here),
        "ahead",
        scal,
        [mixed_own, mixed_oth, packed],
        [cot, *weights, up_offset, *small],
        [
            (width, F32),
            (width, F32),
            (128, F32),
            (hidden, BF16),
            (width, BF16),
            (width, BF16),
        ],
        [(24, width), (128, width), (128, width), (8, 128)],
        [
            pltpu.VMEM((2 * share, width), BF16),
            pltpu.VMEM((BLK, hidden), BF16),
            pltpu.VMEM((4, hidden // 4, width), F32),
        ],
        2 * rows * width * (3 * hidden + width),
        42,
        [(2, hidden // 4, width)] * 2,
    )


def behind(scal, rowed, weights, gains, pooled, maps_all):
    rows, width = rowed[0].shape
    share = weights[0].shape[0]
    hidden = rowed[4].shape[1]
    hid = hidden // 4
    return row_call(
        functools.partial(behind_kernel, maps_all),
        "behind",
        scal,
        rowed,
        [*weights, gains, pooled],
        [(width, F32), (share, BF16), (share, BF16)],
        [(24, width), (8, hidden)],
        [
            pltpu.VMEM((2 * share, width), BF16),
            pltpu.VMEM((4, width, hid), F32),
            pltpu.VMEM((2, share, width), F32),
        ],
        2 * rows * width * (3 * hidden + 2 * width),
        44,
        [(2, width + share // 2, hid)] * 2,
    )


def attend_back_kernel(
    frames_here,
    scal,
    k,
    v,
    kfeat,
    q,
    qfeat,
    grad_oth,
    grad_own,
    wide_oth,
    wide_own,
    log_oth,
    log_own,
    out_oth,
    out_own,
    queries,
    grads,
    inner,
    logs,
    dq,
    dkv,
):
    step = pl.program_id(0)
    half = grad_oth.shape[0] // BLK
    blocks = 2 * half
    flip = half * (1 - scal[0])
    edge = clip_edge(scal[2], frames_here, half * BLK)
    low, high = clip_span(step ^ flip, edge, blocks)
    bq = half * BLK
    low, high = low // half, (high + half - 1) // half
    qflip = 1 - scal[0]
    lane = lax.broadcasted_iota(jnp.int32, (BLK, 128), 1)
    left = lane < HEAD_DIM
    none = jnp.zeros((BLK, 128), BF16)

    @pl.when(step == 0)
    def _():
        dq[...] = jnp.zeros_like(dq)
        for side, (grad, wide, log_total) in enumerate(
            ((grad_oth, wide_oth, log_oth), (grad_own, wide_own, log_own))
        ):
            for block in range(bq // BLK):
                here = slice(block * BLK, (block + 1) * BLK)
                rows = slice(side * bq + block * BLK, side * bq + (block + 1) * BLK)
                grads[rows, :] = grad[here, :]
                queries[rows, :128] = q[rows, :]
                queries[rows, 128:] = qfeat[rows, :]
                product = (grad[here, :].astype(F32) * wide[here, :]).T
                inner[side, 0:1, here] = jnp.sum(product[:HEAD_DIM], axis=0, keepdims=True)
                inner[side, 1:2, here] = jnp.sum(product[HEAD_DIM:], axis=0, keepdims=True)
                logs[side, :, here] = log_total[0, block]

    ka = jnp.where(left, k[...], none)
    kb = jnp.where(left, none, k[...])
    key_a = jnp.concatenate([ka, kfeat[...]], axis=1)
    key_b = jnp.concatenate([kb, kfeat[...]], axis=1)
    keys = jnp.concatenate([ka, kb], axis=0)
    va = jnp.where(left, v[...], none)
    vb = jnp.where(left, none, v[...])
    dkv[...] = jnp.zeros_like(dkv)

    def pair(block, carry):
        local = block ^ qflip
        rows = pl.ds(pl.multiple_of(local * bq, bq), bq)
        query = queries[rows, :]
        grad = grads[rows, :]
        soft_a = jnp.exp(nt(key_a, query) - logs[local, 0:1])
        soft_b = jnp.exp(nt(key_b, query) - logs[local, 1:2])
        score_a = (soft_a * (nt(va, grad) - inner[local, 0:1])).astype(BF16)
        score_b = (soft_b * (nt(vb, grad) - inner[local, 1:2])).astype(BF16)
        dkv[0] += nn(soft_a.astype(BF16), grad)
        dkv[1] += nn(soft_b.astype(BF16), grad)
        dkv[2] += nn(score_a, query[:, :128])
        dkv[3] += nn(score_b, query[:, :128])
        dq[rows, :] += tn(jnp.concatenate([score_a, score_b], axis=0), keys)
        return carry

    lax.fori_loop(low, high, pair, 0)
    dk = jnp.where(left, dkv[2], dkv[3]).astype(BF16)
    dv = jnp.where(left, dkv[0], dkv[1]).astype(BF16)
    within = pl.ds(pl.multiple_of(lax.rem(step, half) * BLK, BLK), BLK)

    @pl.when(step < half)
    def _():
        out_oth[within, 128:256] = dk
        out_oth[within, 256:] = dv

    @pl.when(step >= half)
    def _():
        out_own[within, 128:256] = dk
        out_own[within, 256:] = dv

    @pl.when(step == blocks - 1)
    def _():
        half_rows = out_oth.shape[0]
        out_oth[:, :128] = (dq[:half_rows, :] * HEAD_DIM**-0.5).astype(BF16)
        out_own[:, :128] = (dq[half_rows:, :] * HEAD_DIM**-0.5).astype(BF16)

def attend_back(scal, qkv, qfeat, kfeat, grad_oth, grad_own, wide, logs, frames_here):
    rows = qkv.shape[0]
    blocks = rows // BLK
    one = pl.Buffered(1)
    half_rows = pl.BlockSpec((rows // 2, 128), lambda j, scal: (0, scal[3]), pipeline_mode=one)
    half_logs = pl.BlockSpec(
        (1, blocks // 2, 8, BLK), lambda j, scal: (scal[3], 0, 0, 0), pipeline_mode=one
    )
    return pl.pallas_call(
        functools.partial(attend_back_kernel, frames_here),
        grid_spec=pltpu.PrefetchScalarGridSpec(
            num_scalar_prefetch=1,
            grid=(blocks,),
            in_specs=[
                pl.BlockSpec((BLK, 128), lambda j, scal: (j, 3 * scal[3] + 1)),
                pl.BlockSpec((BLK, 128), lambda j, scal: (j, 3 * scal[3] + 2)),
                pl.BlockSpec((BLK, 128), lambda j, *_: (j, 0)),
                pl.BlockSpec((rows, 128), lambda j, scal: (0, 3 * scal[3]), pipeline_mode=one),
                whole((rows, 128)),
                half_rows,
                half_rows,
                half_rows,
                half_rows,
                half_logs,
                half_logs,
            ],
            out_specs=[pl.BlockSpec((rows // 2, 384), lambda j, *_: (0, 0))] * 2,
            scratch_shapes=[
                pltpu.VMEM((rows, 256), BF16),
                pltpu.VMEM((rows, 128), BF16),
                pltpu.VMEM((2, 8, rows // 2), F32),
                pltpu.VMEM((2, 8, rows // 2), F32),
                pltpu.VMEM((rows, 128), F32),
                pltpu.VMEM((4, BLK, 128), F32),
            ],
        ),
        out_shape=[jax.ShapeDtypeStruct((rows // 2, 384), BF16)] * 2,
        compiler_params=params(1, 14),
        cost_estimate=cost(40 * rows * rows * 128, 30 * rows * 128),
        name="attend_back",
    )(scal, qkv, qkv, kfeat, qkv, qfeat, grad_oth, grad_own, *wide, *logs)


def project_grad_kernel(pairs, scal, first, *refs):
    oth, own = refs[:pairs], refs[pairs : 2 * pairs]
    theirs, mine, offsets = refs[2 * pairs :]
    step = pl.program_id(0)
    half = oth[0].shape[0]
    one = jnp.concatenate([x[...] for x in oth], axis=1)
    two = jnp.concatenate([x[...] for x in own], axis=1)
    out = (tn(first[:half, :], one) + tn(first[half:, :], two)).astype(BF16)

    @pl.when(step == 0)
    def _():
        theirs[...] = out
        offsets[...] = fold8(one.astype(F32)) + fold8(two.astype(F32))

    @pl.when(step == 1)
    def _():
        mine[...] = out


def project_grad(scal, first, oth, own):
    pairs = len(oth)
    rows, width = first.shape
    cols = 384 * pairs
    return pl.pallas_call(
        functools.partial(project_grad_kernel, pairs),
        grid_spec=pltpu.PrefetchScalarGridSpec(
            num_scalar_prefetch=1,
            grid=(2,),
            in_specs=[
                pl.BlockSpec((rows, width // 2), lambda n, scal: (0, (1 - scal[0]) ^ n)),
            ]
            + [whole((rows // 2, 384))] * (2 * pairs),
            out_specs=[held((width // 2, cols)), held((width // 2, cols)), held((8, cols))],
        ),
        out_shape=[
            jax.ShapeDtypeStruct((width // 2, cols), BF16),
            jax.ShapeDtypeStruct((width // 2, cols), BF16),
            jax.ShapeDtypeStruct((8, cols), F32),
        ],
        compiler_params=params(1, 12),
        cost_estimate=cost(2 * rows * width * cols, 2 * rows * (width + cols)),
        name="project_grad",
    )(scal, first, *oth, *own)


def first_grad_kernel(pairs, *refs):
    own, got = refs[:pairs], refs[pairs : 2 * pairs]
    mine, theirs, tokens, out, sums = refs[2 * pairs :]
    total = nt(jnp.concatenate([x[...] for x in own], axis=1), mine[...])
    total = total + nt(jnp.concatenate([x[...] for x in got], axis=1), theirs[...])
    out[...] = total.astype(BF16)

    @pl.when(pl.program_id(0) == 0)
    def _():
        sums[...] = jnp.zeros_like(sums)

    xhat, _ = centre(tokens[...].astype(F32))
    sums[0:8, :] += fold8(total * xhat)
    sums[8:16, :] += fold8(total)


def first_grad(own, got, mine, theirs, packed):
    pairs = len(own)
    rows, cols = own[0].shape
    width = mine.shape[0]
    return pl.pallas_call(
        functools.partial(first_grad_kernel, pairs),
        grid=(rows // BLK,),
        in_specs=[pl.BlockSpec((BLK, cols), lambda i: (i, 0))] * (2 * pairs)
        + [whole(mine.shape), whole(theirs.shape), pl.BlockSpec((BLK, width), lambda i: (i, 0))],
        out_specs=[
            pl.BlockSpec((BLK, width), lambda i: (i, 0)),
            pl.BlockSpec((16, width), lambda i: (0, 0)),
        ],
        out_shape=[
            jax.ShapeDtypeStruct((rows, width), BF16),
            jax.ShapeDtypeStruct((16, width), F32),
        ],
        compiler_params=params(1, 12),
        cost_estimate=cost(
            4 * pairs * rows * width * cols, 4 * pairs * rows * cols + 4 * width * cols * pairs
        ),
        name="first_grad",
    )(*own, *got, mine, theirs, packed)


def last_kernel(scal, tokens, grad, grad_got, residual, residual_got, gain, out):
    xhat, scale = centre(tokens[...].astype(F32))
    straight = scal[0] == scal[1]
    wide = jnp.where(straight, grad[...], grad_got[...]).astype(F32)
    base = jnp.where(straight, residual[...], residual_got[...])
    out[...] = base + norm_back(xhat, scale, gain[...], wide)


def last(scal, packed, grad, grad_got, residual, residual_got, gain, tokens_here):
    rows, width = grad.shape
    return pl.pallas_call(
        last_kernel,
        grid_spec=pltpu.PrefetchScalarGridSpec(
            num_scalar_prefetch=1,
            grid=(rows // BLK,),
            in_specs=[row_block(width)] * 5 + [whole((1, width))],
            out_specs=row_block(width),
        ),
        out_shape=jax.ShapeDtypeStruct((tokens_here, width), F32),
        compiler_params=params(1, 12),
        cost_estimate=cost(20 * rows * width, 12 * rows * width),
        name="last",
    )(scal, packed, grad, grad_got, residual, residual_got, gain)


def table_kernel(
    frames_here, scal, ahead_sums, behind_sums, first_sums, learner, learner_offset, up, *refs
):
    offsets, out = refs[:-1], refs[-1]
    core, plane = scal[0], scal[1]
    width = out.shape[1]
    hid = up.shape[1] // 4

    def total(ref, at):
        return jnp.sum(ref[at : at + 8, :], axis=0, keepdims=True)

    out[...] = jnp.zeros_like(out)
    for row, (ref, at) in enumerate(
        (
            (first_sums, 0),
            (behind_sums, 0),
            (ahead_sums, 0),
            (first_sums, 8),
            (behind_sums, 8),
            (ahead_sums, 8),
            (behind_sums, 16),
            (ahead_sums, 16),
        )
    ):
        out[row : row + 1, :] = total(ref, at)
    out[8:16, :] = sum(learner[MAPS * i : MAPS * (i + 1), :] for i in range(frames_here))
    row = total(learner_offset, 0)
    lane = lax.broadcasted_iota(jnp.int32, (1, 128), 1)
    kept = row
    for i in range(1, frames_here):
        kept = kept + pltpu.roll(row, 128 - MAPS * i, 1)
    out[16:17, :128] = jnp.where(lane < MAPS, kept, 0.0)
    for chunk in range(4):
        side = (1 - plane) if chunk < 2 else plane
        pick = (1 - core) if chunk % 2 == 0 else core
        out[pl.ds(17 + 2 * side + pick, 1), :] = jnp.sum(
            up[:, chunk * hid : (chunk + 1) * hid], axis=0, keepdims=True
        )
    pair = 0
    for ref in offsets:
        for at in range(0, ref.shape[1], 384):
            to = pl.ds(pl.multiple_of(core * (width // 2) + pair * 128, 128), 128)
            out[21:22, to] = jnp.sum(ref[:, at : at + 128], axis=0, keepdims=True)
            out[22:23, to] = jnp.sum(ref[:, at + 256 : at + 384], axis=0, keepdims=True)
            pair += 1


def small_table(scal, frames_here, *parts):
    width = parts[0].shape[1]
    return pl.pallas_call(
        functools.partial(table_kernel, frames_here),
        grid_spec=pltpu.PrefetchScalarGridSpec(
            num_scalar_prefetch=1,
            grid=(1,),
            in_specs=[held(x.shape) for x in parts],
            out_specs=held((24, width)),
        ),
        out_shape=jax.ShapeDtypeStruct((24, width), F32),
        compiler_params=pltpu.CompilerParams(vmem_limit_bytes=6 * 1024 * 1024),
        cost_estimate=cost(0, 1 << 20),
        name="small_table",
    )(scal, *parts)


def body(
    tokens,
    frame_counts,
    norm_gains,
    norm_shifts,
    attend_weight,
    attend_offset,
    output_weight,
    output_offset,
    expand_weight,
    expand_offset,
    contract_weight,
    contract_offset,
    learner_weight,
    learner_offset,
    pooled_cotangent,
):
    tokens_here, width = tokens.shape
    frames_here = tokens_here // FRAME_TOK
    half_rows = -(-tokens_here // BLK) * BLK
    share = attend_weight.shape[2]
    hid = contract_weight.shape[0] // 2
    chips = lax.axis_size("chip")
    core, plane = lax.axis_index("core"), lax.axis_index("mp")
    straight = core == plane
    flip2 = [(0, 1), (1, 0)]

    def turn(x):
        return lax.ppermute(x, ("core", "mp"), [(1, 2), (2, 1)])

    def to_core(x):
        return lax.ppermute(x, "core", flip2)

    def to_plane(x):
        return lax.ppermute(x, "mp", flip2)

    chip = lax.axis_index("chip")
    side = chip % 2
    hops = []
    while (2 << len(hops)) < chips:
        hops.append(2 << len(hops))

    def hop(x, step):
        return lax.ppermute(x, "chip", [(i, i ^ step) for i in range(chips)])

    def low(x):
        return x.astype(BF16)

    def plus(a, b):
        return a.astype(F32) + b.astype(F32)

    def pick(x, index):
        return lax.dynamic_index_in_dim(x, index, 0, keepdims=False)

    def halves_of(x):
        rows = x.shape[-2] // 2
        return x.reshape(*x.shape[:-2], 2, rows, x.shape[-1])

    def join(x, other, index, axis):
        return jnp.concatenate(
            [jnp.where(index == 0, x, other), jnp.where(index == 0, other, x)], axis=axis
        )

    pairs = share // 128

    weight_mine = attend_weight.reshape(width, 3 * share)
    weight_part = lax.dynamic_slice_in_dim(attend_weight, side * (width // 2), width // 2, 0)
    weight_part = weight_part.reshape(width // 2, 3 * share)
    weight_got = turn(weight_part)
    packed = pack(
        after(tokens, weight_part),
        pooled_cotangent.reshape(frames_here * MAPS, width),
        attend_offset.reshape(1, 2 * share),
        frame_counts[:, :1].astype(F32),
        half_rows,
    )
    got_packed = turn(packed)
    weight_rest = lax.ppermute(
        weight_got,
        ("chip", "core", "mp"),
        [(4 * i + j, 4 * (i ^ 1) + j) for i in range(chips) for j in (1, 2)],
    )
    weight_here = relay(
        jnp.stack([core, plane, side]).astype(jnp.int32), weight_mine, weight_got, weight_rest
    )
    left, notes = expand_offset.reshape(2, hid), []
    for _ in range(3):
        notes.append(lax.reduce_precision(left, 8, 7))
        left = left - notes[-1]
    notes = jnp.stack(notes, axis=1).reshape(6, hid)
    up_quarter = jnp.concatenate(
        [
            lax.dynamic_slice_in_dim(expand_weight, core * hid, hid, 1),
            lax.dynamic_slice_in_dim(output_weight, core * (share // 2), share // 2, 0),
            jnp.pad(notes, ((0, 10), (0, 0))).astype(BF16),
        ],
        axis=0,
    )
    down_quarter = lax.dynamic_slice_in_dim(contract_weight, core * hid, hid, 0)
    own = jnp.where(
        straight, packed, after(got_packed, weight_here, up_quarter, down_quarter)
    )
    oth = to_core(own)
    count = own[tokens_here + NOTE + 3, 0].astype(jnp.int32)
    numbered = [
        jnp.stack([core.astype(jnp.int32), plane.astype(jnp.int32), count, jnp.int32(i)])
        for i in range(pairs)
    ]
    scal = numbered[0]

    up_got_a = to_plane(after(up_quarter, own, weight_here))
    down_got_a = to_plane(after(down_quarter, oth))

    first, qkv, qfeat, kfeat = project(
        scal,
        oth,
        own,
        norm_gains[0:1],
        norm_shifts[0:1],
        weight_here,
        frames_here,
        half_rows,
    )
    weight_there = to_core(after(weight_here, qkv))
    mixed_send, wide_oth, logs_oth = attend(numbered[0], qkv, qfeat, kfeat, frames_here)
    mixed_oth = to_core(mixed_send)
    up_got_b = to_core(after(up_got_a, mixed_send))
    mixed_own, wide_own, logs_own = attend(
        after(numbered[1], mixed_send, weight_there), qkv, qfeat, kfeat, frames_here
    )
    down_got_b = to_core(after(down_got_a, mixed_own))

    maps_all = frames_here * MAPS
    cot = jnp.pad(own[half_rows:], ((0, 128 - maps_all), (0, 0)))
    learner = jnp.pad(jnp.tile(learner_weight.T, (frames_here, 1)), ((0, 128 - maps_all), (0, 0)))
    learner_bias = jnp.pad(jnp.tile(learner_offset, frames_here), (0, 128 - maps_all))[None]
    weights = (
        *(
            pltpu.with_memory_space_constraint(x, pltpu.HBM)
            for x in (output_weight, expand_weight, contract_weight)
        ),
        up_got_a,
        down_got_a,
        up_got_b,
        down_got_b,
    )
    (
        out_grad,
        xhat_two,
        scale_two,
        slope,
        second,
        out_low,
        sums_ahead,
        pooled,
        learner_sums,
        learner_offset_sums,
        down_theirs,
        down_mine,
    ) = ahead(
        scal,
        mixed_own,
        mixed_oth,
        own,
        cot,
        weights,
        expand_offset.reshape(2, hid),
        (
            norm_gains,
            norm_shifts,
            output_offset[None],
            contract_offset[None],
            learner,
            learner_bias,
        ),
        frames_here,
    )

    down_got = to_core(down_theirs)
    down_send = low(plus(down_got[0], down_mine[0]))
    down_keep = plus(down_got[1], down_mine[1])
    down_plane = to_plane(down_send)

    (
        residual_grad,
        grad_own,
        grad_send,
        sums_behind,
        up_sums,
        up_theirs,
        up_mine,
    ) = behind(
        after(scal, down_send),
        [out_grad, out_low, xhat_two, scale_two, slope, second, mixed_own, mixed_oth],
        weights,
        norm_gains,
        pooled,
        maps_all,
    )
    down_half = halves_of(plus(down_keep, after(down_plane, residual_grad)))
    down_x_send = low(pick(down_half, 1 - side))
    down_x_keep = pick(down_half, side)
    down_x = hop(down_x_send, 1)
    up_got = to_core(after(up_theirs, down_x_send))
    grad_oth = to_core(after(grad_send, down_x_send))
    up_half = halves_of(plus(up_got, after(up_mine, down_x_send)))
    up_x_send = low(lax.dynamic_index_in_dim(up_half, 1 - side, 1, keepdims=False))
    up_x_keep = lax.dynamic_index_in_dim(up_half, side, 1, keepdims=False)
    up_x = hop(up_x_send, 1)

    def back(pair, *gate):
        return attend_back(
            after(numbered[pair], *gate),
            qkv,
            qfeat,
            kfeat,
            grad_oth,
            grad_own,
            (wide_oth, wide_own),
            (logs_oth, logs_own),
            frames_here,
        )

    def project_fold(their, mine):
        got = to_core(their)
        return jnp.where(straight, got, mine), jnp.where(straight, mine, got)

    bit = (chip // 2) % 2

    def split(x):
        parts = halves_of(x)
        return low(pick(parts, 1 - bit)), pick(parts, bit)

    residual_got = turn(after(residual_grad, up_x_send))
    down_send, down_keep = split(plus(down_x_keep, after(down_x, up_x_send)))
    down_z = hop(down_send, hops[0])
    oth_0, own_0 = back(0, down_send)
    got_0 = to_core(oth_0)
    down_sum = plus(down_keep, after(down_z, oth_0))
    down_low = low(down_sum)
    down_z = hop(down_low, hops[1])
    up_y = plus(up_x_keep, after(up_x, oth_0))
    up_y_send = low(up_y[0])
    up_y_got = to_plane(up_y_send)

    residual_got = after(residual_got, oth_0)
    oth_1, own_1 = back(1, down_low, up_y_send, residual_got, got_0)
    got_1 = to_core(oth_1)

    def rest(total, got, steps):
        total = plus(total, got)
        for step in steps:
            total = plus(total, hop(low(total), step))
        return low(total)

    down_sum = rest(down_sum, after(down_z, oth_1), hops[2:])
    down_z = hop(down_sum, hops[0])
    up_send, up_keep = split(plus(up_y[1], after(up_y_got, oth_1)))
    up_z = hop(up_send, hops[0])
    their_0, mine_0, offsets_0 = project_grad(
        after(scal, down_sum, up_send), first, (oth_0, oth_1), (own_0, own_1)
    )
    early_send, early_keep = project_fold(their_0, mine_0)
    early_got = to_plane(early_send)
    up_sum = plus(up_keep, after(up_z, mine_0))
    up_low = low(up_sum)
    up_z = hop(up_low, hops[1])

    down_sum = join(down_sum, after(down_z, mine_0), bit, 0)
    down_x = hop(down_sum, 1)

    oth_2, own_2 = back(2, early_send, up_low, down_sum, got_1)
    got_2 = to_core(oth_2)
    up_sum = rest(up_sum, after(up_z, oth_2), hops[2:])
    up_z = hop(up_sum, hops[0])
    early_half = halves_of(plus(early_keep, after(early_got, oth_2)))
    early_send = low(pick(early_half, 1 - side))
    early_keep = pick(early_half, side)
    early_x = hop(early_send, 1)
    their_2, mine_2, offsets_2 = project_grad(
        after(scal, up_sum, early_send), first, (oth_2,), (own_2,)
    )
    late_send, late_keep = project_fold(their_2, mine_2)
    late_got = to_plane(late_send)
    up_sum = join(up_sum, after(up_z, mine_2), bit, 0)
    down_sum = join(down_sum, after(down_x, mine_2), side, 0)
    down_got = to_core(down_sum)
    early_sum = plus(early_keep, after(early_x, mine_2))
    early_low = low(early_sum)
    early_z = hop(early_low, hops[0])
    first_low, first_sums = first_grad(
        (own_0, own_1, own_2),
        (got_0, got_1, got_2),
        weight_here,
        weight_there,
        after(own, late_send, up_sum, early_low),
    )
    first_got = turn(first_low)
    table = small_table(
        scal,
        frames_here,
        sums_ahead,
        sums_behind,
        first_sums,
        learner_sums,
        learner_offset_sums,
        up_sums,
        offsets_0,
        offsets_2,
    )

    early_sum = plus(early_sum, after(early_z, table))
    early_low = low(early_sum)
    early_z = hop(early_low, hops[1])
    late_half = halves_of(plus(late_keep, after(late_got, early_low)))
    late_send = low(pick(late_half, 1 - side))
    late_keep = pick(late_half, side)
    late_x = hop(late_send, 1)
    table = table + after(to_core(table), late_send)
    table_got = to_plane(table)
    up_x = hop(after(up_sum, table), 1)
    late_sum = plus(late_keep, after(late_x, table))
    late_low = low(late_sum)
    late_z = hop(late_low, hops[0])
    table = table + after(table_got, late_low)
    late_sum = plus(late_sum, after(late_z, table))
    late_low = low(late_sum)
    late_z = hop(late_low, hops[1])
    table_got = hop(after(table, late_low), hops[0])
    early_sum = rest(early_sum, after(early_z, late_low), hops[2:])
    early_x = hop(early_sum, 1)
    table = table + after(table_got, early_sum)
    table_got = hop(table, hops[1])
    up_sum = join(up_sum, after(up_x, table), side, 0)
    up_got = to_core(up_sum)
    late_sum = rest(late_sum, after(late_z, up_sum), hops[2:])
    late_x = hop(late_sum, 1)
    table = table + after(table_got, late_sum)
    for step in hops[2:]:
        table = table + hop(table, step)
    table_got = hop(table, 1)
    tokens_gradient = last(
        after(scal, table),
        packed,
        first_low,
        first_got,
        residual_grad,
        residual_got,
        norm_gains[0:1],
        tokens_here,
    )
    table = table + after(table_got, tokens_gradient)
    early_sum = join(early_sum, after(early_x, tokens_gradient), side, 0)
    early_got = to_core(early_sum)
    late_sum = join(late_sum, after(late_x, early_sum), side, 0)
    late_got = to_core(late_sum)

    def two(x, other):
        return jnp.where(core == 0, x, other), jnp.where(core == 0, other, x)

    def out_block(x):
        return jnp.concatenate([x[width:, : width // 2], x[width:, width // 2 :]], axis=0)

    down_first, down_second = two(down_sum, down_got)
    up_first, up_second = two(up_sum, up_got)
    contract_gradient = jnp.concatenate([down_first, down_second], axis=0).astype(F32)
    expand_gradient = jnp.concatenate([up_first[:width], up_second[:width]], axis=1).astype(F32)
    output_gradient = jnp.concatenate([out_block(up_first), out_block(up_second)], axis=1).astype(F32)

    early_two, late_two = two(early_sum, early_got), two(late_sum, late_got)

    def column(pair, part):
        halves, at = (early_two, pair) if pair < pairs - 1 else (late_two, 0)
        at = at * 384 + part * 128
        return jnp.concatenate([x[:, at : at + 128] for x in halves], axis=0)

    attend_gradient = jnp.stack(
        [
            jnp.concatenate([column(pair, part) for pair in range(pairs)], axis=1)
            for part in range(3)
        ],
        axis=1,
    ).astype(F32)
    return (
        jnp.where(straight, pooled[:maps_all], residual_got[half_rows - maps_all :]).reshape(
            frames_here, MAPS, width
        ),
        tokens_gradient,
        table[0:3],
        table[3:6],
        attend_gradient,
        lax.dynamic_slice_in_dim(table[21:23], plane * share, share, 1),
        output_gradient,
        table[6],
        expand_gradient,
        lax.dynamic_slice_in_dim(table[17:21], 2 * plane, 2, 0).reshape(2 * hid),
        contract_gradient,
        table[7],
        table[8:16].T,
        table[16, :MAPS],
    )


def solution(mesh):
    groups, sides = mesh.devices.shape
    fine = Mesh(mesh.devices.reshape(groups // 2, 2, sides), ("chip", "core", "mp"))
    dp = ("chip", "core")
    every = ("chip", "core", "mp")
    return jax.shard_map(
        body,
        mesh=fine,
        in_specs=(
            P(every, None),
            P(dp, None),
            P(),
            P(),
            P(None, None, "mp"),
            P(None, "mp"),
            P("mp", None),
            P(),
            P(None, "mp"),
            P("mp"),
            P("mp", None),
            P(),
            P(),
            P(),
            P(every, None, None),
        ),
        out_specs=(
            P(every, None, None),
            P(every, None),
            P(),
            P(),
            P(None, None, "mp"),
            P(None, "mp"),
            P("mp", None),
            P(),
            P(None, "mp"),
            P("mp"),
            P("mp", None),
            P(),
            P(),
            P(),
        ),
        check_vma=False,
    )
```

```python
import functools

import jax
import jax.numpy as jnp
from jax import lax
from jax.experimental import pallas as pl
from jax.experimental.pallas import tpu as pltpu
from jax.sharding import Mesh, PartitionSpec as P

HEAD_DIM = 64
MAPS = 8
FRAME_TOK = 196
EPS = 1e-06
BLK = 256
COST = 20.0
FAR = 1e30
GELU_C = 0.7978845608028654
GELU_A = 0.044715

F32 = jnp.float32
BF16 = jnp.bfloat16


def nn(a, b):
    return lax.dot_general(a, b, (((1,), (0,)), ((), ())), preferred_element_type=F32)


def nt(a, b):
    return lax.dot_general(a, b, (((1,), (1,)), ((), ())), preferred_element_type=F32)


def tn(a, b):
    return lax.dot_general(a, b, (((0,), (0,)), ((), ())), preferred_element_type=F32)


def fold8(values):
    rows, width = values.shape
    return jnp.sum(values.reshape(rows // 8, 8, width), axis=0)


def centre(values):
    average = jnp.mean(values, axis=-1, keepdims=True)
    centred = values - average
    spread = jnp.mean(centred * centred, axis=-1, keepdims=True)
    scale = lax.rsqrt(spread + EPS)
    return centred * scale, scale


def norm_back(xhat, scale, gain, grad):
    scaled = grad * gain
    along = jnp.mean(scaled * xhat, axis=-1, keepdims=True)
    return scale * (scaled - jnp.mean(scaled, axis=-1, keepdims=True) - xhat * along)


def cost(flops, nbytes):
    return pl.CostEstimate(
        flops=int(flops * COST), bytes_accessed=int(nbytes * COST), transcendentals=0
    )


def params(n, mib=60):
    return pltpu.CompilerParams(
        dimension_semantics=("arbitrary",) * n, vmem_limit_bytes=mib * 1024 * 1024
    )


def whole(shape):
    return pl.BlockSpec(shape, lambda *_: (0,) * len(shape), pipeline_mode=pl.Buffered(1))


def after(value, *others):
    return lax.optimization_barrier((value, others))[0]


NOTE = 4


def pack_kernel(tokens, cot, offset, count, out):
    here = tokens.shape[0]
    rows = out.shape[0] - cot.shape[0]
    edge = here // 16 * 16
    width = out.shape[1]
    out[:here, :] = tokens[...]
    left = offset[...]
    lines = []
    for _ in range(3):
        line = left.astype(BF16)
        lines.append(line.astype(F32))
        left = left - lines[-1]
    lines.append(jnp.broadcast_to(count[...], (1, width)))
    tail = rows - here
    row = lax.broadcasted_iota(jnp.int32, (tail, width), 0)
    block = jnp.zeros((tail, width), F32)
    for i, line in enumerate(lines):
        block = jnp.where(row == NOTE + i, line, block)
    out[here:rows, :] = block.astype(BF16)
    out[rows:, :] = cot[...]


def pack(tokens, cot, offset, count, half_rows):
    rows, width = half_rows + cot.shape[0], tokens.shape[1]
    return pl.pallas_call(
        pack_kernel,
        in_specs=[pl.BlockSpec(x.shape) for x in (tokens, cot, offset, count)],
        out_specs=pl.BlockSpec((rows, width)),
        out_shape=jax.ShapeDtypeStruct((rows, width), BF16),
        compiler_params=pltpu.CompilerParams(vmem_limit_bytes=8 * 1024 * 1024),
        cost_estimate=cost(0, 4 * rows * width),
        name="pack",
    )(tokens, cot, offset, count)


def relay_kernel(scal, mine, first, second, out):
    straight = scal[0] == scal[1]
    rows = first.shape[0]
    swap = scal[2] == 1
    for half in range(2):
        here = slice(half * rows, (half + 1) * rows)
        one, two = (first, second) if half == 0 else (second, first)
        got = jnp.where(swap, two[...], one[...])
        kept = jnp.where(straight, mine[here, :], got)
        share = kept.shape[1] // 3
        for pair in range(share // 128):
            for item in range(3):
                to = pair * 384 + item * 128
                at = item * share + pair * 128
                out[here, to : to + 128] = kept[:, at : at + 128]


def relay(scal, mine, first, second):
    return pl.pallas_call(
        relay_kernel,
        grid_spec=pltpu.PrefetchScalarGridSpec(
            num_scalar_prefetch=1,
            grid=(1,),
            in_specs=[held(mine.shape), held(first.shape), held(first.shape)],
            out_specs=held(mine.shape),
        ),
        out_shape=jax.ShapeDtypeStruct(mine.shape, BF16),
        compiler_params=params(1, 10),
        cost_estimate=cost(0, 0),
        name="relay",
    )(scal, mine, first, second)


def project_kernel(
    frames_here, scal, oth, own, gain, shift, weight, first, qkv, qfeat, kfeat, offset
):
    step = pl.program_id(0)
    half_blocks = pl.num_programs(0) // 2
    half_rows = half_blocks * BLK
    within = lax.rem(step, half_blocks) * BLK
    rows = pl.ds(pl.multiple_of(within, BLK), BLK)

    @pl.when(step == 0)
    def _():
        start = frames_here * FRAME_TOK // 16 * 16
        at = frames_here * FRAME_TOK + NOTE - start
        block = own[start : start + 32, :].astype(F32)
        note = block[at : at + 1, :] + block[at + 1 : at + 2, :] + block[at + 2 : at + 3, :]
        share = weight.shape[1] // 3
        offset[...] = jnp.zeros_like(offset)
        for pair in range(share // 128):
            here = pair * 128
            offset[:, 3 * here : 3 * here + 128] = note[:, here : here + 128]
            offset[:, 3 * here + 256 : 3 * here + 384] = note[:, share + here : share + here + 128]

    values = jnp.where(step < half_blocks, oth[rows, :], own[rows, :]).astype(F32)
    xhat, _ = centre(values)
    low = (xhat * gain[...] + shift[...]).astype(BF16)
    first[...] = low
    out = (nn(low, weight[...]) + offset[...]).astype(BF16)
    for pair in range(out.shape[1] // 384):
        at = pair * 384
        qkv[:, at : at + 128] = out[:, at : at + 128] * jnp.asarray(HEAD_DIM**-0.5, BF16)
        qkv[:, at + 128 : at + 384] = out[:, at + 128 : at + 384]
    core, count = scal[0], scal[2]
    half = jnp.where(step < half_blocks, 1 - core, core)
    edge = clip_edge(count, frames_here, half_rows)
    token = within + lax.broadcasted_iota(jnp.int32, (BLK, 128), 0)
    lane = lax.broadcasted_iota(jnp.int32, (BLK, 128), 1)
    clip = jnp.where(half * half_rows + token >= edge, 1, 0)
    clip = jnp.where(token >= frames_here * FRAME_TOK, 2, clip)
    hit = lane == clip
    qfeat[...] = jnp.where(hit, 1.0, 0.0).astype(BF16)
    kfeat[...] = jnp.where(hit, 0.0, jnp.where(lane < 3, -FAR, 0.0)).astype(BF16)


def clip_edge(count, frames_here, half_rows):
    return jnp.where(
        count < frames_here,
        count * FRAME_TOK,
        half_rows + (count - frames_here) * FRAME_TOK,
    )


def clip_span(block, edge, blocks):
    low = jnp.where(block * BLK >= edge, edge // BLK, 0)
    high = jnp.where(block * BLK + BLK - 1 < edge, (edge + BLK - 1) // BLK, blocks)
    return low, high


def project(scal, oth, own, gain, shift, weight, frames_here, half_rows):
    width, cols = weight.shape
    steps = 2 * half_rows // BLK
    rows = 2 * half_rows
    return pl.pallas_call(
        functools.partial(project_kernel, frames_here),
        grid_spec=pltpu.PrefetchScalarGridSpec(
            num_scalar_prefetch=1,
            grid=(steps,),
            in_specs=[
                whole(oth.shape),
                whole(own.shape),
                whole((1, width)),
                whole((1, width)),
                whole((width, cols)),
            ],
            out_specs=[
                pl.BlockSpec((BLK, width), lambda i, *_: (i, 0)),
                pl.BlockSpec((BLK, cols), lambda i, *_: (i, 0)),
                pl.BlockSpec((BLK, 128), lambda i, *_: (i, 0)),
                pl.BlockSpec((BLK, 128), lambda i, *_: (i, 0)),
            ],
            scratch_shapes=[pltpu.VMEM((1, cols), F32)],
        ),
        out_shape=[
            jax.ShapeDtypeStruct((rows, width), BF16),
            jax.ShapeDtypeStruct((rows, cols), BF16),
            jax.ShapeDtypeStruct((rows, 128), BF16),
            jax.ShapeDtypeStruct((rows, 128), BF16),
        ],
        compiler_params=params(1, 10),
        cost_estimate=cost(2 * rows * width * cols, 4 * rows * width + 2 * rows * cols),
        name="project",
    )(scal, oth, own, gain, shift, weight)


def attend_kernel(
    frames_here,
    bk,
    scal,
    q,
    qfeat,
    qkv,
    kfeat,
    mixed,
    wide,
    log_total,
    scores,
    tops,
    acc,
    keys_all,
    values_all,
):
    step = pl.program_id(0)
    half = pl.num_programs(0)
    blocks = 2 * half
    pairs = q.shape[1] // 384
    flip = half * (1 - scal[0])
    edge = clip_edge(scal[2], frames_here, half * BLK)
    low, high = clip_span((step + half * scal[3]) ^ flip, edge, blocks)
    per = bk // BLK
    low, high = low // per, (high + per - 1) // per
    kflip = flip // per
    lane = lax.broadcasted_iota(jnp.int32, (BLK, 128), 1)
    left = lane < HEAD_DIM
    none = jnp.zeros((BLK, 128), BF16)
    queries = []
    for pair in range(pairs):
        both = q[:, pair * 384 : pair * 384 + 128]
        queries.append(jnp.concatenate([jnp.where(left, both, none), qfeat[...]], axis=1))
        queries.append(jnp.concatenate([jnp.where(left, none, both), qfeat[...]], axis=1))
    @pl.when(step == 0)
    def _():
        def prepare(block, carry):
            rows = pl.ds(pl.multiple_of(block * BLK, BLK), BLK)
            for pair in range(pairs):
                at = pair * 384
                keys_all[pair, rows, :128] = qkv[rows, at + 128 : at + 256]
                keys_all[pair, rows, 128:] = kfeat[rows, :]
                both = qkv[rows, at + 256 : at + 384]
                values_all[2 * pair, rows, :128] = jnp.where(left, both, none)
                values_all[2 * pair, rows, 128:] = jnp.where(left, 1.0, 0.0).astype(BF16)
                values_all[2 * pair + 1, rows, :128] = jnp.where(left, none, both)
                values_all[2 * pair + 1, rows, 128:] = jnp.where(left, 0.0, 1.0).astype(BF16)
            return carry

        lax.fori_loop(0, blocks, prepare, 0)

    for head in range(2 * pairs):
        tops[head] = jnp.full((BLK, 128), -3e38, F32)

    def score(block, carry):
        rows = pl.ds(pl.multiple_of((block ^ kflip) * bk, bk), bk)
        for pair in range(pairs):
            keys = keys_all[pair, rows, :]
            for head in (2 * pair, 2 * pair + 1):
                values = nt(queries[head], keys)
                scores[head, block] = values
                top = tops[head]
                for part in range(bk // 128):
                    top = jnp.maximum(top, values[:, part * 128 : (part + 1) * 128])
                tops[head] = top
        return carry

    lax.fori_loop(low, high, score, 0)
    for head in range(2 * pairs):
        tops[head] = jnp.broadcast_to(jnp.max(tops[head], axis=1, keepdims=True), (BLK, 128))
    acc[...] = jnp.zeros_like(acc)
    def mix(block, carry):
        rows = pl.ds(pl.multiple_of((block ^ kflip) * bk, bk), bk)
        for pair in range(pairs):
            soft = []
            for head in (2 * pair, 2 * pair + 1):
                top = tops[head]
                for part in range(bk // 128):
                    piece = scores[head, block, :, part * 128 : (part + 1) * 128]
                    soft.append(jnp.exp(piece - top).astype(BF16))
            values = jnp.concatenate(
                [values_all[2 * pair, rows, :], values_all[2 * pair + 1, rows, :]], axis=0
            )
            acc[pair] += nn(jnp.concatenate(soft, axis=1), values)
        return carry

    lax.fori_loop(low, high, mix, 0)
    for pair in range(pairs):
        cols = slice(pair * 128, (pair + 1) * 128)
        totals = acc[pair, :, 128:]
        out = acc[pair, :, :128] / totals
        wide[:, cols] = out
        mixed[:, cols] = out.astype(BF16)
        logs = (jnp.where(left, tops[2 * pair], tops[2 * pair + 1]) + jnp.log(totals)).T
        log_total[pair, 0, 0:1] = logs[0:1]
        log_total[pair, 0, 1:2] = logs[HEAD_DIM : HEAD_DIM + 1]


def attend(scal, qkv, qfeat, kfeat, frames_here):
    rows, cols = qkv.shape
    width = cols // 3
    pairs = width // 128
    half = rows // BLK // 2
    bk = rows // 2
    return pl.pallas_call(
        functools.partial(attend_kernel, frames_here, bk),
        grid_spec=pltpu.PrefetchScalarGridSpec(
            num_scalar_prefetch=1,
            grid=(half,),
            in_specs=[
                pl.BlockSpec((BLK, cols), lambda i, scal: (i + half * scal[3], 0)),
                pl.BlockSpec((BLK, 128), lambda i, scal: (i + half * scal[3], 0)),
                whole((rows, cols)),
                whole((rows, 128)),
            ],
            out_specs=[
                pl.BlockSpec((BLK, width), lambda i, *_: (i, 0)),
                pl.BlockSpec((BLK, width), lambda i, *_: (i, 0)),
                pl.BlockSpec((pairs, 1, 8, BLK), lambda i, *_: (0, i, 0, 0)),
            ],
            scratch_shapes=[
                pltpu.VMEM((2 * pairs, rows // bk, BLK, bk), F32),
                pltpu.VMEM((2 * pairs, BLK, 128), F32),
                pltpu.VMEM((pairs, BLK, 256), F32),
                pltpu.VMEM((pairs, rows, 256), BF16),
                pltpu.VMEM((2 * pairs, rows, 256), BF16),
            ],
        ),
        out_shape=[
            jax.ShapeDtypeStruct((rows // 2, width), BF16),
            jax.ShapeDtypeStruct((rows // 2, width), F32),
            jax.ShapeDtypeStruct((pairs, half, 8, BLK), F32),
        ],
        compiler_params=params(1, 28),
        cost_estimate=cost(8 * rows * rows * width, 16 * rows * width),
        name="attend",
    )(scal, qkv, qfeat, qkv, kfeat)


def gather_out_weight(scal, own_out, got_up, more_up, out_weight, hid):
    core, plane = scal[0], scal[1]
    share = own_out.shape[0]
    quarter = share // 2
    out_weight[pl.ds(pl.multiple_of(plane * share, 64), share), :] = own_out[...]
    base = (1 - plane) * share
    out_weight[pl.ds(pl.multiple_of(base + core * quarter, 64), quarter), :] = got_up[
        hid : hid + quarter, :
    ]
    out_weight[pl.ds(pl.multiple_of(base + (1 - core) * quarter, 64), quarter), :] = more_up[
        hid : hid + quarter, :
    ]


def up_weight(core, own_up, got_up, more_up, chunk):
    hid = got_up.shape[1]
    if chunk < 2:
        return (more_up, got_up)[chunk][:hid, :]
    pick = (1 - core) if chunk == 2 else core
    return own_up[:, pl.ds(pl.multiple_of(pick * hid, 128), hid)]


def down_weight(core, own_down, got_down, more_down, chunk):
    hid = got_down.shape[1]
    if chunk < 2:
        return (more_down, got_down)[chunk][...]
    pick = (1 - core) if chunk == 2 else core
    return own_down[pl.ds(pl.multiple_of(pick * hid, 128), hid), :]


def ahead_kernel(
    frames_here,
    scal,
    mixed_own,
    mixed_oth,
    tokens,
    cot,
    own_out,
    own_up,
    own_down,
    got_up,
    got_down,
    more_up,
    more_down,
    up_offset,
    gains,
    shifts,
    out_offset,
    down_offset,
    learner,
    learner_offset,
    out_grad_out,
    xhat_out,
    scale_out,
    slope_out,
    second_out,
    out_low_out,
    sums,
    pooled,
    learner_sums,
    learner_offset_sums,
    theirs_out,
    mine_out,
    out_weight,
    hidden_kept,
    down_total,
):
    step = pl.program_id(0)
    core, plane = scal[0], scal[1]
    hid = got_up.shape[1]
    share = own_out.shape[0]

    @pl.when(step == 0)
    def _():
        gather_out_weight(scal, own_out, got_up, more_up, out_weight, hid)
        for ref in (sums, pooled, learner_sums, learner_offset_sums, down_total):
            ref[...] = jnp.zeros_like(ref)

    def up_bias(chunk):
        pick = (1 - core) if chunk % 2 == 0 else core
        if chunk >= 2:
            return up_offset[pl.ds(pick, 1), :]
        note = got_up[hid + share // 2 :, :].astype(F32)
        sums = [
            note[3 * i : 3 * i + 1] + note[3 * i + 1 : 3 * i + 2] + note[3 * i + 2 : 3 * i + 3]
            for i in range(2)
        ]
        return jnp.where(pick == 0, sums[0], sums[1])

    mine = pl.ds(pl.multiple_of(core * share, 64), share)
    theirs = pl.ds(pl.multiple_of((1 - core) * share, 64), share)
    attended = nn(mixed_own[...], out_weight[mine, :]) + nn(mixed_oth[...], out_weight[theirs, :])
    residual = tokens[...].astype(F32) + attended + out_offset[...]
    xhat_two, scale_two = centre(residual)
    xhat_out[...] = xhat_two
    scale_out[...] = jnp.broadcast_to(scale_two, scale_out.shape)
    second = (xhat_two * gains[1:2, :] + shifts[1:2, :]).astype(BF16)
    second_out[...] = second
    block_out = residual + down_offset[...]
    for chunk in range(4):
        cols = slice(chunk * hid, (chunk + 1) * hid)
        pre = nn(second, up_weight(core, own_up, got_up, more_up, chunk)) + up_bias(chunk)
        square = pre * pre
        gate = 0.5 + 0.5 * jnp.tanh(pre * (GELU_C + (GELU_A * GELU_C) * square))
        product = pre * gate
        hidden = product.astype(BF16)
        bend = (1.0 - gate) * (2.0 * GELU_C + (6.0 * GELU_A * GELU_C) * square)
        slope_out[:, cols] = (gate + product * bend).astype(BF16)
        hidden_kept[:, cols] = hidden
        block_out = block_out + nn(hidden, down_weight(core, own_down, got_down, more_down, chunk))
    xhat_three, scale_three = centre(block_out)
    third = (xhat_three * gains[2:3, :] + shifts[2:3, :]).astype(BF16)
    logits = nt(third, learner[...]) + learner_offset[...]
    sig = 1.0 / (1.0 + jnp.exp(-logits))
    token = step * BLK + lax.broadcasted_iota(jnp.int32, (BLK, 128), 0)
    first_token = (lax.broadcasted_iota(jnp.int32, (BLK, 128), 1) >> 3) * FRAME_TOK
    inside = (token >= first_token) & (token < first_token + FRAME_TOK)
    inside = inside & (first_token < frames_here * FRAME_TOK)
    maps = jnp.where(inside, sig, 0.0).astype(BF16)
    feature = block_out.astype(BF16)
    pooled[...] += tn(maps, feature)
    maps_grad = nt(feature, cot[...])
    pool_grad = nn(maps, cot[...])
    logits_grad = jnp.where(inside, maps_grad * sig * (1.0 - sig), 0.0).astype(BF16)
    learner_sums[...] += tn(logits_grad, third)
    learner_offset_sums[...] += fold8(logits_grad.astype(F32))
    third_grad = nn(logits_grad, learner[...])
    sums[0:8, :] += fold8(third_grad * xhat_three)
    sums[8:16, :] += fold8(third_grad)
    out_grad = pool_grad + norm_back(xhat_three, scale_three, gains[2:3, :], third_grad)
    sums[16:24, :] += fold8(out_grad)
    out_grad_out[...] = out_grad
    out_low = out_grad.astype(BF16)
    out_low_out[...] = out_low
    for chunk in range(4):
        down_total[chunk] += tn(hidden_kept[:, chunk * hid : (chunk + 1) * hid], out_low)

    @pl.when(step == pl.num_programs(0) - 1)
    def _():
        for n in range(2):
            theirs_out[n] = down_total[2 * n].astype(BF16)
            mine_out[n] = down_total[2 * n + 1].astype(BF16)


def behind_kernel(
    pooled_rows,
    scal,
    out_grad,
    out_low,
    xhat_two,
    scale_two,
    slope,
    second,
    mixed_own,
    mixed_oth,
    own_out,
    own_up,
    own_down,
    got_up,
    got_down,
    more_up,
    more_down,
    gains,
    pooled,
    residual_grad_out,
    grad_own,
    grad_oth,
    sums,
    up_sums,
    theirs_out,
    mine_out,
    out_weight,
    up_total,
    out_total,
):
    core, plane = scal[0], scal[1]
    hid = got_up.shape[1]
    share = own_out.shape[0]

    @pl.when(pl.program_id(0) == 0)
    def _():
        gather_out_weight(scal, own_out, got_up, more_up, out_weight, hid)
        for ref in (sums, up_sums, up_total, out_total):
            ref[...] = jnp.zeros_like(ref)

    mine = pl.ds(pl.multiple_of(core * share, 64), share)
    theirs = pl.ds(pl.multiple_of((1 - core) * share, 64), share)
    low = out_low[...]
    second_turned = second[...].T
    second_grad = None
    for chunk in range(4):
        cols = slice(chunk * hid, (chunk + 1) * hid)
        hidden_grad = nt(low, down_weight(core, own_down, got_down, more_down, chunk))
        pre_grad = (hidden_grad * slope[:, cols].astype(F32)).astype(BF16)
        up_total[chunk] += nn(second_turned, pre_grad)
        up_sums[:, cols] += fold8(pre_grad.astype(F32))
        term = nt(pre_grad, up_weight(core, own_up, got_up, more_up, chunk))
        second_grad = term if second_grad is None else second_grad + term
    xhat = xhat_two[...]
    sums[0:8, :] += fold8(second_grad * xhat)
    sums[8:16, :] += fold8(second_grad)
    residual_grad = out_grad[...] + norm_back(
        xhat, scale_two[:, :1], gains[1:2, :], second_grad
    )
    sums[16:24, :] += fold8(residual_grad)
    residual_grad_out[...] = residual_grad

    @pl.when(pl.program_id(0) == pl.num_programs(0) - 1)
    def _():
        residual_grad_out[BLK - pooled_rows :, :] = pooled[:pooled_rows, :]

    residual_low = residual_grad.astype(BF16)
    grad_own[...] = nt(residual_low, out_weight[mine, :]).astype(BF16)
    grad_oth[...] = nt(residual_low, out_weight[theirs, :]).astype(BF16)
    out_total[0] += tn(mixed_own[...], residual_low)
    out_total[1] += tn(mixed_oth[...], residual_low)

    @pl.when(pl.program_id(0) == pl.num_programs(0) - 1)
    def _():
        width = second.shape[1]
        half = width // 2
        for odd, (out, column) in enumerate(((theirs_out, 1 - core), (mine_out, core))):
            for n in range(2):
                out[n, :width, :] = up_total[2 * n + odd].astype(BF16)
                side = (1 - plane) if n == 0 else plane
                at = pl.ds(pl.multiple_of(column * half, 128), half)
                grad = out_total[jnp.where(side == core, 0, 1), :, at].astype(BF16)
                out[n, width:, :half] = grad[: share // 2]
                out[n, width:, half:] = grad[share // 2 :]


def row_block(cols):
    return pl.BlockSpec((BLK, cols), lambda i, *_: (i, 0))


def held(shape):
    return pl.BlockSpec(shape, lambda *_: (0,) * len(shape))


def row_call(kernel, name, scal, rowed, wholes, row_outs, held_outs, scratch, flops, mib, low_outs=()):
    rows = rowed[0].shape[0]
    nbytes = sum(x.size * x.dtype.itemsize for x in wholes)
    nbytes += rows * sum(c * (2 if t == BF16 else 4) for c, t in row_outs)
    return pl.pallas_call(
        kernel,
        grid_spec=pltpu.PrefetchScalarGridSpec(
            num_scalar_prefetch=1,
            grid=(rows // BLK,),
            in_specs=[row_block(x.shape[1]) for x in rowed] + [whole(x.shape) for x in wholes],
            out_specs=[row_block(cols) for cols, _ in row_outs]
            + [held(s) for s in held_outs]
            + [whole(s) for s in low_outs],
            scratch_shapes=scratch,
        ),
        out_shape=[jax.ShapeDtypeStruct((rows, cols), t) for cols, t in row_outs]
        + [jax.ShapeDtypeStruct(s, F32) for s in held_outs]
        + [jax.ShapeDtypeStruct(s, BF16) for s in low_outs],
        compiler_params=params(1, mib),
        cost_estimate=cost(flops, nbytes),
        name=name,
    )(scal, *rowed, *wholes)


def ahead(scal, mixed_own, mixed_oth, packed, cot, weights, up_offset, small, frames_here):
    rows, share = mixed_own.shape
    width = packed.shape[1]
    hidden = 2 * up_offset.size
    return row_call(
        functools.partial(ahead_kernel, frames_here),
        "ahead",
        scal,
        [mixed_own, mixed_oth, packed],
        [cot, *weights, up_offset, *small],
        [
            (width, F32),
            (width, F32),
            (128, F32),
            (hidden, BF16),
            (width, BF16),
            (width, BF16),
        ],
        [(24, width), (128, width), (128, width), (8, 128)],
        [
            pltpu.VMEM((2 * share, width), BF16),
            pltpu.VMEM((BLK, hidden), BF16),
            pltpu.VMEM((4, hidden // 4, width), F32),
        ],
        2 * rows * width * (3 * hidden + width),
        42,
        [(2, hidden // 4, width)] * 2,
    )


def behind(scal, rowed, weights, gains, pooled, maps_all):
    rows, width = rowed[0].shape
    share = weights[0].shape[0]
    hidden = rowed[4].shape[1]
    hid = hidden // 4
    return row_call(
        functools.partial(behind_kernel, maps_all),
        "behind",
        scal,
        rowed,
        [*weights, gains, pooled],
        [(width, F32), (share, BF16), (share, BF16)],
        [(24, width), (8, hidden)],
        [
            pltpu.VMEM((2 * share, width), BF16),
            pltpu.VMEM((4, width, hid), F32),
            pltpu.VMEM((2, share, width), F32),
        ],
        2 * rows * width * (3 * hidden + 2 * width),
        44,
        [(2, width + share // 2, hid)] * 2,
    )


def attend_back_kernel(
    frames_here,
    scal,
    k,
    v,
    kfeat,
    q,
    qfeat,
    grad_oth,
    grad_own,
    wide_oth,
    wide_own,
    log_oth,
    log_own,
    out_oth,
    out_own,
    queries,
    grads,
    inner,
    logs,
    dq,
    dkv,
):
    step = pl.program_id(0)
    half = grad_oth.shape[0] // BLK
    blocks = 2 * half
    flip = half * (1 - scal[0])
    edge = clip_edge(scal[2], frames_here, half * BLK)
    low, high = clip_span(step ^ flip, edge, blocks)
    bq = half * BLK
    low, high = low // half, (high + half - 1) // half
    qflip = 1 - scal[0]
    lane = lax.broadcasted_iota(jnp.int32, (BLK, 128), 1)
    left = lane < HEAD_DIM
    none = jnp.zeros((BLK, 128), BF16)

    @pl.when(step == 0)
    def _():
        dq[...] = jnp.zeros_like(dq)
        for side, (grad, wide, log_total) in enumerate(
            ((grad_oth, wide_oth, log_oth), (grad_own, wide_own, log_own))
        ):
            for block in range(bq // BLK):
                here = slice(block * BLK, (block + 1) * BLK)
                rows = slice(side * bq + block * BLK, side * bq + (block + 1) * BLK)
                grads[rows, :] = grad[here, :]
                queries[rows, :128] = q[rows, :]
                queries[rows, 128:] = qfeat[rows, :]
                product = (grad[here, :].astype(F32) * wide[here, :]).T
                inner[side, 0:1, here] = jnp.sum(product[:HEAD_DIM], axis=0, keepdims=True)
                inner[side, 1:2, here] = jnp.sum(product[HEAD_DIM:], axis=0, keepdims=True)
                logs[side, :, here] = log_total[0, block]

    ka = jnp.where(left, k[...], none)
    kb = jnp.where(left, none, k[...])
    key_a = jnp.concatenate([ka, kfeat[...]], axis=1)
    key_b = jnp.concatenate([kb, kfeat[...]], axis=1)
    keys = jnp.concatenate([ka, kb], axis=0)
    va = jnp.where(left, v[...], none)
    vb = jnp.where(left, none, v[...])
    dkv[...] = jnp.zeros_like(dkv)

    def pair(block, carry):
        local = block ^ qflip
        rows = pl.ds(pl.multiple_of(local * bq, bq), bq)
        query = queries[rows, :]
        grad = grads[rows, :]
        soft_a = jnp.exp(nt(key_a, query) - logs[local, 0:1])
        soft_b = jnp.exp(nt(key_b, query) - logs[local, 1:2])
        score_a = (soft_a * (nt(va, grad) - inner[local, 0:1])).astype(BF16)
        score_b = (soft_b * (nt(vb, grad) - inner[local, 1:2])).astype(BF16)
        dkv[0] += nn(soft_a.astype(BF16), grad)
        dkv[1] += nn(soft_b.astype(BF16), grad)
        dkv[2] += nn(score_a, query[:, :128])
        dkv[3] += nn(score_b, query[:, :128])
        dq[rows, :] += tn(jnp.concatenate([score_a, score_b], axis=0), keys)
        return carry

    lax.fori_loop(low, high, pair, 0)
    dk = jnp.where(left, dkv[2], dkv[3]).astype(BF16)
    dv = jnp.where(left, dkv[0], dkv[1]).astype(BF16)
    within = pl.ds(pl.multiple_of(lax.rem(step, half) * BLK, BLK), BLK)

    @pl.when(step < half)
    def _():
        out_oth[within, 128:256] = dk
        out_oth[within, 256:] = dv

    @pl.when(step >= half)
    def _():
        out_own[within, 128:256] = dk
        out_own[within, 256:] = dv

    @pl.when(step == blocks - 1)
    def _():
        half_rows = out_oth.shape[0]
        out_oth[:, :128] = (dq[:half_rows, :] * HEAD_DIM**-0.5).astype(BF16)
        out_own[:, :128] = (dq[half_rows:, :] * HEAD_DIM**-0.5).astype(BF16)

def attend_back(scal, qkv, qfeat, kfeat, grad_oth, grad_own, wide, logs, frames_here):
    rows = qkv.shape[0]
    blocks = rows // BLK
    one = pl.Buffered(1)
    half_rows = pl.BlockSpec((rows // 2, 128), lambda j, scal: (0, scal[3]), pipeline_mode=one)
    half_logs = pl.BlockSpec(
        (1, blocks // 2, 8, BLK), lambda j, scal: (scal[3], 0, 0, 0), pipeline_mode=one
    )
    return pl.pallas_call(
        functools.partial(attend_back_kernel, frames_here),
        grid_spec=pltpu.PrefetchScalarGridSpec(
            num_scalar_prefetch=1,
            grid=(blocks,),
            in_specs=[
                pl.BlockSpec((BLK, 128), lambda j, scal: (j, 3 * scal[3] + 1)),
                pl.BlockSpec((BLK, 128), lambda j, scal: (j, 3 * scal[3] + 2)),
                pl.BlockSpec((BLK, 128), lambda j, *_: (j, 0)),
                pl.BlockSpec((rows, 128), lambda j, scal: (0, 3 * scal[3]), pipeline_mode=one),
                whole((rows, 128)),
                half_rows,
                half_rows,
                half_rows,
                half_rows,
                half_logs,
                half_logs,
            ],
            out_specs=[pl.BlockSpec((rows // 2, 384), lambda j, *_: (0, 0))] * 2,
            scratch_shapes=[
                pltpu.VMEM((rows, 256), BF16),
                pltpu.VMEM((rows, 128), BF16),
                pltpu.VMEM((2, 8, rows // 2), F32),
                pltpu.VMEM((2, 8, rows // 2), F32),
                pltpu.VMEM((rows, 128), F32),
                pltpu.VMEM((4, BLK, 128), F32),
            ],
        ),
        out_shape=[jax.ShapeDtypeStruct((rows // 2, 384), BF16)] * 2,
        compiler_params=params(1, 14),
        cost_estimate=cost(40 * rows * rows * 128, 30 * rows * 128),
        name="attend_back",
    )(scal, qkv, qkv, kfeat, qkv, qfeat, grad_oth, grad_own, *wide, *logs)


def project_grad_kernel(pairs, more, scal, first, *refs):
    oth, own = refs[:pairs], refs[pairs : 2 * pairs]
    refs = refs[2 * pairs :]
    if more:
        got, weight_mine, weight_theirs = refs[:pairs], refs[pairs], refs[pairs + 1]
        theirs, mine, offsets, part = refs[pairs + 2 :]
    else:
        theirs, mine, offsets = refs
    step = pl.program_id(0)
    half = oth[0].shape[0]
    one = jnp.concatenate([x[...] for x in oth], axis=1)
    two = jnp.concatenate([x[...] for x in own], axis=1)
    out = (tn(first[:half, :], one) + tn(first[half:, :], two)).astype(BF16)

    @pl.when(step == 0)
    def _():
        theirs[...] = out
        offsets[...] = fold8(one.astype(F32)) + fold8(two.astype(F32))

    @pl.when(step == 1)
    def _():
        mine[...] = out

    if more:
        lines = half // 2
        rows = pl.ds(pl.multiple_of(step * lines, BLK), lines)
        total = nt(jnp.concatenate([x[rows, :] for x in own], axis=1), weight_mine[...])
        part[...] = total + nt(
            jnp.concatenate([x[rows, :] for x in got], axis=1), weight_theirs[...]
        )


def project_grad(scal, first, oth, own, *more):
    pairs = len(oth)
    rows, width = first.shape
    cols = 384 * pairs
    got, weights = (more[0], more[1:]) if more else ((), ())
    weight = pl.BlockSpec((width, cols), lambda *_: (0, 0), pipeline_mode=pl.Buffered(1))
    shapes = [
        jax.ShapeDtypeStruct((width // 2, cols), BF16),
        jax.ShapeDtypeStruct((width // 2, cols), BF16),
        jax.ShapeDtypeStruct((8, cols), F32),
    ]
    specs = [held((width // 2, cols)), held((width // 2, cols)), held((8, cols))]
    if more:
        shapes.append(jax.ShapeDtypeStruct((rows // 2, width), F32))
        specs.append(pl.BlockSpec((rows // 4, width), lambda n, *_: (n, 0)))
    return pl.pallas_call(
        functools.partial(project_grad_kernel, pairs, bool(more)),
        grid_spec=pltpu.PrefetchScalarGridSpec(
            num_scalar_prefetch=1,
            grid=(2,),
            in_specs=[
                pl.BlockSpec((rows, width // 2), lambda n, scal: (0, (1 - scal[0]) ^ n)),
            ]
            + [whole((rows // 2, 384))] * (2 * pairs + len(got))
            + [weight] * len(weights),
            out_specs=specs,
        ),
        out_shape=shapes,
        compiler_params=params(1, 24),
        cost_estimate=cost(2 * rows * width * cols, 2 * rows * (width + cols)),
        name="project_grad",
    )(scal, first, *oth, *own, *got, *weights)


def first_grad_kernel(own, got, mine, theirs, part, tokens, out, sums):
    total = part[...] + nt(own[...], mine[...]) + nt(got[...], theirs[...])
    out[...] = total.astype(BF16)

    @pl.when(pl.program_id(0) == 0)
    def _():
        sums[...] = jnp.zeros_like(sums)

    xhat, _ = centre(tokens[...].astype(F32))
    sums[0:8, :] += fold8(total * xhat)
    sums[8:16, :] += fold8(total)


def first_grad(own, got, mine, theirs, part, packed):
    rows, cols = own.shape
    width = mine.shape[0]
    last_pair = mine.shape[1] // cols - 1
    weight = pl.BlockSpec(
        (width, cols), lambda *_: (0, last_pair), pipeline_mode=pl.Buffered(1)
    )
    row = pl.BlockSpec((BLK, width), lambda i: (i, 0))
    return pl.pallas_call(
        first_grad_kernel,
        grid=(rows // BLK,),
        in_specs=[pl.BlockSpec((BLK, cols), lambda i: (i, 0))] * 2 + [weight] * 2 + [row] * 2,
        out_specs=[row, pl.BlockSpec((16, width), lambda i: (0, 0))],
        out_shape=[
            jax.ShapeDtypeStruct((rows, width), BF16),
            jax.ShapeDtypeStruct((16, width), F32),
        ],
        compiler_params=params(1, 16),
        cost_estimate=cost(4 * rows * width * cols, 12 * rows * width),
        name="first_grad",
    )(own, got, mine, theirs, part, packed)


def last_kernel(scal, tokens, grad, grad_got, residual, residual_got, gain, out):
    xhat, scale = centre(tokens[...].astype(F32))
    straight = scal[0] == scal[1]
    wide = jnp.where(straight, grad[...], grad_got[...]).astype(F32)
    base = jnp.where(straight, residual[...], residual_got[...])
    out[...] = base + norm_back(xhat, scale, gain[...], wide)


def last(scal, packed, grad, grad_got, residual, residual_got, gain, tokens_here):
    rows, width = grad.shape
    return pl.pallas_call(
        last_kernel,
        grid_spec=pltpu.PrefetchScalarGridSpec(
            num_scalar_prefetch=1,
            grid=(rows // BLK,),
            in_specs=[row_block(width)] * 5 + [whole((1, width))],
            out_specs=row_block(width),
        ),
        out_shape=jax.ShapeDtypeStruct((tokens_here, width), F32),
        compiler_params=params(1, 12),
        cost_estimate=cost(20 * rows * width, 12 * rows * width),
        name="last",
    )(scal, packed, grad, grad_got, residual, residual_got, gain)


def table_kernel(
    frames_here, scal, ahead_sums, behind_sums, first_sums, learner, learner_offset, up, *refs
):
    offsets, out = refs[:-1], refs[-1]
    core, plane = scal[0], scal[1]
    width = out.shape[1]
    hid = up.shape[1] // 4

    def total(ref, at):
        return jnp.sum(ref[at : at + 8, :], axis=0, keepdims=True)

    out[...] = jnp.zeros_like(out)
    for row, (ref, at) in enumerate(
        (
            (first_sums, 0),
            (behind_sums, 0),
            (ahead_sums, 0),
            (first_sums, 8),
            (behind_sums, 8),
            (ahead_sums, 8),
            (behind_sums, 16),
            (ahead_sums, 16),
        )
    ):
        out[row : row + 1, :] = total(ref, at)
    out[8:16, :] = sum(learner[MAPS * i : MAPS * (i + 1), :] for i in range(frames_here))
    row = total(learner_offset, 0)
    lane = lax.broadcasted_iota(jnp.int32, (1, 128), 1)
    kept = row
    for i in range(1, frames_here):
        kept = kept + pltpu.roll(row, 128 - MAPS * i, 1)
    out[16:17, :128] = jnp.where(lane < MAPS, kept, 0.0)
    for chunk in range(4):
        side = (1 - plane) if chunk < 2 else plane
        pick = (1 - core) if chunk % 2 == 0 else core
        out[pl.ds(17 + 2 * side + pick, 1), :] = jnp.sum(
            up[:, chunk * hid : (chunk + 1) * hid], axis=0, keepdims=True
        )
    pair = 0
    for ref in offsets:
        for at in range(0, ref.shape[1], 384):
            to = pl.ds(pl.multiple_of(core * (width // 2) + pair * 128, 128), 128)
            out[21:22, to] = jnp.sum(ref[:, at : at + 128], axis=0, keepdims=True)
            out[22:23, to] = jnp.sum(ref[:, at + 256 : at + 384], axis=0, keepdims=True)
            pair += 1


def small_table(scal, frames_here, *parts):
    width = parts[0].shape[1]
    return pl.pallas_call(
        functools.partial(table_kernel, frames_here),
        grid_spec=pltpu.PrefetchScalarGridSpec(
            num_scalar_prefetch=1,
            grid=(1,),
            in_specs=[held(x.shape) for x in parts],
            out_specs=held((24, width)),
        ),
        out_shape=jax.ShapeDtypeStruct((24, width), F32),
        compiler_params=pltpu.CompilerParams(vmem_limit_bytes=6 * 1024 * 1024),
        cost_estimate=cost(0, 1 << 20),
        name="small_table",
    )(scal, *parts)


def body(
    tokens,
    frame_counts,
    norm_gains,
    norm_shifts,
    attend_weight,
    attend_offset,
    output_weight,
    output_offset,
    expand_weight,
    expand_offset,
    contract_weight,
    contract_offset,
    learner_weight,
    learner_offset,
    pooled_cotangent,
):
    tokens_here, width = tokens.shape
    frames_here = tokens_here // FRAME_TOK
    half_rows = -(-tokens_here // BLK) * BLK
    share = attend_weight.shape[2]
    hid = contract_weight.shape[0] // 2
    chips = lax.axis_size("chip")
    core, plane = lax.axis_index("core"), lax.axis_index("mp")
    straight = core == plane
    flip2 = [(0, 1), (1, 0)]

    def turn(x):
        return lax.ppermute(x, ("core", "mp"), [(1, 2), (2, 1)])

    def to_core(x):
        return lax.ppermute(x, "core", flip2)

    def to_plane(x):
        return lax.ppermute(x, "mp", flip2)

    chip = lax.axis_index("chip")
    side = chip % 2
    hops = []
    while (2 << len(hops)) < chips:
        hops.append(2 << len(hops))

    def hop(x, step):
        return lax.ppermute(x, "chip", [(i, i ^ step) for i in range(chips)])

    def low(x):
        return x.astype(BF16)

    def plus(a, b):
        return a.astype(F32) + b.astype(F32)

    def pick(x, index):
        return lax.dynamic_index_in_dim(x, index, 0, keepdims=False)

    def halves_of(x):
        rows = x.shape[-2] // 2
        return x.reshape(*x.shape[:-2], 2, rows, x.shape[-1])

    def join(x, other, index, axis):
        return jnp.concatenate(
            [jnp.where(index == 0, x, other), jnp.where(index == 0, other, x)], axis=axis
        )

    pairs = share // 128

    weight_mine = attend_weight.reshape(width, 3 * share)
    weight_part = lax.dynamic_slice_in_dim(attend_weight, side * (width // 2), width // 2, 0)
    weight_part = weight_part.reshape(width // 2, 3 * share)
    weight_got = turn(weight_part)
    packed = pack(
        after(tokens, weight_part),
        pooled_cotangent.reshape(frames_here * MAPS, width),
        attend_offset.reshape(1, 2 * share),
        frame_counts[:, :1].astype(F32),
        half_rows,
    )
    got_packed = turn(packed)
    weight_rest = lax.ppermute(
        weight_got,
        ("chip", "core", "mp"),
        [(4 * i + j, 4 * (i ^ 1) + j) for i in range(chips) for j in (1, 2)],
    )
    weight_here = relay(
        jnp.stack([core, plane, side]).astype(jnp.int32), weight_mine, weight_got, weight_rest
    )
    left, notes = expand_offset.reshape(2, hid), []
    for _ in range(3):
        notes.append(lax.reduce_precision(left, 8, 7))
        left = left - notes[-1]
    notes = jnp.stack(notes, axis=1).reshape(6, hid)
    up_quarter = jnp.concatenate(
        [
            lax.dynamic_slice_in_dim(expand_weight, core * hid, hid, 1),
            lax.dynamic_slice_in_dim(output_weight, core * (share // 2), share // 2, 0),
            jnp.pad(notes, ((0, 10), (0, 0))).astype(BF16),
        ],
        axis=0,
    )
    down_quarter = lax.dynamic_slice_in_dim(contract_weight, core * hid, hid, 0)
    own = jnp.where(
        straight, packed, after(got_packed, weight_here, up_quarter, down_quarter)
    )
    oth = to_core(own)
    count = own[tokens_here + NOTE + 3, 0].astype(jnp.int32)
    numbered = [
        jnp.stack([core.astype(jnp.int32), plane.astype(jnp.int32), count, jnp.int32(i)])
        for i in range(pairs)
    ]
    scal = numbered[0]

    up_got_a = to_plane(after(up_quarter, own, weight_here))
    down_got_a = to_plane(after(down_quarter, oth))

    first, qkv, qfeat, kfeat = project(
        scal,
        oth,
        own,
        norm_gains[0:1],
        norm_shifts[0:1],
        weight_here,
        frames_here,
        half_rows,
    )
    weight_there = to_core(after(weight_here, qkv))
    mixed_send, wide_oth, logs_oth = attend(numbered[0], qkv, qfeat, kfeat, frames_here)
    mixed_oth = to_core(mixed_send)
    up_got_b = to_core(after(up_got_a, mixed_send))
    mixed_own, wide_own, logs_own = attend(
        after(numbered[1], mixed_send, weight_there), qkv, qfeat, kfeat, frames_here
    )
    down_got_b = to_core(after(down_got_a, mixed_own))

    maps_all = frames_here * MAPS
    cot = jnp.pad(own[half_rows:], ((0, 128 - maps_all), (0, 0)))
    learner = jnp.pad(jnp.tile(learner_weight.T, (frames_here, 1)), ((0, 128 - maps_all), (0, 0)))
    learner_bias = jnp.pad(jnp.tile(learner_offset, frames_here), (0, 128 - maps_all))[None]
    weights = (
        *(
            pltpu.with_memory_space_constraint(x, pltpu.HBM)
            for x in (output_weight, expand_weight, contract_weight)
        ),
        up_got_a,
        down_got_a,
        up_got_b,
        down_got_b,
    )
    (
        out_grad,
        xhat_two,
        scale_two,
        slope,
        second,
        out_low,
        sums_ahead,
        pooled,
        learner_sums,
        learner_offset_sums,
        down_theirs,
        down_mine,
    ) = ahead(
        scal,
        mixed_own,
        mixed_oth,
        own,
        cot,
        weights,
        expand_offset.reshape(2, hid),
        (
            norm_gains,
            norm_shifts,
            output_offset[None],
            contract_offset[None],
            learner,
            learner_bias,
        ),
        frames_here,
    )

    down_got = to_core(down_theirs)
    down_send = low(plus(down_got[0], down_mine[0]))
    down_keep = plus(down_got[1], down_mine[1])
    down_plane = to_plane(down_send)

    (
        residual_grad,
        grad_own,
        grad_send,
        sums_behind,
        up_sums,
        up_theirs,
        up_mine,
    ) = behind(
        after(scal, down_send),
        [out_grad, out_low, xhat_two, scale_two, slope, second, mixed_own, mixed_oth],
        weights,
        norm_gains,
        pooled,
        maps_all,
    )
    down_half = halves_of(plus(down_keep, after(down_plane, residual_grad)))
    down_x_send = low(pick(down_half, 1 - side))
    down_x_keep = pick(down_half, side)
    down_x = hop(down_x_send, 1)
    up_got = to_core(after(up_theirs, down_x_send))
    grad_oth = to_core(after(grad_send, down_x_send))
    up_half = halves_of(plus(up_got, after(up_mine, down_x_send)))
    up_x_send = low(lax.dynamic_index_in_dim(up_half, 1 - side, 1, keepdims=False))
    up_x_keep = lax.dynamic_index_in_dim(up_half, side, 1, keepdims=False)
    up_x = hop(up_x_send, 1)

    def back(pair, *gate):
        return attend_back(
            after(numbered[pair], *gate),
            qkv,
            qfeat,
            kfeat,
            grad_oth,
            grad_own,
            (wide_oth, wide_own),
            (logs_oth, logs_own),
            frames_here,
        )

    def project_fold(their, mine):
        got = to_core(their)
        return jnp.where(straight, got, mine), jnp.where(straight, mine, got)

    bit = (chip // 2) % 2

    def split(x):
        parts = halves_of(x)
        return low(pick(parts, 1 - bit)), pick(parts, bit)

    residual_got = turn(after(residual_grad, up_x_send))
    down_send, down_keep = split(plus(down_x_keep, after(down_x, up_x_send)))
    down_z = hop(down_send, hops[0])
    oth_0, own_0 = back(0, down_send)
    got_0 = to_core(oth_0)
    down_sum = plus(down_keep, after(down_z, oth_0))
    down_low = low(down_sum)
    down_z = hop(down_low, hops[1])
    up_y = plus(up_x_keep, after(up_x, oth_0))
    up_y_send = low(up_y[0])
    up_y_got = to_plane(up_y_send)

    residual_got = after(residual_got, oth_0)
    oth_1, own_1 = back(1, down_low, up_y_send, residual_got, got_0)
    got_1 = to_core(oth_1)

    def rest(total, got, steps):
        total = plus(total, got)
        for step in steps:
            total = plus(total, hop(low(total), step))
        return low(total)

    down_sum = rest(down_sum, after(down_z, oth_1), hops[2:])
    down_z = hop(down_sum, hops[0])
    up_send, up_keep = split(plus(up_y[1], after(up_y_got, oth_1)))
    up_z = hop(up_send, hops[0])
    their_0, mine_0, offsets_0, part = project_grad(
        after(scal, down_sum, up_send),
        first,
        (oth_0, oth_1),
        (own_0, own_1),
        (got_0, got_1),
        weight_here,
        weight_there,
    )
    early_send, early_keep = project_fold(their_0, mine_0)
    early_got = to_plane(early_send)
    up_sum = plus(up_keep, after(up_z, part))
    up_low = low(up_sum)
    up_z = hop(up_low, hops[1])

    down_sum = join(down_sum, after(down_z, part), bit, 0)
    down_x = hop(down_sum, 1)

    oth_2, own_2 = back(2, early_send, up_low, down_sum, got_1)
    got_2 = to_core(oth_2)
    up_sum = rest(up_sum, after(up_z, oth_2), hops[2:])
    up_z = hop(up_sum, hops[0])
    early_half = halves_of(plus(early_keep, after(early_got, oth_2)))
    early_send = low(pick(early_half, 1 - side))
    early_keep = pick(early_half, side)
    early_x = hop(early_send, 1)
    their_2, mine_2, offsets_2 = project_grad(
        after(scal, up_sum, early_send), first, (oth_2,), (own_2,)
    )
    late_send, late_keep = project_fold(their_2, mine_2)
    late_got = to_plane(late_send)
    up_sum = join(up_sum, after(up_z, mine_2), bit, 0)
    down_sum = join(down_sum, after(down_x, mine_2), side, 0)
    down_got = to_core(down_sum)
    early_sum = plus(early_keep, after(early_x, mine_2))
    early_low = low(early_sum)
    early_z = hop(early_low, hops[0])
    first_low, first_sums = first_grad(
        own_2,
        got_2,
        weight_here,
        weight_there,
        part,
        after(own, late_send, up_sum, early_low),
    )
    first_got = turn(first_low)
    table = small_table(
        scal,
        frames_here,
        sums_ahead,
        sums_behind,
        first_sums,
        learner_sums,
        learner_offset_sums,
        up_sums,
        offsets_0,
        offsets_2,
    )

    early_sum = plus(early_sum, after(early_z, table))
    early_low = low(early_sum)
    early_z = hop(early_low, hops[1])
    late_half = halves_of(plus(late_keep, after(late_got, early_low)))
    late_send = low(pick(late_half, 1 - side))
    late_keep = pick(late_half, side)
    late_x = hop(late_send, 1)
    table = table + after(to_core(table), late_send)
    table_got = to_plane(table)
    up_x = hop(after(up_sum, table), 1)
    late_sum = plus(late_keep, after(late_x, table))
    late_low = low(late_sum)
    late_z = hop(late_low, hops[0])
    table = table + after(table_got, late_low)
    late_sum = plus(late_sum, after(late_z, table))
    late_low = low(late_sum)
    late_z = hop(late_low, hops[1])
    table_got = hop(after(table, late_low), hops[0])
    early_sum = rest(early_sum, after(early_z, late_low), hops[2:])
    early_x = hop(early_sum, 1)
    table = table + after(table_got, early_sum)
    table_got = hop(table, hops[1])
    up_sum = join(up_sum, after(up_x, table), side, 0)
    up_got = to_core(up_sum)
    late_sum = rest(late_sum, after(late_z, up_sum), hops[2:])
    late_x = hop(late_sum, 1)
    table = table + after(table_got, late_sum)
    for step in hops[2:]:
        table = table + hop(table, step)
    table_got = hop(table, 1)
    tokens_gradient = last(
        after(scal, table),
        packed,
        first_low,
        first_got,
        residual_grad,
        residual_got,
        norm_gains[0:1],
        tokens_here,
    )
    table = table + after(table_got, tokens_gradient)
    early_sum = join(early_sum, after(early_x, tokens_gradient), side, 0)
    early_got = to_core(early_sum)
    late_sum = join(late_sum, after(late_x, early_sum), side, 0)
    late_got = to_core(late_sum)

    def two(x, other):
        return jnp.where(core == 0, x, other), jnp.where(core == 0, other, x)

    def out_block(x):
        return jnp.concatenate([x[width:, : width // 2], x[width:, width // 2 :]], axis=0)

    down_first, down_second = two(down_sum, down_got)
    up_first, up_second = two(up_sum, up_got)
    contract_gradient = jnp.concatenate([down_first, down_second], axis=0).astype(F32)
    expand_gradient = jnp.concatenate([up_first[:width], up_second[:width]], axis=1).astype(F32)
    output_gradient = jnp.concatenate([out_block(up_first), out_block(up_second)], axis=1).astype(F32)

    early_two, late_two = two(early_sum, early_got), two(late_sum, late_got)

    def column(pair, part):
        halves, at = (early_two, pair) if pair < pairs - 1 else (late_two, 0)
        at = at * 384 + part * 128
        return jnp.concatenate([x[:, at : at + 128] for x in halves], axis=0)

    attend_gradient = jnp.stack(
        [
            jnp.concatenate([column(pair, part) for pair in range(pairs)], axis=1)
            for part in range(3)
        ],
        axis=1,
    ).astype(F32)
    return (
        jnp.where(straight, pooled[:maps_all], residual_got[half_rows - maps_all :]).reshape(
            frames_here, MAPS, width
        ),
        tokens_gradient,
        table[0:3],
        table[3:6],
        attend_gradient,
        lax.dynamic_slice_in_dim(table[21:23], plane * share, share, 1),
        output_gradient,
        table[6],
        expand_gradient,
        lax.dynamic_slice_in_dim(table[17:21], 2 * plane, 2, 0).reshape(2 * hid),
        contract_gradient,
        table[7],
        table[8:16].T,
        table[16, :MAPS],
    )


def solution(mesh):
    groups, sides = mesh.devices.shape
    fine = Mesh(mesh.devices.reshape(groups // 2, 2, sides), ("chip", "core", "mp"))
    dp = ("chip", "core")
    every = ("chip", "core", "mp")
    return jax.shard_map(
        body,
        mesh=fine,
        in_specs=(
            P(every, None),
            P(dp, None),
            P(),
            P(),
            P(None, None, "mp"),
            P(None, "mp"),
            P("mp", None),
            P(),
            P(None, "mp"),
            P("mp"),
            P("mp", None),
            P(),
            P(),
            P(),
            P(every, None, None),
        ),
        out_specs=(
            P(every, None, None),
            P(every, None),
            P(),
            P(),
            P(None, None, "mp"),
            P(None, "mp"),
            P("mp", None),
            P(),
            P(None, "mp"),
            P("mp"),
            P("mp", None),
            P(),
            P(),
            P(),
        ),
        check_vma=False,
    )
```

```python
import functools

import jax
import jax.numpy as jnp
from jax import lax
from jax.experimental import pallas as pl
from jax.experimental.pallas import tpu as pltpu
from jax.sharding import Mesh, PartitionSpec as P

HEAD_DIM = 64
MAPS = 8
FRAME_TOK = 196
EPS = 1e-06
BLK = 256
COST = 20.0
FAR = 1e30
GELU_C = 0.7978845608028654
GELU_A = 0.044715

F32 = jnp.float32
BF16 = jnp.bfloat16


def nn(a, b):
    return lax.dot_general(a, b, (((1,), (0,)), ((), ())), preferred_element_type=F32)


def nt(a, b):
    return lax.dot_general(a, b, (((1,), (1,)), ((), ())), preferred_element_type=F32)


def tn(a, b):
    return lax.dot_general(a, b, (((0,), (0,)), ((), ())), preferred_element_type=F32)


def fold8(values):
    rows, width = values.shape
    return jnp.sum(values.reshape(rows // 8, 8, width), axis=0)


def centre(values):
    average = jnp.mean(values, axis=-1, keepdims=True)
    centred = values - average
    spread = jnp.mean(centred * centred, axis=-1, keepdims=True)
    scale = lax.rsqrt(spread + EPS)
    return centred * scale, scale


def norm_back(xhat, scale, gain, grad):
    scaled = grad * gain
    along = jnp.mean(scaled * xhat, axis=-1, keepdims=True)
    return scale * (scaled - jnp.mean(scaled, axis=-1, keepdims=True) - xhat * along)


def cost(flops, nbytes):
    return pl.CostEstimate(
        flops=int(flops * COST), bytes_accessed=int(nbytes * COST), transcendentals=0
    )


def params(n, mib=60):
    return pltpu.CompilerParams(
        dimension_semantics=("arbitrary",) * n, vmem_limit_bytes=mib * 1024 * 1024
    )


def whole(shape):
    return pl.BlockSpec(shape, lambda *_: (0,) * len(shape), pipeline_mode=pl.Buffered(1))


def after(value, *others):
    return lax.optimization_barrier((value, others))[0]


NOTE = 4


def pack_kernel(tokens, cot, offset, count, out):
    here = tokens.shape[0]
    rows = out.shape[0] - cot.shape[0]
    edge = here // 16 * 16
    width = out.shape[1]
    out[:here, :] = tokens[...]
    left = offset[...]
    lines = []
    for _ in range(3):
        line = left.astype(BF16)
        lines.append(line.astype(F32))
        left = left - lines[-1]
    lines.append(jnp.broadcast_to(count[...], (1, width)))
    tail = rows - here
    row = lax.broadcasted_iota(jnp.int32, (tail, width), 0)
    block = jnp.zeros((tail, width), F32)
    for i, line in enumerate(lines):
        block = jnp.where(row == NOTE + i, line, block)
    out[here:rows, :] = block.astype(BF16)
    out[rows:, :] = cot[...]


def pack(tokens, cot, offset, count, half_rows):
    rows, width = half_rows + cot.shape[0], tokens.shape[1]
    return pl.pallas_call(
        pack_kernel,
        in_specs=[pl.BlockSpec(x.shape) for x in (tokens, cot, offset, count)],
        out_specs=pl.BlockSpec((rows, width)),
        out_shape=jax.ShapeDtypeStruct((rows, width), BF16),
        compiler_params=pltpu.CompilerParams(vmem_limit_bytes=8 * 1024 * 1024),
        cost_estimate=cost(0, 4 * rows * width),
        name="pack",
    )(tokens, cot, offset, count)


def relay_kernel(scal, mine, first, second, out):
    straight = scal[0] == scal[1]
    rows = first.shape[0]
    swap = scal[2] == 1
    for half in range(2):
        here = slice(half * rows, (half + 1) * rows)
        one, two = (first, second) if half == 0 else (second, first)
        got = jnp.where(swap, two[...], one[...])
        kept = jnp.where(straight, mine[here, :], got)
        share = kept.shape[1] // 3
        for pair in range(share // 128):
            for item in range(3):
                to = pair * 384 + item * 128
                at = item * share + pair * 128
                out[here, to : to + 128] = kept[:, at : at + 128]


def relay(scal, mine, first, second):
    return pl.pallas_call(
        relay_kernel,
        grid_spec=pltpu.PrefetchScalarGridSpec(
            num_scalar_prefetch=1,
            grid=(1,),
            in_specs=[held(mine.shape), held(first.shape), held(first.shape)],
            out_specs=held(mine.shape),
        ),
        out_shape=jax.ShapeDtypeStruct(mine.shape, BF16),
        compiler_params=params(1, 10),
        cost_estimate=cost(0, 0),
        name="relay",
    )(scal, mine, first, second)


def project_kernel(
    frames_here, scal, oth, own, gain, shift, weight, first, qkv, qfeat, kfeat, offset
):
    step = pl.program_id(0)
    half_blocks = pl.num_programs(0) // 2
    half_rows = half_blocks * BLK
    within = lax.rem(step, half_blocks) * BLK
    rows = pl.ds(pl.multiple_of(within, BLK), BLK)

    @pl.when(step == 0)
    def _():
        start = frames_here * FRAME_TOK // 16 * 16
        at = frames_here * FRAME_TOK + NOTE - start
        block = own[start : start + 32, :].astype(F32)
        note = block[at : at + 1, :] + block[at + 1 : at + 2, :] + block[at + 2 : at + 3, :]
        share = weight.shape[1] // 3
        offset[...] = jnp.zeros_like(offset)
        for pair in range(share // 128):
            here = pair * 128
            offset[:, 3 * here : 3 * here + 128] = note[:, here : here + 128]
            offset[:, 3 * here + 256 : 3 * here + 384] = note[:, share + here : share + here + 128]

    values = jnp.where(step < half_blocks, oth[rows, :], own[rows, :]).astype(F32)
    xhat, _ = centre(values)
    low = (xhat * gain[...] + shift[...]).astype(BF16)
    first[...] = low
    out = (nn(low, weight[...]) + offset[...]).astype(BF16)
    for pair in range(out.shape[1] // 384):
        at = pair * 384
        qkv[:, at : at + 128] = out[:, at : at + 128] * jnp.asarray(HEAD_DIM**-0.5, BF16)
        qkv[:, at + 128 : at + 384] = out[:, at + 128 : at + 384]
    core, count = scal[0], scal[2]
    half = jnp.where(step < half_blocks, 1 - core, core)
    edge = clip_edge(count, frames_here, half_rows)
    token = within + lax.broadcasted_iota(jnp.int32, (BLK, 128), 0)
    lane = lax.broadcasted_iota(jnp.int32, (BLK, 128), 1)
    clip = jnp.where(half * half_rows + token >= edge, 1, 0)
    clip = jnp.where(token >= frames_here * FRAME_TOK, 2, clip)
    hit = lane == clip
    qfeat[...] = jnp.where(hit, 1.0, 0.0).astype(BF16)
    kfeat[...] = jnp.where(hit, 0.0, jnp.where(lane < 3, -FAR, 0.0)).astype(BF16)


def clip_edge(count, frames_here, half_rows):
    return jnp.where(
        count < frames_here,
        count * FRAME_TOK,
        half_rows + (count - frames_here) * FRAME_TOK,
    )


def clip_span(block, edge, blocks):
    low = jnp.where(block * BLK >= edge, edge // BLK, 0)
    high = jnp.where(block * BLK + BLK - 1 < edge, (edge + BLK - 1) // BLK, blocks)
    return low, high


def project(scal, oth, own, gain, shift, weight, frames_here, half_rows):
    width, cols = weight.shape
    steps = 2 * half_rows // BLK
    rows = 2 * half_rows
    return pl.pallas_call(
        functools.partial(project_kernel, frames_here),
        grid_spec=pltpu.PrefetchScalarGridSpec(
            num_scalar_prefetch=1,
            grid=(steps,),
            in_specs=[
                whole(oth.shape),
                whole(own.shape),
                whole((1, width)),
                whole((1, width)),
                whole((width, cols)),
            ],
            out_specs=[
                pl.BlockSpec((BLK, width), lambda i, *_: (i, 0)),
                pl.BlockSpec((BLK, cols), lambda i, *_: (i, 0)),
                pl.BlockSpec((BLK, 128), lambda i, *_: (i, 0)),
                pl.BlockSpec((BLK, 128), lambda i, *_: (i, 0)),
            ],
            scratch_shapes=[pltpu.VMEM((1, cols), F32)],
        ),
        out_shape=[
            jax.ShapeDtypeStruct((rows, width), BF16),
            jax.ShapeDtypeStruct((rows, cols), BF16),
            jax.ShapeDtypeStruct((rows, 128), BF16),
            jax.ShapeDtypeStruct((rows, 128), BF16),
        ],
        compiler_params=params(1, 10),
        cost_estimate=cost(2 * rows * width * cols, 4 * rows * width + 2 * rows * cols),
        name="project",
    )(scal, oth, own, gain, shift, weight)


def attend_kernel(
    frames_here,
    bk,
    scal,
    q,
    qfeat,
    qkv,
    kfeat,
    mixed,
    wide,
    log_total,
    scores,
    tops,
    acc,
    keys_all,
    values_all,
):
    step = pl.program_id(0)
    half = pl.num_programs(0)
    blocks = 2 * half
    pairs = q.shape[1] // 384
    flip = half * (1 - scal[0])
    edge = clip_edge(scal[2], frames_here, half * BLK)
    low, high = clip_span((step + half * scal[3]) ^ flip, edge, blocks)
    per = bk // BLK
    low, high = low // per, (high + per - 1) // per
    kflip = flip // per
    lane = lax.broadcasted_iota(jnp.int32, (BLK, 128), 1)
    left = lane < HEAD_DIM
    none = jnp.zeros((BLK, 128), BF16)
    queries = []
    for pair in range(pairs):
        both = q[:, pair * 384 : pair * 384 + 128]
        queries.append(jnp.concatenate([jnp.where(left, both, none), qfeat[...]], axis=1))
        queries.append(jnp.concatenate([jnp.where(left, none, both), qfeat[...]], axis=1))
    @pl.when(step == 0)
    def _():
        def prepare(block, carry):
            rows = pl.ds(pl.multiple_of(block * BLK, BLK), BLK)
            for pair in range(pairs):
                at = pair * 384
                keys_all[pair, rows, :128] = qkv[rows, at + 128 : at + 256]
                keys_all[pair, rows, 128:] = kfeat[rows, :]
                both = qkv[rows, at + 256 : at + 384]
                values_all[2 * pair, rows, :128] = jnp.where(left, both, none)
                values_all[2 * pair, rows, 128:] = jnp.where(left, 1.0, 0.0).astype(BF16)
                values_all[2 * pair + 1, rows, :128] = jnp.where(left, none, both)
                values_all[2 * pair + 1, rows, 128:] = jnp.where(left, 0.0, 1.0).astype(BF16)
            return carry

        lax.fori_loop(0, blocks, prepare, 0)

    for head in range(2 * pairs):
        tops[head] = jnp.full((BLK, 128), -3e38, F32)

    def score(block, carry):
        rows = pl.ds(pl.multiple_of((block ^ kflip) * bk, bk), bk)
        for pair in range(pairs):
            keys = keys_all[pair, rows, :]
            for head in (2 * pair, 2 * pair + 1):
                values = nt(queries[head], keys)
                scores[head, block] = values
                top = tops[head]
                for part in range(bk // 128):
                    top = jnp.maximum(top, values[:, part * 128 : (part + 1) * 128])
                tops[head] = top
        return carry

    lax.fori_loop(low, high, score, 0)
    for head in range(2 * pairs):
        tops[head] = jnp.broadcast_to(jnp.max(tops[head], axis=1, keepdims=True), (BLK, 128))
    acc[...] = jnp.zeros_like(acc)
    def mix(block, carry):
        rows = pl.ds(pl.multiple_of((block ^ kflip) * bk, bk), bk)
        for pair in range(pairs):
            soft = []
            for head in (2 * pair, 2 * pair + 1):
                top = tops[head]
                for part in range(bk // 128):
                    piece = scores[head, block, :, part * 128 : (part + 1) * 128]
                    soft.append(jnp.exp(piece - top).astype(BF16))
            values = jnp.concatenate(
                [values_all[2 * pair, rows, :], values_all[2 * pair + 1, rows, :]], axis=0
            )
            acc[pair] += nn(jnp.concatenate(soft, axis=1), values)
        return carry

    lax.fori_loop(low, high, mix, 0)
    for pair in range(pairs):
        cols = slice(pair * 128, (pair + 1) * 128)
        totals = acc[pair, :, 128:]
        out = acc[pair, :, :128] / totals
        wide[:, cols] = out
        mixed[:, cols] = out.astype(BF16)
        logs = (jnp.where(left, tops[2 * pair], tops[2 * pair + 1]) + jnp.log(totals)).T
        log_total[pair, 0, 0:1] = logs[0:1]
        log_total[pair, 0, 1:2] = logs[HEAD_DIM : HEAD_DIM + 1]


def attend(scal, qkv, qfeat, kfeat, frames_here):
    rows, cols = qkv.shape
    width = cols // 3
    pairs = width // 128
    half = rows // BLK // 2
    bk = rows // 2
    return pl.pallas_call(
        functools.partial(attend_kernel, frames_here, bk),
        grid_spec=pltpu.PrefetchScalarGridSpec(
            num_scalar_prefetch=1,
            grid=(half,),
            in_specs=[
                pl.BlockSpec((BLK, cols), lambda i, scal: (i + half * scal[3], 0)),
                pl.BlockSpec((BLK, 128), lambda i, scal: (i + half * scal[3], 0)),
                whole((rows, cols)),
                whole((rows, 128)),
            ],
            out_specs=[
                pl.BlockSpec((BLK, width), lambda i, *_: (i, 0)),
                pl.BlockSpec((BLK, width), lambda i, *_: (i, 0)),
                pl.BlockSpec((pairs, 1, 8, BLK), lambda i, *_: (0, i, 0, 0)),
            ],
            scratch_shapes=[
                pltpu.VMEM((2 * pairs, rows // bk, BLK, bk), F32),
                pltpu.VMEM((2 * pairs, BLK, 128), F32),
                pltpu.VMEM((pairs, BLK, 256), F32),
                pltpu.VMEM((pairs, rows, 256), BF16),
                pltpu.VMEM((2 * pairs, rows, 256), BF16),
            ],
        ),
        out_shape=[
            jax.ShapeDtypeStruct((rows // 2, width), BF16),
            jax.ShapeDtypeStruct((rows // 2, width), F32),
            jax.ShapeDtypeStruct((pairs, half, 8, BLK), F32),
        ],
        compiler_params=params(1, 28),
        cost_estimate=cost(8 * rows * rows * width, 16 * rows * width),
        name="attend",
    )(scal, qkv, qfeat, qkv, kfeat)


def gather_out_weight(scal, own_out, got_up, more_up, out_weight, hid):
    core, plane = scal[0], scal[1]
    share = own_out.shape[0]
    quarter = share // 2
    out_weight[pl.ds(pl.multiple_of(plane * share, 64), share), :] = own_out[...]
    base = (1 - plane) * share
    out_weight[pl.ds(pl.multiple_of(base + core * quarter, 64), quarter), :] = got_up[
        hid : hid + quarter, :
    ]
    out_weight[pl.ds(pl.multiple_of(base + (1 - core) * quarter, 64), quarter), :] = more_up[
        hid : hid + quarter, :
    ]


def up_weight(core, own_up, got_up, more_up, chunk):
    hid = got_up.shape[1]
    if chunk < 2:
        return (more_up, got_up)[chunk][:hid, :]
    pick = (1 - core) if chunk == 2 else core
    return own_up[:, pl.ds(pl.multiple_of(pick * hid, 128), hid)]


def down_weight(core, own_down, got_down, more_down, chunk):
    hid = got_down.shape[1]
    if chunk < 2:
        return (more_down, got_down)[chunk][...]
    pick = (1 - core) if chunk == 2 else core
    return own_down[pl.ds(pl.multiple_of(pick * hid, 128), hid), :]


def ahead_kernel(
    frames_here,
    scal,
    mixed_own,
    mixed_oth,
    tokens,
    cot,
    own_out,
    own_up,
    own_down,
    got_up,
    got_down,
    more_up,
    more_down,
    up_offset,
    gains,
    shifts,
    out_offset,
    down_offset,
    learner,
    learner_offset,
    out_grad_out,
    xhat_out,
    scale_out,
    slope_out,
    second_out,
    out_low_out,
    sums,
    pooled,
    learner_sums,
    learner_offset_sums,
    theirs_out,
    mine_out,
    out_weight,
    hidden_kept,
    down_total,
):
    step = pl.program_id(0)
    core, plane = scal[0], scal[1]
    hid = got_up.shape[1]
    share = own_out.shape[0]

    @pl.when(step == 0)
    def _():
        gather_out_weight(scal, own_out, got_up, more_up, out_weight, hid)
        for ref in (sums, pooled, learner_sums, learner_offset_sums, down_total):
            ref[...] = jnp.zeros_like(ref)

    def up_bias(chunk):
        pick = (1 - core) if chunk % 2 == 0 else core
        if chunk >= 2:
            return up_offset[pl.ds(pick, 1), :]
        note = got_up[hid + share // 2 :, :].astype(F32)
        sums = [
            note[3 * i : 3 * i + 1] + note[3 * i + 1 : 3 * i + 2] + note[3 * i + 2 : 3 * i + 3]
            for i in range(2)
        ]
        return jnp.where(pick == 0, sums[0], sums[1])

    mine = pl.ds(pl.multiple_of(core * share, 64), share)
    theirs = pl.ds(pl.multiple_of((1 - core) * share, 64), share)
    attended = nn(mixed_own[...], out_weight[mine, :]) + nn(mixed_oth[...], out_weight[theirs, :])
    residual = tokens[...].astype(F32) + attended + out_offset[...]
    xhat_two, scale_two = centre(residual)
    xhat_out[...] = xhat_two
    scale_out[...] = jnp.broadcast_to(scale_two, scale_out.shape)
    second = (xhat_two * gains[1:2, :] + shifts[1:2, :]).astype(BF16)
    second_out[...] = second
    block_out = residual + down_offset[...]
    for chunk in range(4):
        cols = slice(chunk * hid, (chunk + 1) * hid)
        pre = nn(second, up_weight(core, own_up, got_up, more_up, chunk)) + up_bias(chunk)
        square = pre * pre
        gate = 0.5 + 0.5 * jnp.tanh(pre * (GELU_C + (GELU_A * GELU_C) * square))
        product = pre * gate
        hidden = product.astype(BF16)
        bend = (1.0 - gate) * (2.0 * GELU_C + (6.0 * GELU_A * GELU_C) * square)
        slope_out[:, cols] = (gate + product * bend).astype(BF16)
        hidden_kept[:, cols] = hidden
        block_out = block_out + nn(hidden, down_weight(core, own_down, got_down, more_down, chunk))
    xhat_three, scale_three = centre(block_out)
    third = (xhat_three * gains[2:3, :] + shifts[2:3, :]).astype(BF16)
    logits = nt(third, learner[...]) + learner_offset[...]
    sig = 1.0 / (1.0 + jnp.exp(-logits))
    token = step * BLK + lax.broadcasted_iota(jnp.int32, (BLK, 128), 0)
    first_token = (lax.broadcasted_iota(jnp.int32, (BLK, 128), 1) >> 3) * FRAME_TOK
    inside = (token >= first_token) & (token < first_token + FRAME_TOK)
    inside = inside & (first_token < frames_here * FRAME_TOK)
    maps = jnp.where(inside, sig, 0.0).astype(BF16)
    feature = block_out.astype(BF16)
    pooled[...] += tn(maps, feature)
    maps_grad = nt(feature, cot[...])
    pool_grad = nn(maps, cot[...])
    logits_grad = jnp.where(inside, maps_grad * sig * (1.0 - sig), 0.0).astype(BF16)
    learner_sums[...] += tn(logits_grad, third)
    learner_offset_sums[...] += fold8(logits_grad.astype(F32))
    third_grad = nn(logits_grad, learner[...])
    sums[0:8, :] += fold8(third_grad * xhat_three)
    sums[8:16, :] += fold8(third_grad)
    out_grad = pool_grad + norm_back(xhat_three, scale_three, gains[2:3, :], third_grad)
    sums[16:24, :] += fold8(out_grad)
    out_grad_out[...] = out_grad
    out_low = out_grad.astype(BF16)
    out_low_out[...] = out_low
    for chunk in range(4):
        down_total[chunk] += tn(hidden_kept[:, chunk * hid : (chunk + 1) * hid], out_low)

    @pl.when(step == pl.num_programs(0) - 1)
    def _():
        for n in range(2):
            theirs_out[n] = down_total[2 * n].astype(BF16)
            mine_out[n] = down_total[2 * n + 1].astype(BF16)


def behind_kernel(
    pooled_rows,
    scal,
    out_grad,
    out_low,
    xhat_two,
    scale_two,
    slope,
    second,
    mixed_own,
    mixed_oth,
    own_out,
    own_up,
    own_down,
    got_up,
    got_down,
    more_up,
    more_down,
    gains,
    pooled,
    residual_grad_out,
    grad_own,
    grad_oth,
    sums,
    up_sums,
    theirs_out,
    mine_out,
    out_weight,
    up_total,
    out_total,
):
    core, plane = scal[0], scal[1]
    hid = got_up.shape[1]
    share = own_out.shape[0]

    @pl.when(pl.program_id(0) == 0)
    def _():
        gather_out_weight(scal, own_out, got_up, more_up, out_weight, hid)
        for ref in (sums, up_sums, up_total, out_total):
            ref[...] = jnp.zeros_like(ref)

    mine = pl.ds(pl.multiple_of(core * share, 64), share)
    theirs = pl.ds(pl.multiple_of((1 - core) * share, 64), share)
    low = out_low[...]
    second_turned = second[...].T
    second_grad = None
    for chunk in range(4):
        cols = slice(chunk * hid, (chunk + 1) * hid)
        hidden_grad = nt(low, down_weight(core, own_down, got_down, more_down, chunk))
        pre_grad = (hidden_grad * slope[:, cols].astype(F32)).astype(BF16)
        up_total[chunk] += nn(second_turned, pre_grad)
        up_sums[:, cols] += fold8(pre_grad.astype(F32))
        term = nt(pre_grad, up_weight(core, own_up, got_up, more_up, chunk))
        second_grad = term if second_grad is None else second_grad + term
    xhat = xhat_two[...]
    sums[0:8, :] += fold8(second_grad * xhat)
    sums[8:16, :] += fold8(second_grad)
    residual_grad = out_grad[...] + norm_back(
        xhat, scale_two[:, :1], gains[1:2, :], second_grad
    )
    sums[16:24, :] += fold8(residual_grad)
    residual_grad_out[...] = residual_grad

    @pl.when(pl.program_id(0) == pl.num_programs(0) - 1)
    def _():
        residual_grad_out[BLK - pooled_rows :, :] = pooled[:pooled_rows, :]

    residual_low = residual_grad.astype(BF16)
    grad_own[...] = nt(residual_low, out_weight[mine, :]).astype(BF16)
    grad_oth[...] = nt(residual_low, out_weight[theirs, :]).astype(BF16)
    out_total[0] += tn(mixed_own[...], residual_low)
    out_total[1] += tn(mixed_oth[...], residual_low)

    @pl.when(pl.program_id(0) == pl.num_programs(0) - 1)
    def _():
        width = second.shape[1]
        half = width // 2
        for odd, (out, column) in enumerate(((theirs_out, 1 - core), (mine_out, core))):
            for n in range(2):
                out[n, :width, :] = up_total[2 * n + odd].astype(BF16)
                side = (1 - plane) if n == 0 else plane
                at = pl.ds(pl.multiple_of(column * half, 128), half)
                grad = out_total[jnp.where(side == core, 0, 1), :, at].astype(BF16)
                out[n, width:, :half] = grad[: share // 2]
                out[n, width:, half:] = grad[share // 2 :]


def row_block(cols):
    return pl.BlockSpec((BLK, cols), lambda i, *_: (i, 0))


def held(shape):
    return pl.BlockSpec(shape, lambda *_: (0,) * len(shape))


def row_call(kernel, name, scal, rowed, wholes, row_outs, held_outs, scratch, flops, mib, low_outs=()):
    rows = rowed[0].shape[0]
    nbytes = sum(x.size * x.dtype.itemsize for x in wholes)
    nbytes += rows * sum(c * (2 if t == BF16 else 4) for c, t in row_outs)
    return pl.pallas_call(
        kernel,
        grid_spec=pltpu.PrefetchScalarGridSpec(
            num_scalar_prefetch=1,
            grid=(rows // BLK,),
            in_specs=[row_block(x.shape[1]) for x in rowed] + [whole(x.shape) for x in wholes],
            out_specs=[row_block(cols) for cols, _ in row_outs]
            + [held(s) for s in held_outs]
            + [whole(s) for s in low_outs],
            scratch_shapes=scratch,
        ),
        out_shape=[jax.ShapeDtypeStruct((rows, cols), t) for cols, t in row_outs]
        + [jax.ShapeDtypeStruct(s, F32) for s in held_outs]
        + [jax.ShapeDtypeStruct(s, BF16) for s in low_outs],
        compiler_params=params(1, mib),
        cost_estimate=cost(flops, nbytes),
        name=name,
    )(scal, *rowed, *wholes)


def ahead(scal, mixed_own, mixed_oth, packed, cot, weights, up_offset, small, frames_here):
    rows, share = mixed_own.shape
    width = packed.shape[1]
    hidden = 2 * up_offset.size
    return row_call(
        functools.partial(ahead_kernel, frames_here),
        "ahead",
        scal,
        [mixed_own, mixed_oth, packed],
        [cot, *weights, up_offset, *small],
        [
            (width, F32),
            (width, F32),
            (128, F32),
            (hidden, BF16),
            (width, BF16),
            (width, BF16),
        ],
        [(24, width), (128, width), (128, width), (8, 128)],
        [
            pltpu.VMEM((2 * share, width), BF16),
            pltpu.VMEM((BLK, hidden), BF16),
            pltpu.VMEM((4, hidden // 4, width), F32),
        ],
        2 * rows * width * (3 * hidden + width),
        42,
        [(2, hidden // 4, width)] * 2,
    )


def behind(scal, rowed, weights, gains, pooled, maps_all):
    rows, width = rowed[0].shape
    share = weights[0].shape[0]
    hidden = rowed[4].shape[1]
    hid = hidden // 4
    return row_call(
        functools.partial(behind_kernel, maps_all),
        "behind",
        scal,
        rowed,
        [*weights, gains, pooled],
        [(width, F32), (share, BF16), (share, BF16)],
        [(24, width), (8, hidden)],
        [
            pltpu.VMEM((2 * share, width), BF16),
            pltpu.VMEM((4, width, hid), F32),
            pltpu.VMEM((2, share, width), F32),
        ],
        2 * rows * width * (3 * hidden + 2 * width),
        44,
        [(2, width + share // 2, hid)] * 2,
    )


def attend_back_kernel(
    frames_here,
    scal,
    k,
    v,
    kfeat,
    q,
    qfeat,
    grad_oth,
    grad_own,
    wide_oth,
    wide_own,
    log_oth,
    log_own,
    out_oth,
    out_own,
    queries,
    grads,
    inner,
    logs,
    dq,
    dkv,
):
    step = pl.program_id(0)
    half = grad_oth.shape[0] // BLK
    blocks = 2 * half
    flip = half * (1 - scal[0])
    edge = clip_edge(scal[2], frames_here, half * BLK)
    low, high = clip_span(step ^ flip, edge, blocks)
    bq = half * BLK
    low, high = low // half, (high + half - 1) // half
    qflip = 1 - scal[0]
    lane = lax.broadcasted_iota(jnp.int32, (BLK, 128), 1)
    left = lane < HEAD_DIM
    none = jnp.zeros((BLK, 128), BF16)

    @pl.when(step == 0)
    def _():
        dq[...] = jnp.zeros_like(dq)
        for side, (grad, wide, log_total) in enumerate(
            ((grad_oth, wide_oth, log_oth), (grad_own, wide_own, log_own))
        ):
            for block in range(bq // BLK):
                here = slice(block * BLK, (block + 1) * BLK)
                rows = slice(side * bq + block * BLK, side * bq + (block + 1) * BLK)
                grads[rows, :] = grad[here, :]
                queries[rows, :128] = q[rows, :]
                queries[rows, 128:] = qfeat[rows, :]
                product = (grad[here, :].astype(F32) * wide[here, :]).T
                inner[side, 0:1, here] = jnp.sum(product[:HEAD_DIM], axis=0, keepdims=True)
                inner[side, 1:2, here] = jnp.sum(product[HEAD_DIM:], axis=0, keepdims=True)
                logs[side, :, here] = log_total[0, block]

    ka = jnp.where(left, k[...], none)
    kb = jnp.where(left, none, k[...])
    key_a = jnp.concatenate([ka, kfeat[...]], axis=1)
    key_b = jnp.concatenate([kb, kfeat[...]], axis=1)
    keys = jnp.concatenate([ka, kb], axis=0)
    va = jnp.where(left, v[...], none)
    vb = jnp.where(left, none, v[...])
    dkv[...] = jnp.zeros_like(dkv)

    def pair(block, carry):
        local = block ^ qflip
        rows = pl.ds(pl.multiple_of(local * bq, bq), bq)
        query = queries[rows, :]
        grad = grads[rows, :]
        soft_a = jnp.exp(nt(key_a, query) - logs[local, 0:1])
        soft_b = jnp.exp(nt(key_b, query) - logs[local, 1:2])
        score_a = (soft_a * (nt(va, grad) - inner[local, 0:1])).astype(BF16)
        score_b = (soft_b * (nt(vb, grad) - inner[local, 1:2])).astype(BF16)
        dkv[0] += nn(soft_a.astype(BF16), grad)
        dkv[1] += nn(soft_b.astype(BF16), grad)
        dkv[2] += nn(score_a, query[:, :128])
        dkv[3] += nn(score_b, query[:, :128])
        dq[rows, :] += tn(jnp.concatenate([score_a, score_b], axis=0), keys)
        return carry

    lax.fori_loop(low, high, pair, 0)
    dk = jnp.where(left, dkv[2], dkv[3]).astype(BF16)
    dv = jnp.where(left, dkv[0], dkv[1]).astype(BF16)
    within = pl.ds(pl.multiple_of(lax.rem(step, half) * BLK, BLK), BLK)

    @pl.when(step < half)
    def _():
        out_oth[within, 128:256] = dk
        out_oth[within, 256:] = dv

    @pl.when(step >= half)
    def _():
        out_own[within, 128:256] = dk
        out_own[within, 256:] = dv

    @pl.when(step == blocks - 1)
    def _():
        half_rows = out_oth.shape[0]
        out_oth[:, :128] = (dq[:half_rows, :] * HEAD_DIM**-0.5).astype(BF16)
        out_own[:, :128] = (dq[half_rows:, :] * HEAD_DIM**-0.5).astype(BF16)

def attend_back(scal, qkv, qfeat, kfeat, grad_oth, grad_own, wide, logs, frames_here):
    rows = qkv.shape[0]
    blocks = rows // BLK
    one = pl.Buffered(1)
    half_rows = pl.BlockSpec((rows // 2, 128), lambda j, scal: (0, scal[3]), pipeline_mode=one)
    half_logs = pl.BlockSpec(
        (1, blocks // 2, 8, BLK), lambda j, scal: (scal[3], 0, 0, 0), pipeline_mode=one
    )
    return pl.pallas_call(
        functools.partial(attend_back_kernel, frames_here),
        grid_spec=pltpu.PrefetchScalarGridSpec(
            num_scalar_prefetch=1,
            grid=(blocks,),
            in_specs=[
                pl.BlockSpec((BLK, 128), lambda j, scal: (j, 3 * scal[3] + 1)),
                pl.BlockSpec((BLK, 128), lambda j, scal: (j, 3 * scal[3] + 2)),
                pl.BlockSpec((BLK, 128), lambda j, *_: (j, 0)),
                pl.BlockSpec((rows, 128), lambda j, scal: (0, 3 * scal[3]), pipeline_mode=one),
                whole((rows, 128)),
                half_rows,
                half_rows,
                half_rows,
                half_rows,
                half_logs,
                half_logs,
            ],
            out_specs=[pl.BlockSpec((rows // 2, 384), lambda j, *_: (0, 0))] * 2,
            scratch_shapes=[
                pltpu.VMEM((rows, 256), BF16),
                pltpu.VMEM((rows, 128), BF16),
                pltpu.VMEM((2, 8, rows // 2), F32),
                pltpu.VMEM((2, 8, rows // 2), F32),
                pltpu.VMEM((rows, 128), F32),
                pltpu.VMEM((4, BLK, 128), F32),
            ],
        ),
        out_shape=[jax.ShapeDtypeStruct((rows // 2, 384), BF16)] * 2,
        compiler_params=params(1, 14),
        cost_estimate=cost(40 * rows * rows * 128, 30 * rows * 128),
        name="attend_back",
    )(scal, qkv, qkv, kfeat, qkv, qfeat, grad_oth, grad_own, *wide, *logs)


def project_grad_kernel(pairs, more, scal, first, *refs):
    oth, own = refs[:pairs], refs[pairs : 2 * pairs]
    refs = refs[2 * pairs :]
    if more:
        got, weight_mine, weight_theirs = refs[:pairs], refs[pairs], refs[pairs + 1]
        theirs, mine, offsets, part = refs[pairs + 2 :]
    else:
        theirs, mine, offsets = refs
    step = pl.program_id(0)
    half = oth[0].shape[0]
    one = jnp.concatenate([x[...] for x in oth], axis=1)
    two = jnp.concatenate([x[...] for x in own], axis=1)
    out = (tn(first[:half, :], one) + tn(first[half:, :], two)).astype(BF16)

    @pl.when(step == 0)
    def _():
        theirs[...] = out
        offsets[...] = fold8(one.astype(F32)) + fold8(two.astype(F32))

    @pl.when(step == 1)
    def _():
        mine[...] = out

    if more:
        lines = half // 2
        rows = pl.ds(pl.multiple_of(step * lines, BLK), lines)
        total = nt(jnp.concatenate([x[rows, :] for x in own], axis=1), weight_mine[...])
        part[...] = total + nt(
            jnp.concatenate([x[rows, :] for x in got], axis=1), weight_theirs[...]
        )


def project_grad(scal, first, oth, own, *more):
    pairs = len(oth)
    rows, width = first.shape
    cols = 384 * pairs
    got, weights = (more[0], more[1:]) if more else ((), ())
    weight = pl.BlockSpec((width, cols), lambda *_: (0, 0), pipeline_mode=pl.Buffered(1))
    shapes = [
        jax.ShapeDtypeStruct((width // 2, cols), BF16),
        jax.ShapeDtypeStruct((width // 2, cols), BF16),
        jax.ShapeDtypeStruct((8, cols), F32),
    ]
    specs = [held((width // 2, cols)), held((width // 2, cols)), held((8, cols))]
    if more:
        shapes.append(jax.ShapeDtypeStruct((rows // 2, width), F32))
        specs.append(pl.BlockSpec((rows // 4, width), lambda n, *_: (n, 0)))
    return pl.pallas_call(
        functools.partial(project_grad_kernel, pairs, bool(more)),
        grid_spec=pltpu.PrefetchScalarGridSpec(
            num_scalar_prefetch=1,
            grid=(2,),
            in_specs=[
                pl.BlockSpec((rows, width // 2), lambda n, scal: (0, (1 - scal[0]) ^ n)),
            ]
            + [whole((rows // 2, 384))] * (2 * pairs + len(got))
            + [weight] * len(weights),
            out_specs=specs,
        ),
        out_shape=shapes,
        compiler_params=params(1, 24),
        cost_estimate=cost(2 * rows * width * cols, 2 * rows * (width + cols)),
        name="project_grad",
    )(scal, first, *oth, *own, *got, *weights)


def first_grad_kernel(own, got, mine, theirs, part, tokens, out, sums):
    total = part[...] + nt(own[...], mine[...]) + nt(got[...], theirs[...])
    out[...] = total.astype(BF16)

    @pl.when(pl.program_id(0) == 0)
    def _():
        sums[...] = jnp.zeros_like(sums)

    xhat, _ = centre(tokens[...].astype(F32))
    sums[0:8, :] += fold8(total * xhat)
    sums[8:16, :] += fold8(total)


def first_grad(own, got, mine, theirs, part, packed):
    rows, cols = own.shape
    width = mine.shape[0]
    last_pair = mine.shape[1] // cols - 1
    weight = pl.BlockSpec(
        (width, cols), lambda *_: (0, last_pair), pipeline_mode=pl.Buffered(1)
    )
    row = pl.BlockSpec((BLK, width), lambda i: (i, 0))
    return pl.pallas_call(
        first_grad_kernel,
        grid=(rows // BLK,),
        in_specs=[pl.BlockSpec((BLK, cols), lambda i: (i, 0))] * 2 + [weight] * 2 + [row] * 2,
        out_specs=[row, pl.BlockSpec((16, width), lambda i: (0, 0))],
        out_shape=[
            jax.ShapeDtypeStruct((rows, width), BF16),
            jax.ShapeDtypeStruct((16, width), F32),
        ],
        compiler_params=params(1, 16),
        cost_estimate=cost(4 * rows * width * cols, 12 * rows * width),
        name="first_grad",
    )(own, got, mine, theirs, part, packed)


def last_kernel(scal, tokens, grad, grad_got, residual, residual_got, gain, out):
    xhat, scale = centre(tokens[...].astype(F32))
    straight = scal[0] == scal[1]
    wide = jnp.where(straight, grad[...], grad_got[...]).astype(F32)
    base = jnp.where(straight, residual[...], residual_got[...])
    out[...] = base + norm_back(xhat, scale, gain[...], wide)


def last(scal, packed, grad, grad_got, residual, residual_got, gain, tokens_here):
    rows, width = grad.shape
    return pl.pallas_call(
        last_kernel,
        grid_spec=pltpu.PrefetchScalarGridSpec(
            num_scalar_prefetch=1,
            grid=(rows // BLK,),
            in_specs=[row_block(width)] * 5 + [whole((1, width))],
            out_specs=row_block(width),
        ),
        out_shape=jax.ShapeDtypeStruct((tokens_here, width), F32),
        compiler_params=params(1, 12),
        cost_estimate=cost(20 * rows * width, 12 * rows * width),
        name="last",
    )(scal, packed, grad, grad_got, residual, residual_got, gain)


def table_kernel(
    frames_here, scal, ahead_sums, behind_sums, first_sums, learner, learner_offset, up, *refs
):
    offsets, out = refs[:-1], refs[-1]
    core, plane = scal[0], scal[1]
    width = out.shape[1]
    hid = up.shape[1] // 4

    def total(ref, at):
        return jnp.sum(ref[at : at + 8, :], axis=0, keepdims=True)

    out[...] = jnp.zeros_like(out)
    for row, (ref, at) in enumerate(
        (
            (first_sums, 0),
            (behind_sums, 0),
            (ahead_sums, 0),
            (first_sums, 8),
            (behind_sums, 8),
            (ahead_sums, 8),
            (behind_sums, 16),
            (ahead_sums, 16),
        )
    ):
        out[row : row + 1, :] = total(ref, at)
    out[8:16, :] = sum(learner[MAPS * i : MAPS * (i + 1), :] for i in range(frames_here))
    row = total(learner_offset, 0)
    lane = lax.broadcasted_iota(jnp.int32, (1, 128), 1)
    kept = row
    for i in range(1, frames_here):
        kept = kept + pltpu.roll(row, 128 - MAPS * i, 1)
    out[16:17, :128] = jnp.where(lane < MAPS, kept, 0.0)
    for chunk in range(4):
        side = (1 - plane) if chunk < 2 else plane
        pick = (1 - core) if chunk % 2 == 0 else core
        out[pl.ds(17 + 2 * side + pick, 1), :] = jnp.sum(
            up[:, chunk * hid : (chunk + 1) * hid], axis=0, keepdims=True
        )
    pair = 0
    for ref in offsets:
        for at in range(0, ref.shape[1], 384):
            to = pl.ds(pl.multiple_of(core * (width // 2) + pair * 128, 128), 128)
            out[21:22, to] = jnp.sum(ref[:, at : at + 128], axis=0, keepdims=True)
            out[22:23, to] = jnp.sum(ref[:, at + 256 : at + 384], axis=0, keepdims=True)
            pair += 1


def small_table(scal, frames_here, *parts):
    width = parts[0].shape[1]
    return pl.pallas_call(
        functools.partial(table_kernel, frames_here),
        grid_spec=pltpu.PrefetchScalarGridSpec(
            num_scalar_prefetch=1,
            grid=(1,),
            in_specs=[held(x.shape) for x in parts],
            out_specs=held((24, width)),
        ),
        out_shape=jax.ShapeDtypeStruct((24, width), F32),
        compiler_params=pltpu.CompilerParams(vmem_limit_bytes=6 * 1024 * 1024),
        cost_estimate=cost(0, 1 << 20),
        name="small_table",
    )(scal, *parts)


def body(
    tokens,
    frame_counts,
    norm_gains,
    norm_shifts,
    attend_weight,
    attend_offset,
    output_weight,
    output_offset,
    expand_weight,
    expand_offset,
    contract_weight,
    contract_offset,
    learner_weight,
    learner_offset,
    pooled_cotangent,
):
    tokens_here, width = tokens.shape
    frames_here = tokens_here // FRAME_TOK
    half_rows = -(-tokens_here // BLK) * BLK
    share = attend_weight.shape[2]
    hid = contract_weight.shape[0] // 2
    chips = lax.axis_size("chip")
    core, plane = lax.axis_index("core"), lax.axis_index("mp")
    straight = core == plane
    flip2 = [(0, 1), (1, 0)]

    def turn(x):
        return lax.ppermute(x, ("core", "mp"), [(1, 2), (2, 1)])

    def to_core(x):
        return lax.ppermute(x, "core", flip2)

    def to_plane(x):
        return lax.ppermute(x, "mp", flip2)

    chip = lax.axis_index("chip")
    side = chip % 2
    hops = []
    while (2 << len(hops)) < chips:
        hops.append(2 << len(hops))

    def hop(x, step):
        return lax.ppermute(x, "chip", [(i, i ^ step) for i in range(chips)])

    def low(x):
        return x.astype(BF16)

    def plus(a, b):
        return a.astype(F32) + b.astype(F32)

    def pick(x, index):
        return lax.dynamic_index_in_dim(x, index, 0, keepdims=False)

    def halves_of(x):
        rows = x.shape[-2] // 2
        return x.reshape(*x.shape[:-2], 2, rows, x.shape[-1])

    def join(x, other, index, axis):
        return jnp.concatenate(
            [jnp.where(index == 0, x, other), jnp.where(index == 0, other, x)], axis=axis
        )

    pairs = share // 128

    weight_mine = attend_weight.reshape(width, 3 * share)
    weight_part = lax.dynamic_slice_in_dim(attend_weight, side * (width // 2), width // 2, 0)
    weight_part = weight_part.reshape(width // 2, 3 * share)
    weight_got = turn(weight_part)
    packed = pack(
        after(tokens, weight_part),
        pooled_cotangent.reshape(frames_here * MAPS, width),
        attend_offset.reshape(1, 2 * share),
        frame_counts[:, :1].astype(F32),
        half_rows,
    )
    got_packed = turn(packed)
    weight_rest = lax.ppermute(
        weight_got,
        ("chip", "core", "mp"),
        [(4 * i + j, 4 * (i ^ 1) + j) for i in range(chips) for j in (1, 2)],
    )
    weight_here = relay(
        jnp.stack([core, plane, side]).astype(jnp.int32), weight_mine, weight_got, weight_rest
    )
    left, notes = expand_offset.reshape(2, hid), []
    for _ in range(3):
        notes.append(lax.reduce_precision(left, 8, 7))
        left = left - notes[-1]
    notes = jnp.stack(notes, axis=1).reshape(6, hid)
    up_quarter = jnp.concatenate(
        [
            lax.dynamic_slice_in_dim(expand_weight, core * hid, hid, 1),
            lax.dynamic_slice_in_dim(output_weight, core * (share // 2), share // 2, 0),
            jnp.pad(notes, ((0, 10), (0, 0))).astype(BF16),
        ],
        axis=0,
    )
    down_quarter = lax.dynamic_slice_in_dim(contract_weight, core * hid, hid, 0)
    own = jnp.where(
        straight, packed, after(got_packed, weight_here, up_quarter, down_quarter)
    )
    oth = to_core(own)
    count = own[tokens_here + NOTE + 3, 0].astype(jnp.int32)
    numbered = [
        jnp.stack([core.astype(jnp.int32), plane.astype(jnp.int32), count, jnp.int32(i)])
        for i in range(pairs)
    ]
    scal = numbered[0]

    up_got_a = to_plane(after(up_quarter, own, weight_here))
    down_got_a = to_plane(after(down_quarter, oth))

    first, qkv, qfeat, kfeat = project(
        scal,
        oth,
        own,
        norm_gains[0:1],
        norm_shifts[0:1],
        weight_here,
        frames_here,
        half_rows,
    )
    weight_there = to_core(after(weight_here, qkv))
    mixed_send, wide_oth, logs_oth = attend(numbered[0], qkv, qfeat, kfeat, frames_here)
    mixed_oth = to_core(mixed_send)
    up_got_b = to_core(after(up_got_a, mixed_send))
    mixed_own, wide_own, logs_own = attend(
        after(numbered[1], mixed_send, weight_there), qkv, qfeat, kfeat, frames_here
    )
    down_got_b = to_core(after(down_got_a, mixed_own))

    maps_all = frames_here * MAPS
    cot = jnp.pad(own[half_rows:], ((0, 128 - maps_all), (0, 0)))
    learner = jnp.pad(jnp.tile(learner_weight.T, (frames_here, 1)), ((0, 128 - maps_all), (0, 0)))
    learner_bias = jnp.pad(jnp.tile(learner_offset, frames_here), (0, 128 - maps_all))[None]
    weights = (
        *(
            pltpu.with_memory_space_constraint(x, pltpu.HBM)
            for x in (output_weight, expand_weight, contract_weight)
        ),
        up_got_a,
        down_got_a,
        up_got_b,
        down_got_b,
    )
    (
        out_grad,
        xhat_two,
        scale_two,
        slope,
        second,
        out_low,
        sums_ahead,
        pooled,
        learner_sums,
        learner_offset_sums,
        down_theirs,
        down_mine,
    ) = ahead(
        scal,
        mixed_own,
        mixed_oth,
        own,
        cot,
        weights,
        expand_offset.reshape(2, hid),
        (
            norm_gains,
            norm_shifts,
            output_offset[None],
            contract_offset[None],
            learner,
            learner_bias,
        ),
        frames_here,
    )

    down_got = to_core(down_theirs)
    down_send = low(plus(down_got[0], down_mine[0]))
    down_keep = plus(down_got[1], down_mine[1])
    down_plane = to_plane(down_send)

    (
        residual_grad,
        grad_own,
        grad_send,
        sums_behind,
        up_sums,
        up_theirs,
        up_mine,
    ) = behind(
        after(scal, down_send),
        [out_grad, out_low, xhat_two, scale_two, slope, second, mixed_own, mixed_oth],
        weights,
        norm_gains,
        pooled,
        maps_all,
    )
    down_half = halves_of(plus(down_keep, after(down_plane, residual_grad)))
    down_x_send = low(pick(down_half, 1 - side))
    down_x_keep = pick(down_half, side)
    down_x = hop(down_x_send, 1)
    up_got = to_core(after(up_theirs, down_x_send))
    grad_oth = to_core(after(grad_send, down_x_send))
    up_half = halves_of(plus(up_got, after(up_mine, down_x_send)))
    up_x_send = low(lax.dynamic_index_in_dim(up_half, 1 - side, 1, keepdims=False))
    up_x_keep = lax.dynamic_index_in_dim(up_half, side, 1, keepdims=False)
    up_x = hop(up_x_send, 1)

    def back(pair, *gate):
        return attend_back(
            after(numbered[pair], *gate),
            qkv,
            qfeat,
            kfeat,
            grad_oth,
            grad_own,
            (wide_oth, wide_own),
            (logs_oth, logs_own),
            frames_here,
        )

    def project_fold(their, mine):
        got = to_core(their)
        return jnp.where(straight, got, mine), jnp.where(straight, mine, got)

    bit = (chip // 2) % 2

    def split(x):
        parts = halves_of(x)
        return low(pick(parts, 1 - bit)), pick(parts, bit)

    residual_got = turn(after(residual_grad, up_x_send))
    down_send, down_keep = split(plus(down_x_keep, after(down_x, up_x_send)))
    down_z = hop(down_send, hops[0])
    oth_0, own_0 = back(0, down_send)
    got_0 = to_core(oth_0)
    down_sum = plus(down_keep, after(down_z, oth_0))
    down_low = low(down_sum)
    down_z = hop(down_low, hops[1])
    up_y = plus(up_x_keep, after(up_x, oth_0))
    up_y_send = low(up_y[0])
    up_y_got = to_plane(up_y_send)

    residual_got = after(residual_got, oth_0)
    oth_1, own_1 = back(1, down_low, up_y_send, residual_got, got_0)
    got_1 = to_core(oth_1)

    def rest(total, got, steps):
        total = plus(total, got)
        for step in steps:
            total = plus(total, hop(low(total), step))
        return low(total)

    down_sum = rest(down_sum, after(down_z, oth_1), hops[2:])
    down_z = hop(down_sum, hops[0])
    up_send, up_keep = split(plus(up_y[1], after(up_y_got, oth_1)))
    up_z = hop(up_send, hops[0])
    their_0, mine_0, offsets_0, part = project_grad(
        after(scal, down_sum, up_send),
        first,
        (oth_0, oth_1),
        (own_0, own_1),
        (got_0, got_1),
        weight_here,
        weight_there,
    )
    early_send, early_keep = project_fold(their_0, mine_0)
    early_got = to_plane(early_send)
    up_sum = plus(up_keep, after(up_z, part))
    up_low = low(up_sum)
    up_z = hop(up_low, hops[1])

    down_sum = join(down_sum, after(down_z, part), bit, 0)
    down_x = hop(down_sum, 1)

    oth_2, own_2 = back(2, early_send, up_low, down_sum, got_1)
    got_2 = to_core(oth_2)
    up_sum = rest(up_sum, after(up_z, oth_2), hops[2:])
    up_z = hop(up_sum, hops[0])
    early_half = halves_of(plus(early_keep, after(early_got, oth_2)))
    early_send = low(pick(early_half, 1 - side))
    early_keep = pick(early_half, side)
    early_x = hop(early_send, 1)
    their_2, mine_2, offsets_2 = project_grad(
        after(scal, up_sum, early_send), first, (oth_2,), (own_2,)
    )
    late_send, late_keep = project_fold(their_2, mine_2)
    late_got = to_plane(late_send)
    up_sum = join(up_sum, after(up_z, mine_2), bit, 0)
    down_sum = join(down_sum, after(down_x, mine_2), side, 0)
    down_got = to_core(down_sum)
    early_low, early_keep = split(plus(early_keep, after(early_x, mine_2)))
    early_z = hop(early_low, hops[0])
    first_low, first_sums = first_grad(
        own_2,
        got_2,
        weight_here,
        weight_there,
        part,
        after(own, late_send, up_sum, early_low),
    )
    first_got = turn(first_low)
    table = small_table(
        scal,
        frames_here,
        sums_ahead,
        sums_behind,
        first_sums,
        learner_sums,
        learner_offset_sums,
        up_sums,
        offsets_0,
        offsets_2,
    )

    early_sum = plus(early_keep, after(early_z, table))
    early_low = low(early_sum)
    early_z = hop(early_low, hops[1])
    late_half = halves_of(plus(late_keep, after(late_got, early_low)))
    late_send = low(pick(late_half, 1 - side))
    late_keep = pick(late_half, side)
    late_x = hop(late_send, 1)
    table = table + after(to_core(table), late_send)
    table_got = to_plane(table)
    up_x = hop(after(up_sum, table), 1)
    late_sum = plus(late_keep, after(late_x, table))
    late_low = low(late_sum)
    late_z = hop(late_low, hops[0])
    table = table + after(table_got, late_low)
    late_sum = plus(late_sum, after(late_z, table))
    late_low = low(late_sum)
    late_z = hop(late_low, hops[1])
    table_got = hop(after(table, late_low), hops[0])
    early_sum = rest(early_sum, after(early_z, late_low), hops[2:])
    early_z = hop(early_sum, hops[0])
    table = table + after(table_got, early_sum)
    table_got = hop(table, hops[1])
    up_sum = join(up_sum, after(up_x, table), side, 0)
    up_got = to_core(up_sum)
    early_sum = join(early_sum, after(early_z, up_sum), bit, 0)
    early_x = hop(early_sum, 1)
    late_sum = rest(late_sum, after(late_z, early_sum), hops[2:])
    late_x = hop(late_sum, 1)
    table = table + after(table_got, late_sum)
    for step in hops[2:]:
        table = table + hop(table, step)
    table_got = hop(table, 1)
    tokens_gradient = last(
        after(scal, table),
        packed,
        first_low,
        first_got,
        residual_grad,
        residual_got,
        norm_gains[0:1],
        tokens_here,
    )
    table = table + after(table_got, tokens_gradient)
    early_sum = join(early_sum, after(early_x, tokens_gradient), side, 0)
    early_got = to_core(early_sum)
    late_sum = join(late_sum, after(late_x, early_sum), side, 0)
    late_got = to_core(late_sum)

    def two(x, other):
        return jnp.where(core == 0, x, other), jnp.where(core == 0, other, x)

    def out_block(x):
        return jnp.concatenate([x[width:, : width // 2], x[width:, width // 2 :]], axis=0)

    down_first, down_second = two(down_sum, down_got)
    up_first, up_second = two(up_sum, up_got)
    contract_gradient = jnp.concatenate([down_first, down_second], axis=0).astype(F32)
    expand_gradient = jnp.concatenate([up_first[:width], up_second[:width]], axis=1).astype(F32)
    output_gradient = jnp.concatenate([out_block(up_first), out_block(up_second)], axis=1).astype(F32)

    early_two, late_two = two(early_sum, early_got), two(late_sum, late_got)

    def column(pair, part):
        halves, at = (early_two, pair) if pair < pairs - 1 else (late_two, 0)
        at = at * 384 + part * 128
        return jnp.concatenate([x[:, at : at + 128] for x in halves], axis=0)

    attend_gradient = jnp.stack(
        [
            jnp.concatenate([column(pair, part) for pair in range(pairs)], axis=1)
            for part in range(3)
        ],
        axis=1,
    ).astype(F32)
    return (
        jnp.where(straight, pooled[:maps_all], residual_got[half_rows - maps_all :]).reshape(
            frames_here, MAPS, width
        ),
        tokens_gradient,
        table[0:3],
        table[3:6],
        attend_gradient,
        lax.dynamic_slice_in_dim(table[21:23], plane * share, share, 1),
        output_gradient,
        table[6],
        expand_gradient,
        lax.dynamic_slice_in_dim(table[17:21], 2 * plane, 2, 0).reshape(2 * hid),
        contract_gradient,
        table[7],
        table[8:16].T,
        table[16, :MAPS],
    )


def solution(mesh):
    groups, sides = mesh.devices.shape
    fine = Mesh(mesh.devices.reshape(groups // 2, 2, sides), ("chip", "core", "mp"))
    dp = ("chip", "core")
    every = ("chip", "core", "mp")
    return jax.shard_map(
        body,
        mesh=fine,
        in_specs=(
            P(every, None),
            P(dp, None),
            P(),
            P(),
            P(None, None, "mp"),
            P(None, "mp"),
            P("mp", None),
            P(),
            P(None, "mp"),
            P("mp"),
            P("mp", None),
            P(),
            P(),
            P(),
            P(every, None, None),
        ),
        out_specs=(
            P(every, None, None),
            P(every, None),
            P(),
            P(),
            P(None, None, "mp"),
            P(None, "mp"),
            P("mp", None),
            P(),
            P(None, "mp"),
            P("mp"),
            P("mp", None),
            P(),
            P(),
            P(),
        ),
        check_vma=False,
    )
```
